32 devices in a mesh: rows: 2 (over x), cols: 4 (over y, core), dp: 4 (over z).
Axes of the slice: x: 2, y: 2, z: 4, core: 2. Of those that a mesh axis runs over, the one named last changes fastest.
Arguments:
- fields: float32 [128, 64, 384], P(('dp', 'rows'), 'cols'), parts along dimension 0, may hold values from -6 to 6
- logit_scale: float32 [6], replicated, may hold values from 4 to 25
- w_qkv: bfloat16 [384, 1152], replicated, may hold values from -0.3125 to 0.3125
- w_proj: bfloat16 [384, 384], replicated, may hold values from -0.3125 to 0.3125
- w_merge: bfloat16 [1536, 768], P(None, 'cols'), may hold values from -0.15625 to 0.15625
- w_up: bfloat16 [768, 3072], P('rows', 'cols'), may hold values from -0.21875 to 0.21875
- w_down: bfloat16 [3072, 768], P('cols', 'rows'), may hold values from -0.109375 to 0.109375
- cotangent: bfloat16 [64, 32, 768], P(('dp', 'rows'), 'cols'), parts along dimension 0, may hold values from -0.59765625 to 0.59765625
Outputs:
- coarse: float32 [64, 32, 768], P(('dp', 'rows'), 'cols'), parts along dimension 0
- grad_coarse: float32 [64, 32, 768], P(('dp', 'rows'), 'cols'), parts along dimension 0
- grad_up: float32 [768, 12288], P('rows', ('dp', 'cols')), parts along dimension 1
- grad_down: float32 [3072, 3072], P('cols', ('dp', 'rows')), parts along dimension 1
The draws below stay inside these ranges and needn't reach their ends.
There are 4 independent parts, one for each index of `dp`. The reference program is written for one: setup_inputs(seed, part) draws one part's arguments, and reference() takes and returns one part's arrays. A program takes and returns all parts, laid end to end along the dimension named above; an argument that names none is the same for every part. Nothing has to cross between parts.
All inputs are finite; a program needn't handle non-finite values.
Results may differ from the reference program's by a relative error of at most 0.02.
Values may be sent and summed in bfloat16 or wider, within the bound.
A program may use at most 64 MiB of HBM per device.

```python
import math
import jax
import jax.numpy as jnp
from jax import lax

C3 = 384
C4 = 768
FF4 = 3072
HEADS3 = 6
WIN = 16
NR = 32
NC = 64
N_ROWS = 2


def spiked(array, key, source, target, blocks, factor):
    def block_of(axis_at):
        return (jnp.arange(array.shape[axis_at]) // (array.shape[axis_at] // blocks)).reshape((-1,) + (1,) * (array.ndim - 1 - axis_at))

    near = jax.random.permutation(key, blocks)[block_of(target)]
    far = (block_of(target) + blocks // 2) % blocks
    return jnp.where((block_of(source) == near) | (block_of(source) == far), factor * array, array)


def block_scale(own_key, extent, cuts, least, high):
    level, own = 1.0, jax.random.fold_in(own_key, 6)
    for dim, parts in cuts:
        steps = jnp.exp(jax.random.uniform(jax.random.fold_in(own, dim), (parts,), jnp.float32, least / len(cuts), high / len(cuts)))
        level = level * jnp.repeat(steps, extent[dim] // parts).reshape([-1 if axis == dim else 1 for axis in range(len(extent))])
    return level


def gaussian(own_key, dims, deviation, most, cuts=(), kind=jnp.bfloat16):
    array = jax.random.normal(own_key, dims, jnp.float32) * deviation
    if len(cuts) > 0:
        array = block_scale(own_key, dims, cuts, -0.22, 0.18) * array
    return jnp.clip(array, min=-most, max=most).astype(kind)


def noise_with(key, extent, scale, bound, shards, heavy, dtype=jnp.bfloat16):
    entries = scale * jax.random.normal(key, extent, jnp.float32)
    if shards:
        entries = entries * block_scale(key, extent, shards, -0.22, 0.18)
    return jnp.clip(spiked(entries, jax.random.fold_in(key, 3), *heavy), -bound, bound).astype(dtype)


def setup_inputs(seed: int = 0, part: int = 0) -> dict:
    keys = jax.random.split(jax.random.key(seed), 9)
    part_keys = jax.random.split(jax.random.fold_in(keys[8], part), 9)
    return {
        "fields": gaussian(part_keys[0], (NR, NC, C3), 1.0, 6.0, ((0, 2), (1, 4)), jnp.float32),
        "logit_scale": jnp.clip(jnp.exp(jax.random.uniform(keys[1], (HEADS3,), jnp.float32, math.log(4.0), math.log(25.0))), 4.0, 25.0),
        "w_qkv": gaussian(keys[2], (C3, 3 * C3), C3 ** -0.5, 0.3125),
        "w_proj": gaussian(keys[3], (C3, C3), C3 ** -0.5, 0.3125),
        "w_merge": gaussian(keys[4], (4 * C3, C4), (4 * C3) ** -0.5, 0.15625, ((1, 4),)),
        "w_up": gaussian(keys[5], (C4, FF4), C4 ** -0.5, 0.21875, ((0, 2), (1, 4))),
        "w_down": gaussian(keys[6], (FF4, C4), FF4 ** -0.5, 0.109375, ((0, 4), (1, 2))),
        "cotangent": noise_with(part_keys[7], (NR // 2, NC // 2, C4), 0.1, 0.59765625, ((0, 2), (1, 4)), (0, 2, 2, 2.0)),
    }


eps_norm = 1e-05
eps_unit = 1e-06

def layer_norm(value):
    average = lax.optimization_barrier(jnp.mean(value, axis=-1, keepdims=True))
    centred = value - average
    spread = lax.optimization_barrier(jnp.mean(centred * centred, axis=-1, keepdims=True))
    inverse = lax.rsqrt(spread + eps_norm)
    return (centred * inverse, inverse)

def norm_slope(upstream, normed, inverse):
    first_mean = lax.optimization_barrier(jnp.mean(upstream, axis=-1, keepdims=True))
    second_mean = lax.optimization_barrier(jnp.mean(upstream * normed, axis=-1, keepdims=True))
    return inverse * (upstream - first_mean - normed * second_mean)

def unit_heads(value, head_count):
    shaped = value.reshape(value.shape[:-1] + (head_count, value.shape[-1] // head_count))
    squares = lax.optimization_barrier(jnp.sum(shaped * shaped, axis=-1, keepdims=True))
    return (shaped * lax.rsqrt(squares + eps_unit)).reshape(value.shape)

def windows_of(field_grid, window):
    grid_rows, grid_cols, channels = field_grid.shape
    shaped = field_grid.reshape(grid_rows // window, window, grid_cols // window, window, channels)
    return shaped.transpose(0, 2, 1, 3, 4).reshape(-1, window * window, channels)

def grid_of(blocks, grid_rows, grid_cols, window):
    channels = blocks.shape[-1]
    shaped = blocks.reshape(grid_rows // window, grid_cols // window, window, window, channels)
    return shaped.transpose(0, 2, 1, 3, 4).reshape(grid_rows, grid_cols, channels)

def attend_exact(queries, key_rows, value_rows, logit_scale, head_count):
    number, window_size, channels = queries.shape
    width_head = channels // head_count
    query_heads = queries.astype(jnp.float32).reshape(number, window_size, head_count, width_head)
    key_heads = key_rows.astype(jnp.float32).reshape(number, window_size, head_count, width_head)
    value_heads = value_rows.astype(jnp.float32).reshape(number, window_size, head_count, width_head)
    scores = jnp.einsum('wqhd,wkhd->whqk', query_heads, key_heads) * logit_scale[None, :, None, None]
    weights = jnp.exp(scores)
    weights = (weights / lax.optimization_barrier(jnp.sum(weights, axis=-1, keepdims=True))).astype(jnp.bfloat16)
    mixed_out = jnp.einsum('whqk,wkhd->wqhd', weights.astype(jnp.float32), value_heads)
    return mixed_out.reshape(number, window_size, channels)

def merge_patches(field_grid):
    quarters = (field_grid[0::2, 0::2], field_grid[1::2, 0::2], field_grid[0::2, 1::2], field_grid[1::2, 1::2])
    return jnp.concatenate(quarters, axis=-1)

def exact_gelu(value):
    return jax.nn.gelu(value, approximate=False)

def reference(fields, logit_scale, w_qkv, w_proj, w_merge, w_up, w_down, cotangent):
    offset = WIN // 2
    grid_rows, grid_cols, channels = fields.shape
    head_count = logit_scale.shape[0]
    rolled = jnp.roll(fields, (-offset, -offset), (0, 1)).astype(jnp.bfloat16).reshape(-1, channels)
    projected = jnp.dot(rolled, w_qkv, preferred_element_type=jnp.float32)
    queries = unit_heads(projected[:, :channels], head_count).astype(jnp.bfloat16)
    key_rows = unit_heads(projected[:, channels:2 * channels], head_count).astype(jnp.bfloat16)
    value_rows = projected[:, 2 * channels:].astype(jnp.bfloat16)

    def blocked(flat_rows):
        return windows_of(flat_rows.reshape(grid_rows, grid_cols, channels), WIN)

    def one_window(triple):
        return attend_exact(triple[0][None], triple[1][None], triple[2][None], logit_scale, head_count)[0]
    mixed = lax.map(one_window, (blocked(queries), blocked(key_rows), blocked(value_rows)))
    mixed = grid_of(mixed, grid_rows, grid_cols, WIN)
    mixed = jnp.roll(mixed, (offset, offset), (0, 1)).astype(jnp.bfloat16).reshape(-1, channels)
    branch = jnp.dot(mixed, w_proj, preferred_element_type=jnp.float32)
    normed, _ = layer_norm(branch)
    stream = fields + normed.reshape(fields.shape)
    merged = merge_patches(stream).astype(jnp.bfloat16)
    coarse_rows, coarse_cols = (merged.shape[0], merged.shape[1])
    merged_rows = merged.reshape(-1, merged.shape[-1])
    level, _ = layer_norm(jnp.dot(merged_rows, w_merge, preferred_element_type=jnp.float32))
    level_b = level.astype(jnp.bfloat16)
    hidden_pre = jnp.dot(level_b, w_up, preferred_element_type=jnp.float32)
    hidden = exact_gelu(hidden_pre).astype(jnp.bfloat16)
    branch_out = jnp.dot(hidden, w_down, preferred_element_type=jnp.float32)
    branch_norm, branch_inv = layer_norm(branch_out)
    coarse = level + branch_norm
    upstream = cotangent.astype(jnp.float32).reshape(coarse.shape)
    slope_out = norm_slope(upstream, branch_norm, branch_inv).astype(jnp.bfloat16)
    slope_hidden = jnp.dot(slope_out, w_down.T, preferred_element_type=jnp.float32)
    _, pullback = jax.vjp(exact_gelu, hidden_pre)
    slope_pre = pullback(slope_hidden)[0].astype(jnp.bfloat16)
    grad_coarse = upstream + jnp.dot(slope_pre, w_up.T, preferred_element_type=jnp.float32)

    def banded(value):
        return value.reshape(N_ROWS, -1, value.shape[-1])

    def add_band(running, items):
        inputs_band, pre_band, hidden_band, out_band = items
        term_up = jnp.dot(inputs_band.T, pre_band, preferred_element_type=jnp.float32)
        term_down = jnp.dot(hidden_band.T, out_band, preferred_element_type=jnp.float32)
        term_up = lax.optimization_barrier(term_up.astype(jnp.bfloat16)).astype(jnp.float32)
        term_down = lax.optimization_barrier(term_down.astype(jnp.bfloat16)).astype(jnp.float32)
        return ((running[0] + term_up, running[1] + term_down), None)
    start_up = jnp.zeros((w_up.shape[0], w_up.shape[1]), jnp.float32)
    start_down = jnp.zeros((w_down.shape[0], w_down.shape[1]), jnp.float32)
    (grad_up, grad_down), _ = lax.scan(add_band, (start_up, start_down), (banded(level_b), banded(slope_pre), banded(hidden), banded(slope_out)))
    return (coarse.reshape(coarse_rows, coarse_cols, -1), grad_coarse.reshape(coarse_rows, coarse_cols, -1), grad_up, grad_down)
```

```python
import jax
import jax.numpy as jnp
import numpy as np
from jax import lax
from jax.experimental import pallas as pl
from jax.experimental.pallas import tpu as pltpu
from jax.sharding import PartitionSpec as P

WIN = 16


eps_norm = 1e-05
eps_unit = 1e-06
N_COPIES = 51


def padded_2(cells, sides, width):
    for axis, dim in sides:
        count = lax.axis_size(axis)
        head = lax.slice_in_dim(cells, 0, width, axis=dim)
        tail = lax.slice_in_dim(cells, cells.shape[dim] - width, cells.shape[dim], axis=dim)
        cells = jnp.concatenate(
            [
                lax.ppermute(tail, axis, [(i, (i + 1) % count) for i in range(count)]),
                cells,
                lax.ppermute(head, axis, [((i + 1) % count, i) for i in range(count)]),
            ],
            axis=dim,
        )
    return cells


def layer_norm(value):
    average = jnp.mean(value, axis=-1, keepdims=True)
    centred = value - average
    spread = jnp.mean(centred * centred, axis=-1, keepdims=True)
    inverse = lax.rsqrt(spread + eps_norm)
    return (centred * inverse, inverse)


def norm_slope(upstream, normed, inverse):
    first_mean = jnp.mean(upstream, axis=-1, keepdims=True)
    second_mean = jnp.mean(upstream * normed, axis=-1, keepdims=True)
    return inverse * (upstream - first_mean - normed * second_mean)


def unit_heads(value, head_count):
    shaped = value.reshape(value.shape[:-1] + (head_count, value.shape[-1] // head_count))
    squares = jnp.sum(shaped * shaped, axis=-1, keepdims=True)
    return (shaped * lax.rsqrt(squares + eps_unit)).reshape(value.shape)


def windows_of(field_grid, window):
    grid_rows, grid_cols, channels = field_grid.shape
    shaped = field_grid.reshape(grid_rows // window, window, grid_cols // window, window, channels)
    return shaped.transpose(0, 2, 1, 3, 4).reshape(-1, window * window, channels)


def grid_of(blocks, grid_rows, grid_cols, window):
    channels = blocks.shape[-1]
    shaped = blocks.reshape(grid_rows // window, grid_cols // window, window, window, channels)
    return shaped.transpose(0, 2, 1, 3, 4).reshape(grid_rows, grid_cols, channels)


def attend(queries, key_rows, value_rows, logit_scale, head_count):
    number, window_size, channels = queries.shape
    width_head = channels // head_count
    query_heads = queries.reshape(number, window_size, head_count, width_head)
    key_heads = key_rows.reshape(number, window_size, head_count, width_head)
    value_heads = value_rows.reshape(number, window_size, head_count, width_head)
    scores = jnp.einsum(
        "wqhd,wkhd->whqk", query_heads, key_heads, preferred_element_type=jnp.float32
    )
    weights = jnp.exp(scores * logit_scale[None, :, None, None])
    weights = (weights / jnp.sum(weights, axis=-1, keepdims=True)).astype(jnp.bfloat16)
    mixed_out = jnp.einsum(
        "whqk,wkhd->wqhd", weights, value_heads, preferred_element_type=jnp.float32
    )
    return mixed_out.reshape(number, window_size, channels)


def merge_patches(field_grid):
    quarters = (
        field_grid[0::2, 0::2],
        field_grid[1::2, 0::2],
        field_grid[0::2, 1::2],
        field_grid[1::2, 1::2],
    )
    return jnp.concatenate(quarters, axis=-1)


def exact_gelu(value):
    return jax.nn.gelu(value, approximate=False)


def local(fields, logit_scale, w_qkv, w_proj, w_merge, w_up, w_down, cotangent):
    tile_rows, tile_cols, channels = fields.shape
    offset = WIN // 2
    head_count = logit_scale.shape[0]
    tokens = fields.astype(jnp.bfloat16)
    token_rows = tokens.reshape(-1, channels)
    wide_rows = tile_rows + WIN
    wide_cols = tile_cols + WIN
    widened = padded_2(tokens, (("rows", 0), ("cols", 1)), offset)
    wide_proj = jnp.dot(
        widened.reshape(-1, channels), w_qkv[:, channels:], preferred_element_type=jnp.float32
    )
    key_grid = unit_heads(wide_proj[:, :channels], head_count).astype(jnp.bfloat16)
    value_grid = wide_proj[:, channels:].astype(jnp.bfloat16)
    query_raw = jnp.dot(token_rows, w_qkv[:, :channels], preferred_element_type=jnp.float32)
    queries = (
        unit_heads(query_raw, head_count)
        .astype(jnp.bfloat16)
        .reshape(tile_rows, tile_cols, channels)
    )
    padded = jnp.pad(queries, ((offset, offset), (offset, offset), (0, 0)))
    key_blocks = windows_of(key_grid.reshape(wide_rows, wide_cols, channels), WIN)
    value_blocks = windows_of(value_grid.reshape(wide_rows, wide_cols, channels), WIN)
    mixed = attend(windows_of(padded, WIN), key_blocks, value_blocks, logit_scale, head_count)
    mixed = grid_of(mixed, wide_rows, wide_cols, WIN)[
        offset : offset + tile_rows, offset : offset + tile_cols
    ]
    mixed = mixed.astype(jnp.bfloat16).reshape(-1, channels)
    normed, _ = layer_norm(jnp.dot(mixed, w_proj, preferred_element_type=jnp.float32))
    stream = fields + normed.reshape(fields.shape)
    merged = merge_patches(stream).astype(jnp.bfloat16)
    merged_rows = merged.reshape(-1, merged.shape[-1])
    own_count = merged_rows.shape[0]
    partial_band = jnp.dot(
        lax.all_gather(merged_rows, "cols", axis=0, tiled=True),
        w_merge,
        preferred_element_type=jnp.float32,
    )
    projected_band = lax.all_gather(
        partial_band.astype(jnp.bfloat16), "cols", axis=1, tiled=True
    ).astype(partial_band.dtype)
    level_band, _ = layer_norm(projected_band)
    level_b = level_band.astype(jnp.bfloat16)
    level_own = lax.dynamic_slice_in_dim(
        level_band, lax.axis_index("cols") * own_count, own_count, 0
    )
    up_full = lax.all_gather(w_up, "rows", axis=0, tiled=True)
    down_full = lax.all_gather(w_down, "rows", axis=1, tiled=True)
    hidden_pre = jnp.dot(level_b, up_full, preferred_element_type=jnp.float32)
    hidden = exact_gelu(hidden_pre).astype(jnp.bfloat16)
    rows_part = hidden
    branch_out = lax.psum_scatter(
        jnp.dot(rows_part, down_full, preferred_element_type=jnp.float32).astype(jnp.bfloat16),
        "cols",
        scatter_dimension=0,
        tiled=True,
    ).astype(jnp.float32)
    branch_norm, branch_inv = layer_norm(branch_out)
    coarse = level_own + branch_norm
    upstream = cotangent.astype(jnp.float32).reshape(own_count, -1)
    slope_own = norm_slope(upstream, branch_norm, branch_inv).astype(jnp.bfloat16)
    slope_out = lax.all_gather(slope_own, "cols", axis=0, tiled=True)
    slope_hidden = jnp.einsum("tc,fc->tf", slope_out, down_full, preferred_element_type=jnp.float32)
    _, pullback = jax.vjp(exact_gelu, hidden_pre)
    slope_pre = pullback(slope_hidden)[0].astype(jnp.bfloat16)
    rows_part = slope_pre
    slope_input = lax.psum_scatter(
        jnp.einsum("tf,cf->tc", rows_part, up_full, preferred_element_type=jnp.float32).astype(
            jnp.bfloat16
        ),
        "cols",
        scatter_dimension=0,
        tiled=True,
    ).astype(jnp.float32)
    grad_coarse = upstream + slope_input
    term_up = jnp.einsum("tc,tf->cf", level_b, slope_pre, preferred_element_type=jnp.float32)
    term_down = jnp.einsum("tf,tc->fc", hidden, slope_out, preferred_element_type=jnp.float32)
    grad_up, grad_down = (
        lax.psum_scatter(
            term_up.astype(jnp.bfloat16), "rows", scatter_dimension=0, tiled=True
        ).astype(jnp.float32),
        lax.psum_scatter(
            term_down.astype(jnp.bfloat16), "rows", scatter_dimension=1, tiled=True
        ).astype(jnp.float32),
    )
    coarse_shape = (tile_rows // 2, tile_cols // 2, coarse.shape[-1])
    return (coarse.reshape(coarse_shape), grad_coarse.reshape(coarse_shape), grad_up, grad_down)


def _ln(value):
    average = jnp.mean(value, axis=-1, keepdims=True)
    centred = value - average
    spread = jnp.mean(centred * centred, axis=-1, keepdims=True)
    inverse = lax.rsqrt(spread + eps_norm)
    return centred * inverse, inverse


def _dot(a, b, ca=1, cb=0):
    return lax.dot_general(
        a, b, (((ca,), (cb,)), ((), ())), preferred_element_type=jnp.float32
    )


def fused_kernel(
    fields_h, logit, w_qkv_h, w_proj_h, w_merge, w_up, w_down, cot_h,
    coarse, gcoarse, gup, gdown,
    fields, w_qkv, w_proj, cot, sendq, winq, mixw, mixq, perm, wm, proj, up, down,
    lvl, hid, dgel, bsend, brecv, slo, spre, gsend, grecv, loc, sends, recvs,
):
    f32, bf16 = jnp.float32, jnp.bfloat16
    i, j = lax.axis_index("rows"), lax.axis_index("cols")
    ni, nj = lax.axis_size("rows"), lax.axis_size("cols")
    z = lax.axis_index("dp")
    beside = z + 1 - 2 * (z % 2)
    bit = z % 2
    half_side = WIN // 2
    quad = half_side * half_side
    ch = fields.shape[-1]
    c4 = cot.shape[-1]
    own = cot.shape[0]
    half = c4 // ni
    ff = w_up.shape[1]
    share = w_merge.shape[0]
    heads = logit.shape[0]
    width = ch // heads
    other = (i + 1) % ni
    prev_j, next_j = (j + nj - 1) % nj, (j + 1) % nj
    partner = j + 1 - 2 * (j % 2)
    far = (j + 2) % nj
    far_partner = (partner + 2) % nj
    peers = (partner, far, far_partner)
    started = []

    def remote(src, dst, row, col, part=z):
        n = len(started)
        copy = pltpu.make_async_remote_copy(
            src_ref=src, dst_ref=dst, send_sem=sends.at[n], recv_sem=recvs.at[n],
            device_id={"rows": row, "cols": col, "dp": part},
            device_id_type=pl.DeviceIdType.MESH,
        )
        started.append(copy)
        return copy

    barrier = pltpu.get_barrier_semaphore()
    greet = [(i, p) for p in peers] + [(other, j), (other, prev_j), (other, next_j)]
    for row, col in greet:
        pl.semaphore_signal(
            barrier, inc=1, device_id={"rows": row, "cols": col},
            device_id_type=pl.DeviceIdType.MESH,
        )
    pl.semaphore_signal(
        barrier, inc=1, device_id={"dp": beside}, device_id_type=pl.DeviceIdType.MESH
    )

    def rows_at(start, size):
        return pl.ds(pl.multiple_of(start, 16), size)

    locals_ = [
        pltpu.make_async_copy(src, dst, loc.at[n])
        for n, (src, dst) in enumerate((
            (fields_h, fields),
            (w_qkv_h, w_qkv),
            (w_proj_h, w_proj),
            (cot_h, cot),
            (w_merge, wm.at[rows_at(j * share, share), :]),
            (w_up, up.at[rows_at(i * half, half), :]),
            (w_down, down.at[i]),
        ))
    ]
    for c in locals_:
        c.start()

    lane = lax.broadcasted_iota(jnp.int32, (ch, ch), 0) // width
    lane_t = lax.broadcasted_iota(jnp.int32, (ch, ch), 1) // width
    block_ones = (lane == lane_t).astype(f32).astype(bf16)
    rows_out = lax.broadcasted_iota(jnp.int32, (4 * quad, 4 * quad), 0)
    cols_in = lax.broadcasted_iota(jnp.int32, (4 * quad, 4 * quad), 1)
    which, place = rows_out // quad, rows_out % quad
    r = 2 * (place // half_side) + which % 2
    c = 2 * (place % half_side) + which // 2
    source = ((r // half_side) * 2 + c // half_side) * quad + (r % half_side) * half_side + c % half_side
    perm[...] = (source == cols_in).astype(f32).astype(bf16)

    def quarter(a, b):
        part = fields[a * half_side:(a + 1) * half_side, b * half_side:(b + 1) * half_side, :]
        return part.reshape(quad, ch)

    locals_[0].wait()
    for k in range(3):
        sendq[k] = quarter(k // 2, k % 2).astype(bf16)
    winq[3] = quarter(1, 1).astype(bf16)
    pl.semaphore_wait(barrier, len(greet) + 1)

    targets = ((other, prev_j), (other, j), (i, prev_j))
    backs = ((other, next_j), (other, j), (i, next_j))
    quads = [remote(sendq.at[k], winq.at[k], *targets[k]) for k in range(3)]
    for c in quads:
        c.start()

    part_m = share // 4
    mine_at, theirs_at = bit * part_m, (1 - bit) * part_m

    def merge_out(start):
        return remote(
            w_merge.at[rows_at(start, part_m), :], wm.at[rows_at(j * share + start, part_m), :], i, far
        )

    def merge_pass(start):
        at = rows_at(far * share + start, part_m)
        return remote(wm.at[at, :], wm.at[at, :], i, partner)

    merge_far = [merge_out(start) for start in (mine_at, 2 * part_m, 3 * part_m)]
    merge_on = [merge_pass(start) for start in (mine_at, 2 * part_m, 3 * part_m, theirs_at)]
    at = rows_at(far * share + mine_at, part_m)
    merge_side = remote(wm.at[at, :], wm.at[at, :], i, j, beside)
    merge_beside = remote(w_merge, wm.at[rows_at(j * share, share), :], i, partner)

    piece_u = half // 4

    def up_at(row, part):
        return rows_at(row * half + bit * 2 * piece_u + part * piece_u, piece_u)

    up_out = [
        remote(
            w_up.at[rows_at(bit * 2 * piece_u + q * piece_u, piece_u), :], up.at[up_at(i, q), :], other, j
        )
        for q in range(2)
    ]
    up_on = [
        remote(up.at[up_at(other, q), :], up.at[up_at(other, q), :], i, j, beside) for q in range(2)
    ]
    unit_d = ff // 8
    spans = (
        rows_at(bit * 3 * unit_d, 2 * unit_d),
        rows_at(bit * 3 * unit_d + 2 * unit_d, unit_d),
        pl.ds(6 * unit_d, 2 * unit_d),
    )
    down_out = [remote(w_down.at[at, :], down.at[i, at, :], other, j) for at in spans]
    down_on = [
        remote(down.at[other, at, :], down.at[other, at, :], i, j, beside) for at in spans[:2]
    ]
    for c in (merge_far[0], merge_beside, up_out[0], up_out[1]):
        c.start()

    def unit(value):
        squares = value * value
        top = squares.astype(bf16)
        low = (squares - top.astype(f32)).astype(bf16)
        total = _dot(top, block_ones) + _dot(low, block_ones)
        return (value * lax.rsqrt(total + eps_unit)).astype(bf16)

    def project(first):
        tokens = winq[first:first + 2].reshape(2 * quad, ch)
        return (
            unit(_dot(tokens, w_qkv[:, :ch])),
            unit(_dot(tokens, w_qkv[:, ch:2 * ch])),
            _dot(tokens, w_qkv[:, 2 * ch:]).astype(bf16),
        )

    locals_[1].wait()
    quads[2].wait_recv()
    late = project(2)
    merge_far[1].start()
    quads[0].wait_recv()
    quads[1].wait_recv()
    early = project(0)
    merge_far[2].start()
    qhat, khat, vals = (jnp.concatenate([a, b], axis=0) for a, b in zip(early, late))
    merge_far[0].wait_recv()
    merge_side.start()
    merge_on[0].start()
    per = 128 // width
    lanes = lax.broadcasted_iota(jnp.int32, (4 * quad, 128), 1) // width
    for b in range(ch // 128):
        cut = slice(b * 128, (b + 1) * 128)
        qb, kb, vb = qhat[:, cut], khat[:, cut], vals[:, cut]
        acc = None
        for t in range(per):
            mine = lanes == t
            zero = jnp.zeros_like(qb)
            scores = _dot(jnp.where(mine, qb, zero), kb, 1, 1) * logit[b * per + t]
            weights = jnp.exp(scores)
            weights = (weights / jnp.sum(weights, axis=-1, keepdims=True)).astype(bf16)
            term = _dot(weights, jnp.where(mine, vb, zero))
            acc = term if acc is None else acc + term
        mixw[:, :, cut] = acc.astype(bf16).reshape(4, quad, 128)
    returns = [remote(mixw.at[k], mixq.at[k], *backs[k]) for k in range(3)]
    for c in returns:
        c.start()
    for c in down_out:
        c.start()
    mixq[3] = mixw[3]
    up_out[0].wait_recv()
    up_on[0].start()
    merge_far[1].wait_recv()
    merge_on[1].start()
    locals_[2].wait()
    for cp in returns:
        cp.wait_recv()
    normed, _ = _ln(_dot(mixq[...].reshape(4 * quad, ch), w_proj[...]))
    flat = jnp.concatenate([quarter(k // 2, k % 2) for k in range(4)], axis=0)
    stream = (flat + normed).astype(bf16)
    picked = _dot(perm[...], stream).astype(bf16)
    merged = jnp.concatenate([picked[k * quad:(k + 1) * quad] for k in range(4)], axis=1)
    up_out[1].wait_recv()
    up_on[1].start()
    merge_far[2].wait_recv()
    merge_on[2].start()
    merge_side.wait_recv()
    merge_on[3].start()

    pair = j // 2
    pairs = (pair, (pair + 1) % 2)

    def project_pair(p):
        at = pl.ds(pl.multiple_of(p * 2 * share, 128), 2 * share)
        proj[p] = _dot(merged, wm[at, :], 1, 1)

    locals_[4].wait()
    merge_beside.wait_recv()
    project_pair(pairs[0])
    for c in merge_on:
        c.wait_recv()
    project_pair(pairs[1])
    level, _ = _ln(jnp.concatenate([proj[p] for p in range(2)], axis=1))

    def put(ref, value):
        for k in range(ni):
            ref[0, j, k] = value[:, k * half:(k + 1) * half].astype(bf16)

    def take(ref, b, p):
        return jnp.concatenate(
            [ref[b, pl.ds(p * 2, 2), k].reshape(2 * own, half) for k in range(ni)], axis=1
        )

    put(lvl, level)

    class Gathered:
        def __init__(self, ref):
            def send(b, slot, to, row, col):
                return remote(ref.at[b, slot], ref.at[to, slot], row, col)

            self.out_far = send(0, j, 0, i, far)
            self.out_partner = send(0, j, 0, i, partner)
            self.onward = send(0, far, 0, i, partner)
            self.across = [send(0, s, 1, other, j) for s in (j, far)]
            self.across_on = [send(1, s, 1, i, partner) for s in (j, far)]

    levels = Gathered(lvl)
    levels.out_far.start()
    levels.out_partner.start()

    def forward(b, p):
        pre = _dot(take(lvl, b, p), up[...])
        cdf = 0.5 * (1.0 + lax.erf(pre * np.float32(np.sqrt(0.5))))
        hid[b, p] = (pre * cdf).astype(bf16)
        dgel[b, p] = cdf + pre * (jnp.exp(-0.5 * pre * pre) * np.float32(1 / np.sqrt(2 * np.pi)))

    def branch(p, k):
        bsend[pl.ds(p * 2, 2), k] = _dot(hid[0, p], down[k]).astype(bf16).reshape(2, own, half)

    down_out[0].wait_recv()
    down_on[0].start()
    locals_[5].wait()
    locals_[6].wait()
    up_on[0].wait_recv()
    up_on[1].wait_recv()
    levels.out_partner.wait_recv()
    forward(0, pairs[0])
    branch(pairs[0], i)
    down_out[1].wait_recv()
    down_on[1].start()
    levels.out_far.wait_recv()
    levels.onward.start()
    down_out[2].wait_recv()
    levels.across[0].start()
    levels.across[1].start()
    levels.onward.wait_recv()
    forward(0, pairs[1])
    branch(pairs[1], i)
    down_on[0].wait_recv()
    down_on[1].wait_recv()
    branch(pairs[1], other)
    branch_far = remote(bsend.at[far_partner], brecv.at[1], i, partner)
    branch_far.start()
    branch(pairs[0], other)
    branch_near = remote(bsend.at[partner], brecv.at[0], i, partner)
    branch_near.start()
    branch_far.wait_recv()
    brecv[3] = (bsend[far].astype(f32) + brecv[1].astype(f32)).astype(bf16)
    branch_on = remote(brecv.at[3], brecv.at[2], i, far)
    branch_on.start()
    branch_near.wait_recv()
    levels.across[0].wait_recv()
    levels.across_on[0].start()
    levels.across[1].wait_recv()
    levels.across_on[1].start()
    branch_on.wait_recv()
    locals_[3].wait()
    total = bsend[j].astype(f32) + brecv[0].astype(f32) + brecv[2].astype(f32)
    norm, inverse = _ln(jnp.concatenate([total[k] for k in range(ni)], axis=1))
    coarse[...] = level + norm
    g = cot[...].astype(f32)
    put(
        slo,
        inverse * (
            g - jnp.mean(g, axis=-1, keepdims=True)
            - norm * jnp.mean(g * norm, axis=-1, keepdims=True)
        ),
    )
    slopes = Gathered(slo)
    slopes.out_far.start()
    slopes.out_partner.start()
    slopes.across[0].start()

    def backward(b, p):
        so = [slo[b, pl.ds(p * 2, 2), k].reshape(2 * own, half) for k in range(ni)]
        back = _dot(so[0], down[0], 1, 1)
        for k in range(1, ni):
            back = back + _dot(so[k], down[k], 1, 1)
        spre[b, p] = (dgel[b, p] * back).astype(bf16)

    def slope_in(p):
        gsend[pl.ds(p * 2, 2)] = _dot(spre[0, p], up[...], 1, 1).astype(bf16).reshape(2, own, c4)

    slopes.out_partner.wait_recv()
    backward(0, pairs[0])
    slope_in(pairs[0])
    grad_near = remote(gsend.at[partner], grecv.at[0], i, partner)
    grad_near.start()
    levels.across_on[0].wait_recv()
    levels.across_on[1].wait_recv()
    forward(1, pairs[0])
    slopes.out_far.wait_recv()
    slopes.onward.start()
    slopes.across[1].start()
    forward(1, pairs[1])
    slopes.across[0].wait_recv()
    slopes.across_on[0].start()
    slopes.onward.wait_recv()
    backward(0, pairs[1])
    slope_in(pairs[1])
    grad_far = remote(gsend.at[far_partner], grecv.at[1], i, partner)
    grad_far.start()
    slopes.across_on[0].wait_recv()
    backward(1, pairs[0])
    grad_far.wait_recv()
    grecv[3] = (gsend[far].astype(f32) + grecv[1].astype(f32)).astype(bf16)
    grad_on = remote(grecv.at[3], grecv.at[2], i, far)
    grad_on.start()

    def weight_terms(b):
        sp, hd = spre[b].reshape(nj * own, ff), hid[b].reshape(nj * own, ff)
        return (
            _dot(lvl[b, :, i].reshape(nj * own, half), sp, 0, 0),
            _dot(hd, slo[b, :, i].reshape(nj * own, half), 0, 0),
        )

    gup[...], gdown[...] = weight_terms(0)
    slopes.across[1].wait_recv()
    slopes.across_on[1].start()
    slopes.across_on[1].wait_recv()
    backward(1, pairs[1])
    terms = weight_terms(1)
    gup[...] += terms[0]
    gdown[...] += terms[1]
    grad_near.wait_recv()
    grad_on.wait_recv()
    gcoarse[...] = (
        g + gsend[j].astype(f32) + grecv[0].astype(f32) + grecv[2].astype(f32)
    )
    for cp in started:
        cp.wait_send()
def store_kernel(coarse_in, gcoarse_in, gup_in, gdown_in, coarse, gcoarse, gup, gdown, sem):
    pairs = ((gup_in, gup), (gdown_in, gdown), (coarse_in, coarse), (gcoarse_in, gcoarse))
    copies = [pltpu.make_async_copy(src, dst, sem.at[n]) for n, (src, dst) in enumerate(pairs)]
    for c in copies:
        c.start()
    for c in copies:
        c.wait()


def fused(fields, logit_scale, w_qkv, w_proj, w_merge, w_up, w_down, cotangent):
    tile_rows, tile_cols, ch = fields.shape
    ni, nj = lax.axis_size("rows"), lax.axis_size("cols")
    own = cotangent.shape[0] * cotangent.shape[1]
    c4 = cotangent.shape[-1]
    half, ff = w_up.shape
    f32, bf16 = jnp.float32, jnp.bfloat16
    quad = (WIN // 2) ** 2
    vm = pl.BlockSpec(memory_space=pltpu.VMEM)
    hb = pl.BlockSpec(memory_space=pltpu.HBM)
    anywhere = pl.BlockSpec(memory_space=pl.ANY)
    dma = pltpu.SemaphoreType.DMA
    outs = (
        jax.ShapeDtypeStruct((own, c4), f32),
        jax.ShapeDtypeStruct((own, c4), f32),
        jax.ShapeDtypeStruct((half, ff), f32),
        jax.ShapeDtypeStruct((ff, half), f32),
    )
    gathered = pltpu.VMEM((ni, nj, ni, own, half), bf16)
    operands = [fields, logit_scale, w_qkv, w_proj, w_merge.T, w_up, w_down, cotangent.reshape(own, c4)]
    operands = [pltpu.with_memory_space_constraint(v, pltpu.HBM) for v in operands]
    values = pl.pallas_call(
        fused_kernel,
        out_shape=outs,
        in_specs=[hb, pl.BlockSpec(memory_space=pltpu.SMEM)] + [hb] * 6,
        out_specs=(vm,) * 4,
        scratch_shapes=[
            pltpu.VMEM(fields.shape, f32),
            pltpu.VMEM(w_qkv.shape, bf16),
            pltpu.VMEM(w_proj.shape, bf16),
            pltpu.VMEM((own, c4), bf16),
            pltpu.VMEM((3, quad, ch), bf16),
            pltpu.VMEM((4, quad, ch), bf16),
            pltpu.VMEM((4, quad, ch), bf16),
            pltpu.VMEM((4, quad, ch), bf16),
            pltpu.VMEM((4 * quad, 4 * quad), bf16),
            pltpu.VMEM((c4, w_merge.shape[0]), bf16),
            pltpu.VMEM((2, own, c4 // 2), f32),
            pltpu.VMEM((c4, ff), bf16),
            pltpu.VMEM((ni, ff, half), bf16),
            gathered,
            pltpu.VMEM((ni, 2, 2 * own, ff), bf16),
            pltpu.VMEM((ni, 2, 2 * own, ff), f32),
            pltpu.VMEM((nj, ni, own, half), bf16),
            pltpu.VMEM((4, ni, own, half), bf16),
            gathered,
            pltpu.VMEM((ni, 2, 2 * own, ff), bf16),
            pltpu.VMEM((nj, own, c4), bf16),
            pltpu.VMEM((4, own, c4), bf16),
            dma((7,)),
            dma((N_COPIES,)),
            dma((N_COPIES,)),
        ],
        compiler_params=pltpu.CompilerParams(
            collective_id=0, has_side_effects=True, vmem_limit_bytes=44 << 20
        ),
    )(*operands)
    values = pl.pallas_call(
        store_kernel,
        out_shape=outs,
        in_specs=[anywhere] * 4,
        out_specs=(hb,) * 4,
        scratch_shapes=[dma((4,))],
        compiler_params=pltpu.CompilerParams(vmem_limit_bytes=4 << 20),
    )(*values)
    shape = (tile_rows // 2, tile_cols // 2, c4)
    return values[0].reshape(shape), values[1].reshape(shape), values[2], values[3]


def device_body(*args):
    fields, _, w_qkv, _, w_merge, w_up, w_down, _ = args
    fits = (
        lax.axis_size("rows") == 2
        and lax.axis_size("cols") == 4
        and lax.axis_size("dp") % 2 == 0
        and fields.shape[:2] == (WIN, WIN)
        and w_up.shape[0] % 128 == 0
        and w_up.shape[1] % 128 == 0
        and w_merge.shape[1] % 64 == 0
        and fields.shape[-1] % 128 == 0
    )
    return fused(*args) if fits else local(*args)


def solution(mesh):
    return jax.shard_map(
        device_body,
        mesh=mesh,
        in_specs=(
            P(("dp", "rows"), "cols", None),
            P(),
            P(),
            P(),
            P(None, "cols"),
            P("rows", "cols"),
            P("cols", "rows"),
            P(("dp", "rows"), "cols", None),
        ),
        out_specs=(
            P(("dp", "rows"), "cols", None),
            P(("dp", "rows"), "cols", None),
            P("rows", ("dp", "cols")),
            P("cols", ("dp", "rows")),
        ),
        check_vma=False,
    )
```

```python
import jax
import jax.numpy as jnp
import numpy as np
from jax import lax
from jax.experimental import pallas as pl
from jax.experimental.pallas import tpu as pltpu
from jax.sharding import PartitionSpec as P

WIN = 16


eps_norm = 1e-05
eps_unit = 1e-06
N_SENDS = 8
N_RECVS = 40


def padded_2(cells, sides, width):
    for axis, dim in sides:
        count = lax.axis_size(axis)
        head = lax.slice_in_dim(cells, 0, width, axis=dim)
        tail = lax.slice_in_dim(cells, cells.shape[dim] - width, cells.shape[dim], axis=dim)
        cells = jnp.concatenate(
            [
                lax.ppermute(tail, axis, [(i, (i + 1) % count) for i in range(count)]),
                cells,
                lax.ppermute(head, axis, [((i + 1) % count, i) for i in range(count)]),
            ],
            axis=dim,
        )
    return cells


def layer_norm(value):
    average = jnp.mean(value, axis=-1, keepdims=True)
    centred = value - average
    spread = jnp.mean(centred * centred, axis=-1, keepdims=True)
    inverse = lax.rsqrt(spread + eps_norm)
    return (centred * inverse, inverse)


def norm_slope(upstream, normed, inverse):
    first_mean = jnp.mean(upstream, axis=-1, keepdims=True)
    second_mean = jnp.mean(upstream * normed, axis=-1, keepdims=True)
    return inverse * (upstream - first_mean - normed * second_mean)


def unit_heads(value, head_count):
    shaped = value.reshape(value.shape[:-1] + (head_count, value.shape[-1] // head_count))
    squares = jnp.sum(shaped * shaped, axis=-1, keepdims=True)
    return (shaped * lax.rsqrt(squares + eps_unit)).reshape(value.shape)


def windows_of(field_grid, window):
    grid_rows, grid_cols, channels = field_grid.shape
    shaped = field_grid.reshape(grid_rows // window, window, grid_cols // window, window, channels)
    return shaped.transpose(0, 2, 1, 3, 4).reshape(-1, window * window, channels)


def grid_of(blocks, grid_rows, grid_cols, window):
    channels = blocks.shape[-1]
    shaped = blocks.reshape(grid_rows // window, grid_cols // window, window, window, channels)
    return shaped.transpose(0, 2, 1, 3, 4).reshape(grid_rows, grid_cols, channels)


def attend(queries, key_rows, value_rows, logit_scale, head_count):
    number, window_size, channels = queries.shape
    width_head = channels // head_count
    query_heads = queries.reshape(number, window_size, head_count, width_head)
    key_heads = key_rows.reshape(number, window_size, head_count, width_head)
    value_heads = value_rows.reshape(number, window_size, head_count, width_head)
    scores = jnp.einsum(
        "wqhd,wkhd->whqk", query_heads, key_heads, preferred_element_type=jnp.float32
    )
    weights = jnp.exp(scores * logit_scale[None, :, None, None])
    weights = (weights / jnp.sum(weights, axis=-1, keepdims=True)).astype(jnp.bfloat16)
    mixed_out = jnp.einsum(
        "whqk,wkhd->wqhd", weights, value_heads, preferred_element_type=jnp.float32
    )
    return mixed_out.reshape(number, window_size, channels)


def merge_patches(field_grid):
    quarters = (
        field_grid[0::2, 0::2],
        field_grid[1::2, 0::2],
        field_grid[0::2, 1::2],
        field_grid[1::2, 1::2],
    )
    return jnp.concatenate(quarters, axis=-1)


def exact_gelu(value):
    return jax.nn.gelu(value, approximate=False)


def local(fields, logit_scale, w_qkv, w_proj, w_merge, w_up, w_down, cotangent):
    tile_rows, tile_cols, channels = fields.shape
    offset = WIN // 2
    head_count = logit_scale.shape[0]
    tokens = fields.astype(jnp.bfloat16)
    token_rows = tokens.reshape(-1, channels)
    wide_rows = tile_rows + WIN
    wide_cols = tile_cols + WIN
    widened = padded_2(tokens, (("rows", 0), ("cols", 1)), offset)
    wide_proj = jnp.dot(
        widened.reshape(-1, channels), w_qkv[:, channels:], preferred_element_type=jnp.float32
    )
    key_grid = unit_heads(wide_proj[:, :channels], head_count).astype(jnp.bfloat16)
    value_grid = wide_proj[:, channels:].astype(jnp.bfloat16)
    query_raw = jnp.dot(token_rows, w_qkv[:, :channels], preferred_element_type=jnp.float32)
    queries = (
        unit_heads(query_raw, head_count)
        .astype(jnp.bfloat16)
        .reshape(tile_rows, tile_cols, channels)
    )
    padded = jnp.pad(queries, ((offset, offset), (offset, offset), (0, 0)))
    key_blocks = windows_of(key_grid.reshape(wide_rows, wide_cols, channels), WIN)
    value_blocks = windows_of(value_grid.reshape(wide_rows, wide_cols, channels), WIN)
    mixed = attend(windows_of(padded, WIN), key_blocks, value_blocks, logit_scale, head_count)
    mixed = grid_of(mixed, wide_rows, wide_cols, WIN)[
        offset : offset + tile_rows, offset : offset + tile_cols
    ]
    mixed = mixed.astype(jnp.bfloat16).reshape(-1, channels)
    normed, _ = layer_norm(jnp.dot(mixed, w_proj, preferred_element_type=jnp.float32))
    stream = fields + normed.reshape(fields.shape)
    merged = merge_patches(stream).astype(jnp.bfloat16)
    merged_rows = merged.reshape(-1, merged.shape[-1])
    own_count = merged_rows.shape[0]
    partial_band = jnp.dot(
        lax.all_gather(merged_rows, "cols", axis=0, tiled=True),
        w_merge,
        preferred_element_type=jnp.float32,
    )
    projected_band = lax.all_gather(
        partial_band.astype(jnp.bfloat16), "cols", axis=1, tiled=True
    ).astype(partial_band.dtype)
    level_band, _ = layer_norm(projected_band)
    level_b = level_band.astype(jnp.bfloat16)
    level_own = lax.dynamic_slice_in_dim(
        level_band, lax.axis_index("cols") * own_count, own_count, 0
    )
    up_full = lax.all_gather(w_up, "rows", axis=0, tiled=True)
    down_full = lax.all_gather(w_down, "rows", axis=1, tiled=True)
    hidden_pre = jnp.dot(level_b, up_full, preferred_element_type=jnp.float32)
    hidden = exact_gelu(hidden_pre).astype(jnp.bfloat16)
    rows_part = hidden
    branch_out = lax.psum_scatter(
        jnp.dot(rows_part, down_full, preferred_element_type=jnp.float32).astype(jnp.bfloat16),
        "cols",
        scatter_dimension=0,
        tiled=True,
    ).astype(jnp.float32)
    branch_norm, branch_inv = layer_norm(branch_out)
    coarse = level_own + branch_norm
    upstream = cotangent.astype(jnp.float32).reshape(own_count, -1)
    slope_own = norm_slope(upstream, branch_norm, branch_inv).astype(jnp.bfloat16)
    slope_out = lax.all_gather(slope_own, "cols", axis=0, tiled=True)
    slope_hidden = jnp.einsum("tc,fc->tf", slope_out, down_full, preferred_element_type=jnp.float32)
    _, pullback = jax.vjp(exact_gelu, hidden_pre)
    slope_pre = pullback(slope_hidden)[0].astype(jnp.bfloat16)
    rows_part = slope_pre
    slope_input = lax.psum_scatter(
        jnp.einsum("tf,cf->tc", rows_part, up_full, preferred_element_type=jnp.float32).astype(
            jnp.bfloat16
        ),
        "cols",
        scatter_dimension=0,
        tiled=True,
    ).astype(jnp.float32)
    grad_coarse = upstream + slope_input
    term_up = jnp.einsum("tc,tf->cf", level_b, slope_pre, preferred_element_type=jnp.float32)
    term_down = jnp.einsum("tf,tc->fc", hidden, slope_out, preferred_element_type=jnp.float32)
    grad_up, grad_down = (
        lax.psum_scatter(
            term_up.astype(jnp.bfloat16), "rows", scatter_dimension=0, tiled=True
        ).astype(jnp.float32),
        lax.psum_scatter(
            term_down.astype(jnp.bfloat16), "rows", scatter_dimension=1, tiled=True
        ).astype(jnp.float32),
    )
    coarse_shape = (tile_rows // 2, tile_cols // 2, coarse.shape[-1])
    return (coarse.reshape(coarse_shape), grad_coarse.reshape(coarse_shape), grad_up, grad_down)


def _ln(value):
    average = jnp.mean(value, axis=-1, keepdims=True)
    centred = value - average
    spread = jnp.mean(centred * centred, axis=-1, keepdims=True)
    inverse = lax.rsqrt(spread + eps_norm)
    return centred * inverse, inverse


def _dot(a, b, ca=1, cb=0):
    return lax.dot_general(
        a, b, (((ca,), (cb,)), ((), ())), preferred_element_type=jnp.float32
    )


def fused_kernel(
    fields_h, logit_h, w_qkv_h, w_proj_h, w_merge, w_up, w_down, cot_h,
    coarse, gcoarse, gup, gdown,
    fields, logit, w_qkv, w_proj, cot,
    sendq, winq, mixw, mixq, perm, wm, proj, up, down, up_t, down_t,
    lvl, hid, lvl_t, hid_t, dgel, bsend, brecv, slo, spre, gsend, grecv, loc, sends, recvs,
):
    f32, bf16 = jnp.float32, jnp.bfloat16
    i, j = lax.axis_index("rows"), lax.axis_index("cols")
    ni, nj = lax.axis_size("rows"), lax.axis_size("cols")
    z = lax.axis_index("dp")
    beside = z + 1 - 2 * (z % 2)
    bit = z % 2
    half_side = WIN // 2
    quad = half_side * half_side
    ch = fields.shape[-1]
    c4 = cot.shape[-1]
    own = cot.shape[0]
    half = c4 // ni
    ff = w_up.shape[1]
    share = w_merge.shape[0]
    heads = logit.shape[0]
    width = ch // heads
    other = (i + 1) % ni
    prev_j, next_j = (j + nj - 1) % nj, (j + 1) % nj
    partner = j + 1 - 2 * (j % 2)
    far = (j + 2) % nj
    far_partner = (partner + 2) % nj
    peers = (partner, far, far_partner)
    s_quads, s_back, s_merge, s_up, s_down, s_lvl, s_slo, s_sum = range(N_SENDS)
    numbers = iter(range(N_RECVS))

    def remote(src, dst, row, col, send, recv=None, part=z):
        n = next(numbers) if recv is None else recv
        return pltpu.make_async_remote_copy(
            src_ref=src, dst_ref=dst, send_sem=sends.at[send], recv_sem=recvs.at[n],
            device_id={"rows": row, "cols": col, "dp": part},
            device_id_type=pl.DeviceIdType.MESH,
        )

    def all_of(ref, sem):
        pltpu.make_async_copy(ref, ref, sem).wait()

    first_copy = pltpu.make_async_copy(fields_h, fields, loc.at[0])
    first_copy.start()
    barrier = pltpu.get_barrier_semaphore()
    greet = [(i, p) for p in peers] + [(other, j), (other, prev_j), (other, next_j)]
    for row, col in greet:
        pl.semaphore_signal(
            barrier, inc=1, device_id={"rows": row, "cols": col},
            device_id_type=pl.DeviceIdType.MESH,
        )
    pl.semaphore_signal(
        barrier, inc=1, device_id={"dp": beside}, device_id_type=pl.DeviceIdType.MESH
    )

    def rows_at(start, size):
        return pl.ds(pl.multiple_of(start, 16), size)

    locals_ = [first_copy] + [
        pltpu.make_async_copy(src, dst, loc.at[n + 1])
        for n, (src, dst) in enumerate((
            (w_qkv_h, w_qkv),
            (w_proj_h, w_proj),
            (cot_h, cot),
            (w_merge, wm.at[rows_at(j * share, share), :]),
            (w_up, up.at[rows_at(i * half, half), :]),
            (w_down, down.at[i]),
            (logit_h, logit),
        ))
    ]
    lane = lax.broadcasted_iota(jnp.int32, (ch, ch), 0) // width
    lane_t = lax.broadcasted_iota(jnp.int32, (ch, ch), 1) // width
    block_ones = (lane == lane_t).astype(f32).astype(bf16)
    rows_out = lax.broadcasted_iota(jnp.int32, (4 * quad, 4 * quad), 0)
    cols_in = lax.broadcasted_iota(jnp.int32, (4 * quad, 4 * quad), 1)
    which, place = rows_out // quad, rows_out % quad
    r = 2 * (place // half_side) + which % 2
    c = 2 * (place % half_side) + which // 2
    source = ((r // half_side) * 2 + c // half_side) * quad + (r % half_side) * half_side + c % half_side
    perm[...] = (source == cols_in).astype(f32).astype(bf16)

    def quarter(a, b):
        part = fields[a * half_side:(a + 1) * half_side, b * half_side:(b + 1) * half_side, :]
        return part.reshape(quad, ch)

    locals_[0].wait()
    for k in range(3):
        sendq[k] = quarter(k // 2, k % 2).astype(bf16)
    winq[3] = quarter(1, 1).astype(bf16)
    pl.semaphore_wait(barrier, len(greet) + 1)

    targets = ((other, prev_j), (other, j), (i, prev_j))
    backs = ((other, next_j), (other, j), (i, next_j))
    r_quads = next(numbers)
    quads = [
        remote(sendq.at[k], winq.at[k], *targets[k], s_quads, r_quads if k < 2 else None)
        for k in range(3)
    ]
    for c in quads:
        c.start()

    part_m = share // 6
    mine_at, theirs_at = bit * part_m, (1 - bit) * part_m

    pieces_m = ((mine_at, part_m), (2 * part_m, 2 * part_m), (4 * part_m, 2 * part_m), (theirs_at, part_m))

    def merge_out(start, size):
        return remote(
            w_merge.at[rows_at(start, size), :], wm.at[rows_at(j * share + start, size), :],
            i, far, s_merge,
        )

    r_on = next(numbers)

    def merge_pass(start, size):
        at = rows_at(far * share + start, size)
        return remote(wm.at[at, :], wm.at[at, :], i, partner, s_merge, r_on)

    merge_far = [merge_out(*piece) for piece in pieces_m[:3]]
    merge_on = [merge_pass(*piece) for piece in pieces_m]
    at = rows_at(far * share + mine_at, part_m)
    merge_side = remote(wm.at[at, :], wm.at[at, :], i, j, s_merge, part=beside)
    merge_beside = remote(w_merge, wm.at[rows_at(j * share, share), :], i, partner, s_merge)

    part_u = half // 8
    r_up = next(numbers)

    def up_piece(start, size):
        here = rows_at(other * half + bit * 4 * part_u + start, size)
        return (
            remote(
                w_up.at[rows_at(bit * 4 * part_u + start, size), :],
                up.at[rows_at(i * half + bit * 4 * part_u + start, size), :], other, j, s_up,
            ),
            remote(up.at[here, :], up.at[here, :], i, j, s_up, r_up, beside),
        )

    up_out, up_on = zip(up_piece(0, 3 * part_u), up_piece(3 * part_u, part_u))
    part_d = ff // 4
    spans = (rows_at(bit * part_d, part_d), pl.ds(2 * part_d, 2 * part_d))
    down_out = [remote(w_down.at[at, :], down.at[i, at, :], other, j, s_down) for at in spans]
    down_on = remote(
        down.at[other, spans[0], :], down.at[other, spans[0], :], i, j, s_down, part=beside
    )
    for c in (merge_far[0], merge_beside, up_out[0]):
        c.start()
    for c in locals_[1:]:
        c.start()

    def unit(value):
        squares = value * value
        top = squares.astype(bf16)
        low = (squares - top.astype(f32)).astype(bf16)
        total = _dot(top, block_ones) + _dot(low, block_ones)
        return (value * lax.rsqrt(total + eps_unit)).astype(bf16)

    def project(first):
        tokens = winq[first:first + 2].reshape(2 * quad, ch)
        return (
            unit(_dot(tokens, w_qkv[:, :ch])),
            unit(_dot(tokens, w_qkv[:, ch:2 * ch])),
            _dot(tokens, w_qkv[:, 2 * ch:]).astype(bf16),
        )

    def turn_up(k):
        up_t[k] = up[rows_at(k * half, half), :].T

    def turn_down(k):
        down_t[rows_at(k * half, half), :] = down[k].T

    locals_[1].wait()
    quads[2].wait_recv()
    late = project(2)
    merge_far[1].start()
    all_of(winq.at[pl.ds(0, 2)], recvs.at[r_quads])
    early = project(0)
    qhat, khat, vals = (jnp.concatenate([a, b], axis=0) for a, b in zip(early, late))
    merge_far[0].wait_recv()
    merge_side.start()
    merge_on[0].start()
    locals_[7].wait()
    per = 128 // width
    lanes = lax.broadcasted_iota(jnp.int32, (4 * quad, 128), 1) // width
    for b in range(ch // 128):
        cut = slice(b * 128, (b + 1) * 128)
        qb, kb, vb = qhat[:, cut], khat[:, cut], vals[:, cut]
        acc = None
        for t in range(per):
            mine = lanes == t
            zero = jnp.zeros_like(qb)
            scores = _dot(jnp.where(mine, qb, zero), kb, 1, 1) * logit[b * per + t]
            weights = jnp.exp(scores)
            weights = (weights / jnp.sum(weights, axis=-1, keepdims=True)).astype(bf16)
            term = _dot(weights, jnp.where(mine, vb, zero))
            acc = term if acc is None else acc + term
        mixw[:, :, cut] = acc.astype(bf16).reshape(4, quad, 128)
    r_back = next(numbers)
    for k in range(3):
        remote(mixw.at[k], mixq.at[k], *backs[k], s_back, r_back).start()
    merge_far[2].start()
    up_out[1].start()
    mixq[3] = mixw[3]
    locals_[5].wait()
    locals_[6].wait()
    turn_up(i)
    turn_down(i)
    up_out[0].wait_recv()
    up_on[0].start()
    merge_far[1].wait_recv()
    merge_on[1].start()
    down_out[0].start()
    merge_side.wait_recv()
    merge_on[3].start()
    locals_[2].wait()
    all_of(mixq.at[pl.ds(0, 3)], recvs.at[r_back])
    normed, _ = _ln(_dot(mixq[...].reshape(4 * quad, ch), w_proj[...]))
    flat = jnp.concatenate([quarter(k // 2, k % 2) for k in range(4)], axis=0)
    stream = (flat + normed).astype(bf16)
    picked = _dot(perm[...], stream).astype(bf16)
    merged = jnp.concatenate([picked[k * quad:(k + 1) * quad] for k in range(4)], axis=1)
    up_out[1].wait_recv()
    up_on[1].start()
    down_out[1].start()

    pair = j // 2
    pairs = (pair, (pair + 1) % 2)

    def project_pair(p):
        at = pl.ds(pl.multiple_of(p * 2 * share, 128), 2 * share)
        proj[p] = _dot(merged, wm[at, :], 1, 1)

    locals_[4].wait()
    merge_beside.wait_recv()
    project_pair(pairs[0])
    merge_far[2].wait_recv()
    merge_on[2].start()
    all_of(wm.at[rows_at(far_partner * share, share), :], recvs.at[r_on])
    project_pair(pairs[1])
    level, _ = _ln(jnp.concatenate([proj[p] for p in range(2)], axis=1))

    def put(ref, value):
        for k in range(ni):
            ref[0, j, k] = value[:, k * half:(k + 1) * half].astype(bf16)

    def take(ref, b, p):
        return jnp.concatenate(
            [ref[b, pl.ds(p * 2, 2), k].reshape(2 * own, half) for k in range(ni)], axis=1
        )

    put(lvl, level)
    r_gather = [next(numbers) for _ in range(3)]
    r_sum = [next(numbers) for _ in range(4)]

    class Gathered:
        def __init__(self, ref, group):
            def send(b, slot, to, row, col, recv=None):
                return remote(ref.at[b, slot], ref.at[to, slot], row, col, group, recv)

            self.out_far = send(0, j, 0, i, far, r_gather[0])
            self.out_partner = send(0, j, 0, i, partner, r_gather[1])
            self.onward = send(0, far, 0, i, partner, r_gather[2])
            self.across = [send(0, s, 1, other, j) for s in (j, far)]
            self.across_on = [send(1, s, 1, i, partner) for s in (j, far)]

    levels = Gathered(lvl, s_lvl)
    levels.out_far.start()
    levels.out_partner.start()

    def forward(b, p):
        pre = _dot(take(lvl, b, p), up[...])
        cdf = 0.5 * (1.0 + lax.erf(pre * np.float32(np.sqrt(0.5))))
        hid[b, p] = (pre * cdf).astype(bf16)
        dgel[b, p] = cdf + pre * (jnp.exp(-0.5 * pre * pre) * np.float32(1 / np.sqrt(2 * np.pi)))

    def branch(p, k):
        bsend[pl.ds(p * 2, 2), k] = _dot(hid[0, p], down[k]).astype(bf16).reshape(2, own, half)

    def turn_tokens(b):
        lvl_t[b] = lvl[b, :, i].reshape(nj * own, half).T
        hid_t[b] = hid[b].reshape(nj * own, ff).T

    class Reduced:
        def __init__(self, sent, got, n, k, group):
            self.sent, self.got, self.k = sent, got, k
            self.first = remote(sent.at[far_partner, k], got.at[1, k], i, partner, group, r_sum[n])
            self.near = remote(sent.at[partner, k], got.at[0, k], i, partner, s_sum, r_sum[2])
            self.last = remote(got.at[3, k], got.at[2, k], i, far, s_sum, r_sum[3])

        def pass_on(self):
            self.first.wait_recv()
            k = self.k
            self.got[3, k] = (self.sent[far, k].astype(f32) + self.got[1, k].astype(f32)).astype(bf16)
            self.last.start()

    def total_of(sent, got):
        all_of(got.at[0], recvs.at[r_sum[2]])
        all_of(got.at[2], recvs.at[r_sum[3]])
        total = sent[j].astype(f32) + got[0].astype(f32) + got[2].astype(f32)
        return jnp.concatenate([total[k] for k in range(ni)], axis=1)

    branches = [Reduced(bsend, brecv, n, k, s_lvl) for n, k in enumerate((i, other))]
    down_out[0].wait_recv()
    down_on.start()
    all_of(up.at[rows_at(other * half + (1 - bit) * 4 * part_u, 4 * part_u), :], recvs.at[r_up])
    levels.out_partner.wait_recv()
    forward(0, pairs[0])
    branch(pairs[0], i)
    levels.out_far.wait_recv()
    levels.onward.start()
    turn_up(other)
    levels.onward.wait_recv()
    forward(0, pairs[1])
    branch(pairs[1], i)
    branches[0].first.start()
    branches[0].near.start()
    turn_tokens(0)
    down_out[1].wait_recv()
    levels.across[0].start()
    levels.across[1].start()
    down_on.wait_recv()
    branch(pairs[1], other)
    branches[1].first.start()
    branches[0].pass_on()
    branch(pairs[0], other)
    branches[1].near.start()
    branches[1].pass_on()
    turn_down(other)
    locals_[3].wait()
    total = total_of(bsend, brecv)
    norm, inverse = _ln(total)
    coarse[...] = level + norm
    g = cot[...].astype(f32)
    put(
        slo,
        inverse * (
            g - jnp.mean(g, axis=-1, keepdims=True)
            - norm * jnp.mean(g * norm, axis=-1, keepdims=True)
        ),
    )
    slopes = Gathered(slo, s_slo)
    slopes.out_far.start()
    slopes.out_partner.start()
    slopes.across[0].start()
    levels.across[0].wait_recv()
    levels.across_on[0].start()
    levels.across[1].wait_recv()
    levels.across_on[1].start()

    def backward(b, p):
        spre[b, p] = (dgel[b, p] * _dot(take(slo, b, p), down_t[...])).astype(bf16)

    def slope_in(p):
        turned = jnp.concatenate([up_t[k] for k in range(ni)], axis=1)
        out = _dot(spre[0, p], turned).astype(bf16)
        for k in range(ni):
            gsend[pl.ds(p * 2, 2), k] = out[:, k * half:(k + 1) * half].reshape(2, own, half)

    grads = [Reduced(gsend, grecv, k, k, s_slo) for k in range(ni)]
    slopes.out_partner.wait_recv()
    backward(0, pairs[0])
    slope_in(pairs[0])
    for k in range(ni):
        grads[k].near.start()
    levels.across_on[0].wait_recv()
    levels.across_on[1].wait_recv()
    forward(1, pairs[0])
    forward(1, pairs[1])
    turn_tokens(1)
    slopes.out_far.wait_recv()
    slopes.onward.start()
    slopes.across[1].start()
    slopes.across[0].wait_recv()
    slopes.across_on[0].start()
    slopes.onward.wait_recv()
    backward(0, pairs[1])
    slope_in(pairs[1])
    for k in range(ni):
        grads[k].first.start()
    slopes.across_on[0].wait_recv()
    backward(1, pairs[0])
    for c in grads:
        c.pass_on()

    def weight_terms(b):
        sp = spre[b].reshape(nj * own, ff)
        return _dot(lvl_t[b], sp), _dot(hid_t[b], slo[b, :, i].reshape(nj * own, half))

    gup[...], gdown[...] = weight_terms(0)
    slopes.across[1].wait_recv()
    slopes.across_on[1].start()
    slopes.across_on[1].wait_recv()
    backward(1, pairs[1])
    terms = weight_terms(1)
    gup[...] += terms[0]
    gdown[...] += terms[1]
    total = total_of(gsend, grecv)
    gcoarse[...] = g + total
    for ref, n in (
        (sendq, s_quads), (mixw.at[pl.ds(0, 3)], s_back), (wm.at[pl.ds(0, 3 * share), :], s_merge),
        (up.at[pl.ds(0, half), :], s_up), (down.at[0], s_down), (lvl, s_lvl), (slo, s_slo), (bsend, s_sum),
    ):
        all_of(ref, sends.at[n])
def store_kernel(coarse_in, gcoarse_in, gup_in, gdown_in, coarse, gcoarse, gup, gdown, sem):
    pairs = ((gup_in, gup), (gdown_in, gdown), (coarse_in, coarse), (gcoarse_in, gcoarse))
    copies = [pltpu.make_async_copy(src, dst, sem.at[n]) for n, (src, dst) in enumerate(pairs)]
    for c in copies:
        c.start()
    for c in copies:
        c.wait()


def fused(fields, logit_scale, w_qkv, w_proj, w_merge, w_up, w_down, cotangent):
    tile_rows, tile_cols, ch = fields.shape
    ni, nj = lax.axis_size("rows"), lax.axis_size("cols")
    own = cotangent.shape[0] * cotangent.shape[1]
    c4 = cotangent.shape[-1]
    half, ff = w_up.shape
    f32, bf16 = jnp.float32, jnp.bfloat16
    quad = (WIN // 2) ** 2
    hb = pl.BlockSpec(memory_space=pltpu.HBM)
    anywhere = pl.BlockSpec(memory_space=pl.ANY)
    dma = pltpu.SemaphoreType.DMA
    outs = (
        jax.ShapeDtypeStruct((own, c4), f32),
        jax.ShapeDtypeStruct((own, c4), f32),
        jax.ShapeDtypeStruct((half, ff), f32),
        jax.ShapeDtypeStruct((ff, half), f32),
    )
    gathered = pltpu.VMEM((ni, nj, ni, own, half), bf16)
    operands = [fields, logit_scale, w_qkv, w_proj, w_merge.T, w_up, w_down, cotangent.reshape(own, c4)]
    operands = [pltpu.with_memory_space_constraint(v, pltpu.HBM) for v in operands]
    values = pl.pallas_call(
        fused_kernel,
        out_shape=outs,
        in_specs=[hb] * 8,
        out_specs=(pl.BlockSpec(memory_space=pltpu.VMEM),) * 4,
        scratch_shapes=[
            pltpu.VMEM(fields.shape, f32),
            pltpu.SMEM(logit_scale.shape, f32),
            pltpu.VMEM(w_qkv.shape, bf16),
            pltpu.VMEM(w_proj.shape, bf16),
            pltpu.VMEM((own, c4), bf16),
            pltpu.VMEM((3, quad, ch), bf16),
            pltpu.VMEM((4, quad, ch), bf16),
            pltpu.VMEM((4, quad, ch), bf16),
            pltpu.VMEM((4, quad, ch), bf16),
            pltpu.VMEM((4 * quad, 4 * quad), bf16),
            pltpu.VMEM((c4, w_merge.shape[0]), bf16),
            pltpu.VMEM((2, own, c4 // 2), f32),
            pltpu.VMEM((c4, ff), bf16),
            pltpu.VMEM((ni, ff, half), bf16),
            pltpu.VMEM((ni, ff, half), bf16),
            pltpu.VMEM((c4, ff), bf16),
            gathered,
            pltpu.VMEM((ni, 2, 2 * own, ff), bf16),
            pltpu.VMEM((ni, half, nj * own), bf16),
            pltpu.VMEM((ni, ff, nj * own), bf16),
            pltpu.VMEM((ni, 2, 2 * own, ff), f32),
            pltpu.VMEM((nj, ni, own, half), bf16),
            pltpu.VMEM((4, ni, own, half), bf16),
            gathered,
            pltpu.VMEM((ni, 2, 2 * own, ff), bf16),
            pltpu.VMEM((nj, ni, own, half), bf16),
            pltpu.VMEM((4, ni, own, half), bf16),
            dma((8,)),
            dma((N_SENDS,)),
            dma((N_RECVS,)),
        ],
        compiler_params=pltpu.CompilerParams(
            collective_id=0, has_side_effects=True, vmem_limit_bytes=44 << 20
        ),
    )(*operands)
    values = pl.pallas_call(
        store_kernel,
        out_shape=outs,
        in_specs=[anywhere] * 4,
        out_specs=(hb,) * 4,
        scratch_shapes=[dma((4,))],
        compiler_params=pltpu.CompilerParams(vmem_limit_bytes=4 << 20),
    )(*values)
    shape = (tile_rows // 2, tile_cols // 2, c4)
    return values[0].reshape(shape), values[1].reshape(shape), values[2], values[3]


def device_body(*args):
    fields, _, w_qkv, _, w_merge, w_up, w_down, _ = args
    fits = (
        lax.axis_size("rows") == 2
        and lax.axis_size("cols") == 4
        and lax.axis_size("dp") % 2 == 0
        and fields.shape[:2] == (WIN, WIN)
        and w_up.shape[0] % 128 == 0
        and w_up.shape[1] % 128 == 0
        and w_merge.shape[1] % 96 == 0
        and fields.shape[-1] % 128 == 0
    )
    return fused(*args) if fits else local(*args)


def solution(mesh):
    return jax.shard_map(
        device_body,
        mesh=mesh,
        in_specs=(
            P(("dp", "rows"), "cols", None),
            P(),
            P(),
            P(),
            P(None, "cols"),
            P("rows", "cols"),
            P("cols", "rows"),
            P(("dp", "rows"), "cols", None),
        ),
        out_specs=(
            P(("dp", "rows"), "cols", None),
            P(("dp", "rows"), "cols", None),
            P("rows", ("dp", "cols")),
            P("cols", ("dp", "rows")),
        ),
        check_vma=False,
    )
```

```python
import jax
import jax.numpy as jnp
import numpy as np
from jax import lax
from jax.experimental import pallas as pl
from jax.experimental.pallas import tpu as pltpu
from jax.sharding import PartitionSpec as P

WIN = 16


eps_norm = 1e-05
eps_unit = 1e-06
N_SENDS = 8
N_RECVS = 36


def padded_2(cells, sides, width):
    for axis, dim in sides:
        count = lax.axis_size(axis)
        head = lax.slice_in_dim(cells, 0, width, axis=dim)
        tail = lax.slice_in_dim(cells, cells.shape[dim] - width, cells.shape[dim], axis=dim)
        cells = jnp.concatenate(
            [
                lax.ppermute(tail, axis, [(i, (i + 1) % count) for i in range(count)]),
                cells,
                lax.ppermute(head, axis, [((i + 1) % count, i) for i in range(count)]),
            ],
            axis=dim,
        )
    return cells


def layer_norm(value):
    average = jnp.mean(value, axis=-1, keepdims=True)
    centred = value - average
    spread = jnp.mean(centred * centred, axis=-1, keepdims=True)
    inverse = lax.rsqrt(spread + eps_norm)
    return (centred * inverse, inverse)


def norm_slope(upstream, normed, inverse):
    first_mean = jnp.mean(upstream, axis=-1, keepdims=True)
    second_mean = jnp.mean(upstream * normed, axis=-1, keepdims=True)
    return inverse * (upstream - first_mean - normed * second_mean)


def unit_heads(value, head_count):
    shaped = value.reshape(value.shape[:-1] + (head_count, value.shape[-1] // head_count))
    squares = jnp.sum(shaped * shaped, axis=-1, keepdims=True)
    return (shaped * lax.rsqrt(squares + eps_unit)).reshape(value.shape)


def windows_of(field_grid, window):
    grid_rows, grid_cols, channels = field_grid.shape
    shaped = field_grid.reshape(grid_rows // window, window, grid_cols // window, window, channels)
    return shaped.transpose(0, 2, 1, 3, 4).reshape(-1, window * window, channels)


def grid_of(blocks, grid_rows, grid_cols, window):
    channels = blocks.shape[-1]
    shaped = blocks.reshape(grid_rows // window, grid_cols // window, window, window, channels)
    return shaped.transpose(0, 2, 1, 3, 4).reshape(grid_rows, grid_cols, channels)


def attend(queries, key_rows, value_rows, logit_scale, head_count):
    number, window_size, channels = queries.shape
    width_head = channels // head_count
    query_heads = queries.reshape(number, window_size, head_count, width_head)
    key_heads = key_rows.reshape(number, window_size, head_count, width_head)
    value_heads = value_rows.reshape(number, window_size, head_count, width_head)
    scores = jnp.einsum(
        "wqhd,wkhd->whqk", query_heads, key_heads, preferred_element_type=jnp.float32
    )
    weights = jnp.exp(scores * logit_scale[None, :, None, None])
    weights = (weights / jnp.sum(weights, axis=-1, keepdims=True)).astype(jnp.bfloat16)
    mixed_out = jnp.einsum(
        "whqk,wkhd->wqhd", weights, value_heads, preferred_element_type=jnp.float32
    )
    return mixed_out.reshape(number, window_size, channels)


def merge_patches(field_grid):
    quarters = (
        field_grid[0::2, 0::2],
        field_grid[1::2, 0::2],
        field_grid[0::2, 1::2],
        field_grid[1::2, 1::2],
    )
    return jnp.concatenate(quarters, axis=-1)


def exact_gelu(value):
    return jax.nn.gelu(value, approximate=False)


def local(fields, logit_scale, w_qkv, w_proj, w_merge, w_up, w_down, cotangent):
    tile_rows, tile_cols, channels = fields.shape
    offset = WIN // 2
    head_count = logit_scale.shape[0]
    tokens = fields.astype(jnp.bfloat16)
    token_rows = tokens.reshape(-1, channels)
    wide_rows = tile_rows + WIN
    wide_cols = tile_cols + WIN
    widened = padded_2(tokens, (("rows", 0), ("cols", 1)), offset)
    wide_proj = jnp.dot(
        widened.reshape(-1, channels), w_qkv[:, channels:], preferred_element_type=jnp.float32
    )
    key_grid = unit_heads(wide_proj[:, :channels], head_count).astype(jnp.bfloat16)
    value_grid = wide_proj[:, channels:].astype(jnp.bfloat16)
    query_raw = jnp.dot(token_rows, w_qkv[:, :channels], preferred_element_type=jnp.float32)
    queries = (
        unit_heads(query_raw, head_count)
        .astype(jnp.bfloat16)
        .reshape(tile_rows, tile_cols, channels)
    )
    padded = jnp.pad(queries, ((offset, offset), (offset, offset), (0, 0)))
    key_blocks = windows_of(key_grid.reshape(wide_rows, wide_cols, channels), WIN)
    value_blocks = windows_of(value_grid.reshape(wide_rows, wide_cols, channels), WIN)
    mixed = attend(windows_of(padded, WIN), key_blocks, value_blocks, logit_scale, head_count)
    mixed = grid_of(mixed, wide_rows, wide_cols, WIN)[
        offset : offset + tile_rows, offset : offset + tile_cols
    ]
    mixed = mixed.astype(jnp.bfloat16).reshape(-1, channels)
    normed, _ = layer_norm(jnp.dot(mixed, w_proj, preferred_element_type=jnp.float32))
    stream = fields + normed.reshape(fields.shape)
    merged = merge_patches(stream).astype(jnp.bfloat16)
    merged_rows = merged.reshape(-1, merged.shape[-1])
    own_count = merged_rows.shape[0]
    partial_band = jnp.dot(
        lax.all_gather(merged_rows, "cols", axis=0, tiled=True),
        w_merge,
        preferred_element_type=jnp.float32,
    )
    projected_band = lax.all_gather(
        partial_band.astype(jnp.bfloat16), "cols", axis=1, tiled=True
    ).astype(partial_band.dtype)
    level_band, _ = layer_norm(projected_band)
    level_b = level_band.astype(jnp.bfloat16)
    level_own = lax.dynamic_slice_in_dim(
        level_band, lax.axis_index("cols") * own_count, own_count, 0
    )
    up_full = lax.all_gather(w_up, "rows", axis=0, tiled=True)
    down_full = lax.all_gather(w_down, "rows", axis=1, tiled=True)
    hidden_pre = jnp.dot(level_b, up_full, preferred_element_type=jnp.float32)
    hidden = exact_gelu(hidden_pre).astype(jnp.bfloat16)
    rows_part = hidden
    branch_out = lax.psum_scatter(
        jnp.dot(rows_part, down_full, preferred_element_type=jnp.float32).astype(jnp.bfloat16),
        "cols",
        scatter_dimension=0,
        tiled=True,
    ).astype(jnp.float32)
    branch_norm, branch_inv = layer_norm(branch_out)
    coarse = level_own + branch_norm
    upstream = cotangent.astype(jnp.float32).reshape(own_count, -1)
    slope_own = norm_slope(upstream, branch_norm, branch_inv).astype(jnp.bfloat16)
    slope_out = lax.all_gather(slope_own, "cols", axis=0, tiled=True)
    slope_hidden = jnp.einsum("tc,fc->tf", slope_out, down_full, preferred_element_type=jnp.float32)
    _, pullback = jax.vjp(exact_gelu, hidden_pre)
    slope_pre = pullback(slope_hidden)[0].astype(jnp.bfloat16)
    rows_part = slope_pre
    slope_input = lax.psum_scatter(
        jnp.einsum("tf,cf->tc", rows_part, up_full, preferred_element_type=jnp.float32).astype(
            jnp.bfloat16
        ),
        "cols",
        scatter_dimension=0,
        tiled=True,
    ).astype(jnp.float32)
    grad_coarse = upstream + slope_input
    term_up = jnp.einsum("tc,tf->cf", level_b, slope_pre, preferred_element_type=jnp.float32)
    term_down = jnp.einsum("tf,tc->fc", hidden, slope_out, preferred_element_type=jnp.float32)
    grad_up, grad_down = (
        lax.psum_scatter(
            term_up.astype(jnp.bfloat16), "rows", scatter_dimension=0, tiled=True
        ).astype(jnp.float32),
        lax.psum_scatter(
            term_down.astype(jnp.bfloat16), "rows", scatter_dimension=1, tiled=True
        ).astype(jnp.float32),
    )
    coarse_shape = (tile_rows // 2, tile_cols // 2, coarse.shape[-1])
    return (coarse.reshape(coarse_shape), grad_coarse.reshape(coarse_shape), grad_up, grad_down)


def _ln(value):
    average = jnp.mean(value, axis=-1, keepdims=True)
    centred = value - average
    spread = jnp.mean(centred * centred, axis=-1, keepdims=True)
    inverse = lax.rsqrt(spread + eps_norm)
    return centred * inverse, inverse


def _dot(a, b, ca=1, cb=0):
    return lax.dot_general(
        a, b, (((ca,), (cb,)), ((), ())), preferred_element_type=jnp.float32
    )


def fused_kernel(
    fields_h, logit_h, w_qkv_h, w_proj_h, w_merge, w_up, w_down, cot_h,
    coarse, gcoarse, gup, gdown,
    fields, logit, w_qkv, w_proj, cot,
    sendq, winq, mixw, mixq, perm, wm, proj, up, down, up_t, down_t,
    lvl, hid, lvl_t, hid_t, dgel, bsend, brecv, slo, spre, gsend, grecv, loc, sends, recvs,
):
    f32, bf16 = jnp.float32, jnp.bfloat16
    i, j = lax.axis_index("rows"), lax.axis_index("cols")
    ni, nj = lax.axis_size("rows"), lax.axis_size("cols")
    z = lax.axis_index("dp")
    beside = z + 1 - 2 * (z % 2)
    bit = z % 2
    half_side = WIN // 2
    quad = half_side * half_side
    ch = fields.shape[-1]
    c4 = cot.shape[-1]
    own = cot.shape[0]
    half = c4 // ni
    ff = w_up.shape[1]
    share = w_merge.shape[0]
    heads = logit.shape[0]
    width = ch // heads
    other = (i + 1) % ni
    prev_j, next_j = (j + nj - 1) % nj, (j + 1) % nj
    partner = j + 1 - 2 * (j % 2)
    far = (j + 2) % nj
    far_partner = (partner + 2) % nj
    peers = (partner, far, far_partner)
    s_quads, s_back, s_merge, s_up, s_down, s_lvl, s_slo, s_sum = range(N_SENDS)
    numbers = iter(range(N_RECVS))

    def remote(src, dst, row, col, send, recv=None, part=z):
        n = next(numbers) if recv is None else recv
        return pltpu.make_async_remote_copy(
            src_ref=src, dst_ref=dst, send_sem=sends.at[send], recv_sem=recvs.at[n],
            device_id={"rows": row, "cols": col, "dp": part},
            device_id_type=pl.DeviceIdType.MESH,
        )

    def all_of(ref, sem):
        pltpu.make_async_copy(ref, ref, sem).wait()

    first_copy = pltpu.make_async_copy(fields_h, fields, loc.at[0])
    first_copy.start()
    barrier = pltpu.get_barrier_semaphore()
    greet = [(i, p) for p in peers] + [(other, j), (other, prev_j), (other, next_j)]
    for row, col in greet:
        pl.semaphore_signal(
            barrier, inc=1, device_id={"rows": row, "cols": col},
            device_id_type=pl.DeviceIdType.MESH,
        )
    pl.semaphore_signal(
        barrier, inc=1, device_id={"dp": beside}, device_id_type=pl.DeviceIdType.MESH
    )

    def rows_at(start, size):
        return pl.ds(pl.multiple_of(start, 16), size)

    locals_ = [first_copy] + [
        pltpu.make_async_copy(src, dst, loc.at[n + 1])
        for n, (src, dst) in enumerate((
            (w_qkv_h, w_qkv),
            (w_proj_h, w_proj),
            (cot_h, cot),
            (w_merge, wm.at[rows_at(j * share, share), :]),
            (w_up, up.at[rows_at(i * half, half), :]),
            (w_down, down.at[i]),
            (logit_h, logit),
        ))
    ]
    lane = lax.broadcasted_iota(jnp.int32, (ch, ch), 0) // width
    lane_t = lax.broadcasted_iota(jnp.int32, (ch, ch), 1) // width
    block_ones = (lane == lane_t).astype(f32).astype(bf16)
    rows_out = lax.broadcasted_iota(jnp.int32, (4 * quad, 4 * quad), 0)
    cols_in = lax.broadcasted_iota(jnp.int32, (4 * quad, 4 * quad), 1)
    which, place = rows_out // quad, rows_out % quad
    r = 2 * (place // half_side) + which % 2
    c = 2 * (place % half_side) + which // 2
    source = ((r // half_side) * 2 + c // half_side) * quad + (r % half_side) * half_side + c % half_side
    perm[...] = (source == cols_in).astype(f32).astype(bf16)

    def quarter(a, b):
        part = fields[a * half_side:(a + 1) * half_side, b * half_side:(b + 1) * half_side, :]
        return part.reshape(quad, ch)

    locals_[0].wait()
    for k in range(3):
        sendq[k] = quarter(k // 2, k % 2).astype(bf16)
    winq[3] = quarter(1, 1).astype(bf16)
    pl.semaphore_wait(barrier, len(greet) + 1)

    targets = ((other, prev_j), (other, j), (i, prev_j))
    backs = ((other, next_j), (other, j), (i, next_j))
    r_quads = next(numbers)
    quads = [
        remote(sendq.at[k], winq.at[k], *targets[k], s_quads, r_quads if k < 2 else None)
        for k in range(3)
    ]
    for c in quads:
        c.start()

    part_m = w_merge.shape[1] // 12
    pieces_m = (
        (bit * 2 * part_m, 2 * part_m), (4 * part_m, 4 * part_m), (8 * part_m, 3 * part_m),
        (11 * part_m, part_m), ((1 - bit) * 2 * part_m, 2 * part_m),
    )

    def features(start, size):
        return pl.ds(pl.multiple_of(start, 128), size)

    def merge_out(start, size):
        at = features(start, size)
        return remote(
            w_merge.at[:, at], wm.at[rows_at(j * share, share), at], i, far, s_merge
        )

    r_on, r_on_last = next(numbers), next(numbers)
    far_shard = rows_at(far * share, share)

    def merge_pass(start, size, recv):
        at = features(start, size)
        return remote(wm.at[far_shard, at], wm.at[far_shard, at], i, partner, s_merge, recv)

    merge_far = [merge_out(*piece) for piece in pieces_m[:4]]
    merge_on = [merge_pass(*piece, r_on_last if n == 3 else r_on) for n, piece in enumerate(pieces_m)]
    at = features(*pieces_m[0])
    merge_side = remote(wm.at[far_shard, at], wm.at[far_shard, at], i, j, s_merge, part=beside)
    merge_beside = remote(w_merge, wm.at[rows_at(j * share, share), :], i, partner, s_merge)

    part_u = half // 12
    r_up = next(numbers)

    def up_piece(start, size):
        here = rows_at(other * half + bit * 6 * part_u + start, size)
        return (
            remote(
                w_up.at[rows_at(bit * 6 * part_u + start, size), :],
                up.at[rows_at(i * half + bit * 6 * part_u + start, size), :], other, j, s_up,
            ),
            remote(up.at[here, :], up.at[here, :], i, j, s_up, r_up, beside),
        )

    up_out, up_on = zip(
        up_piece(0, 2 * part_u), up_piece(2 * part_u, 3 * part_u), up_piece(5 * part_u, part_u)
    )
    part_d = ff // 16
    spans = (
        rows_at(bit * 5 * part_d, 2 * part_d),
        rows_at(bit * 5 * part_d + 2 * part_d, 3 * part_d),
        pl.ds(10 * part_d, 6 * part_d),
    )
    r_down = next(numbers)
    down_out = [remote(w_down.at[at, :], down.at[i, at, :], other, j, s_down) for at in spans]
    down_on = [
        remote(down.at[other, at, :], down.at[other, at, :], i, j, s_down, r_down, beside)
        for at in spans[:2]
    ]
    for c in (merge_far[0], merge_beside, up_out[0], up_out[1]):
        c.start()
    for c in locals_[1:]:
        c.start()

    def unit(value):
        squares = value * value
        top = squares.astype(bf16)
        low = (squares - top.astype(f32)).astype(bf16)
        total = _dot(top, block_ones) + _dot(low, block_ones)
        return (value * lax.rsqrt(total + eps_unit)).astype(bf16)

    def project(first):
        tokens = winq[first:first + 2].reshape(2 * quad, ch)
        return (
            unit(_dot(tokens, w_qkv[:, :ch])),
            unit(_dot(tokens, w_qkv[:, ch:2 * ch])),
            _dot(tokens, w_qkv[:, 2 * ch:]).astype(bf16),
        )

    def turn_up(k):
        up_t[k] = up[rows_at(k * half, half), :].T

    def turn_down(k):
        down_t[rows_at(k * half, half), :] = down[k].T

    locals_[1].wait()
    quads[2].wait_recv()
    late = project(2)
    merge_far[1].start()
    all_of(winq.at[pl.ds(0, 2)], recvs.at[r_quads])
    early = project(0)
    qhat, khat, vals = (jnp.concatenate([a, b], axis=0) for a, b in zip(early, late))
    merge_far[0].wait_recv()
    merge_side.start()
    merge_on[0].start()
    locals_[7].wait()
    per = 128 // width
    lanes = lax.broadcasted_iota(jnp.int32, (4 * quad, 128), 1) // width
    for b in range(ch // 128):
        cut = slice(b * 128, (b + 1) * 128)
        qb, kb, vb = qhat[:, cut], khat[:, cut], vals[:, cut]
        acc = None
        for t in range(per):
            mine = lanes == t
            zero = jnp.zeros_like(qb)
            scores = _dot(jnp.where(mine, qb, zero), kb, 1, 1) * logit[b * per + t]
            weights = jnp.exp(scores)
            weights = (weights / jnp.sum(weights, axis=-1, keepdims=True)).astype(bf16)
            term = _dot(weights, jnp.where(mine, vb, zero))
            acc = term if acc is None else acc + term
        mixw[:, :, cut] = acc.astype(bf16).reshape(4, quad, 128)
    r_back = next(numbers)
    for k in range(3):
        remote(mixw.at[k], mixq.at[k], *backs[k], s_back, r_back).start()
    merge_far[2].start()
    merge_far[3].start()
    up_out[2].start()
    mixq[3] = mixw[3]
    up_out[0].wait_recv()
    up_on[0].start()
    locals_[5].wait()
    locals_[6].wait()
    turn_up(i)
    turn_down(i)
    up_out[1].wait_recv()
    up_on[1].start()
    down_out[0].start()
    down_out[1].start()
    merge_far[1].wait_recv()
    merge_on[1].start()
    merge_side.wait_recv()
    merge_on[4].start()
    locals_[2].wait()
    all_of(mixq.at[pl.ds(0, 3)], recvs.at[r_back])
    normed, _ = _ln(_dot(mixq[...].reshape(4 * quad, ch), w_proj[...]))
    flat = jnp.concatenate([quarter(k // 2, k % 2) for k in range(4)], axis=0)
    stream = (flat + normed).astype(bf16)
    picked = _dot(perm[...], stream).astype(bf16)
    merged = jnp.concatenate([picked[k * quad:(k + 1) * quad] for k in range(4)], axis=1)
    up_out[2].wait_recv()
    up_on[2].start()

    pair = j // 2
    pairs = (pair, (pair + 1) % 2)

    def project_pair(p, start, stop):
        at = pl.ds(pl.multiple_of(p * 2 * share, 128), 2 * share)
        return _dot(merged[:, start:stop], wm[at, start:stop], 1, 1)

    features_in = w_merge.shape[1]
    locals_[4].wait()
    merge_beside.wait_recv()
    proj[pairs[0]] = project_pair(pairs[0], 0, features_in)
    down_out[2].start()
    merge_far[2].wait_recv()
    merge_on[2].start()
    merge_far[3].wait_recv()
    merge_on[3].start()
    all_of(wm.at[rows_at(far_partner * share, share), pl.ds(0, 11 * part_m)], recvs.at[r_on])
    proj[pairs[1]] = project_pair(pairs[1], 0, features_in - part_m)
    down_out[0].wait_recv()
    down_on[0].start()
    merge_last = wm.at[rows_at(far_partner * share, share), pl.ds(11 * part_m, part_m)]
    all_of(merge_last, recvs.at[r_on_last])
    proj[pairs[1]] += project_pair(pairs[1], features_in - part_m, features_in)
    level, _ = _ln(jnp.concatenate([proj[p] for p in range(2)], axis=1))

    def put(ref, value):
        for k in range(ni):
            ref[0, j, k] = value[:, k * half:(k + 1) * half].astype(bf16)

    def take(ref, b, p):
        return jnp.concatenate(
            [ref[b, pl.ds(p * 2, 2), k].reshape(2 * own, half) for k in range(ni)], axis=1
        )

    put(lvl, level)
    r_gather = [next(numbers) for _ in range(5)]
    r_sum = [next(numbers) for _ in range(4)]

    class Gathered:
        def __init__(self, ref, group, parts):
            def send(b, slot, to, row, col, recv=None, rows=(0, own)):
                at = pl.ds(*rows)
                return remote(
                    ref.at[b, slot, :, at, :], ref.at[to, slot, :, at, :], row, col, group, recv
                )

            cuts = [(n * own // parts, own // parts) for n in range(parts)]
            self.out_partner = send(0, j, 0, i, partner, r_gather[0])
            self.out_far = [send(0, j, 0, i, far, r_gather[1 + n], c) for n, c in enumerate(cuts)]
            self.onward = [
                send(0, far, 0, i, partner, r_gather[3 + n], c) for n, c in enumerate(cuts)
            ]
            self.across = send(0, j, 1, other, j)
            self.r_far = next(numbers)
            self.across_far = [send(0, far, 1, other, j, self.r_far, c) for c in cuts]
            self.across_on = [send(1, s, 1, i, partner) for s in (j, far)]

    levels = Gathered(lvl, s_lvl, 1)
    levels.out_far[0].start()
    levels.out_partner.start()

    def forward(b, p):
        pre = _dot(take(lvl, b, p), up[...])
        cdf = 0.5 * (1.0 + lax.erf(pre * np.float32(np.sqrt(0.5))))
        hid[b, p] = (pre * cdf).astype(bf16)
        dgel[b, p] = cdf + pre * (jnp.exp(-0.5 * pre * pre) * np.float32(1 / np.sqrt(2 * np.pi)))

    def branch(p, k):
        bsend[pl.ds(p * 2, 2), k] = _dot(hid[0, p], down[k]).astype(bf16).reshape(2, own, half)

    def turn_tokens(b):
        lvl_t[b] = lvl[b, :, i].reshape(nj * own, half).T
        hid_t[b] = hid[b].reshape(nj * own, ff).T

    class Reduced:
        def __init__(self, sent, got, parts, group):
            self.sent, self.got, self.parts = sent, got, parts

            def send(src, slot, dst, to, col, group, recv, part):
                return remote(
                    src.at[(slot, *part)], dst.at[(to, *part)], i, col, group, r_sum[recv]
                )

            self.first = [
                send(sent, far_partner, got, 1, partner, group, n, p) for n, p in enumerate(parts)
            ]
            self.near = [send(sent, partner, got, 0, partner, s_sum, 2, p) for p in parts]
            self.last = [send(got, 3, got, 2, far, s_sum, 3, p) for p in parts]

        def pass_on(self, n):
            self.first[n].wait_recv()
            part = self.parts[n]
            both = self.sent[(far, *part)].astype(f32) + self.got[(1, *part)].astype(f32)
            self.got[(3, *part)] = both.astype(bf16)
            self.last[n].start()

    def total_of(sent, got):
        all_of(got.at[0], recvs.at[r_sum[2]])
        all_of(got.at[2], recvs.at[r_sum[3]])
        total = sent[j].astype(f32) + got[0].astype(f32) + got[2].astype(f32)
        return jnp.concatenate([total[k] for k in range(ni)], axis=1)

    branches = Reduced(bsend, brecv, ((i,), (other,)), s_lvl)
    down_out[1].wait_recv()
    down_on[1].start()
    all_of(up.at[rows_at(other * half + (1 - bit) * 6 * part_u, 6 * part_u), :], recvs.at[r_up])
    levels.out_partner.wait_recv()
    forward(0, pairs[0])
    branch(pairs[0], i)
    levels.out_far[0].wait_recv()
    levels.onward[0].start()
    turn_up(other)
    levels.onward[0].wait_recv()
    forward(0, pairs[1])
    branch(pairs[1], i)
    branches.first[0].start()
    branches.near[0].start()
    down_out[2].wait_recv()
    levels.across.start()
    levels.across_far[0].start()
    all_of(down.at[other, rows_at((1 - bit) * 5 * part_d, 5 * part_d), :], recvs.at[r_down])
    branch(pairs[1], other)
    branches.first[1].start()
    branches.pass_on(0)
    branch(pairs[0], other)
    branches.near[1].start()
    branches.pass_on(1)
    turn_tokens(0)
    turn_down(other)
    locals_[3].wait()
    total = total_of(bsend, brecv)
    norm, inverse = _ln(total)
    coarse[...] = level + norm
    g = cot[...].astype(f32)
    put(
        slo,
        inverse * (
            g - jnp.mean(g, axis=-1, keepdims=True)
            - norm * jnp.mean(g * norm, axis=-1, keepdims=True)
        ),
    )
    slopes = Gathered(slo, s_slo, 2)
    for c in slopes.out_far:
        c.start()
    slopes.out_partner.start()
    slopes.across.start()
    levels.across.wait_recv()
    levels.across_on[0].start()
    levels.across_far[0].wait_recv()
    levels.across_on[1].start()

    rows_h = own // 2

    def backward(b, p):
        spre[b, p] = (dgel[b, p] * _dot(take(slo, b, p), down_t[...])).astype(bf16)

    def slope_in(value):
        turned = jnp.concatenate([up_t[k] for k in range(ni)], axis=1)
        return _dot(value, turned).astype(bf16)

    def backward_rows(p, n):
        at = slice(n * rows_h, (n + 1) * rows_h)
        back = _dot(
            jnp.concatenate(
                [slo[0, pl.ds(p * 2, 2), k, at].reshape(2 * rows_h, half) for k in range(ni)], axis=1
            ),
            down_t[...],
        )
        spans = [slice(q * own + n * rows_h, q * own + (n + 1) * rows_h) for q in range(2)]
        slope = (jnp.concatenate([dgel[0, p, s] for s in spans], axis=0) * back).astype(bf16)
        for q in range(2):
            spre[0, p, spans[q]] = slope[q * rows_h:(q + 1) * rows_h]
        out = slope_in(slope)
        for q in range(2):
            for k in range(ni):
                gsend[p * 2 + q, k, at] = out[q * rows_h:(q + 1) * rows_h, k * half:(k + 1) * half]

    whole = slice(None)
    grads = Reduced(
        gsend, grecv, [(whole, pl.ds(n * rows_h, rows_h)) for n in range(2)], s_slo
    )
    slopes.out_partner.wait_recv()
    backward(0, pairs[0])
    out = slope_in(spre[0, pairs[0]])
    for k in range(ni):
        gsend[pl.ds(pairs[0] * 2, 2), k] = out[:, k * half:(k + 1) * half].reshape(2, own, half)
    for c in grads.near:
        c.start()
    levels.across_on[0].wait_recv()
    levels.across_on[1].wait_recv()
    forward(1, pairs[0])
    slopes.out_far[0].wait_recv()
    slopes.onward[0].start()
    slopes.across_far[0].start()
    forward(1, pairs[1])
    slopes.out_far[1].wait_recv()
    slopes.onward[1].start()
    slopes.across_far[1].start()
    slopes.onward[0].wait_recv()
    backward_rows(pairs[1], 0)
    grads.first[0].start()
    slopes.across.wait_recv()
    slopes.across_on[0].start()
    slopes.onward[1].wait_recv()
    backward_rows(pairs[1], 1)
    grads.first[1].start()
    grads.pass_on(0)
    grads.pass_on(1)
    slopes.across_on[0].wait_recv()
    backward(1, pairs[0])
    turn_tokens(1)
    all_of(slo.at[1, far], recvs.at[slopes.r_far])
    slopes.across_on[1].start()

    def weight_terms(b):
        sp = spre[b].reshape(nj * own, ff)
        return _dot(lvl_t[b], sp), _dot(hid_t[b], slo[b, :, i].reshape(nj * own, half))

    gup[...], gdown[...] = weight_terms(0)
    slopes.across_on[1].wait_recv()
    backward(1, pairs[1])
    terms = weight_terms(1)
    gup[...] += terms[0]
    gdown[...] += terms[1]
    total = total_of(gsend, grecv)
    gcoarse[...] = g + total
    for ref, n in (
        (sendq, s_quads), (mixw.at[pl.ds(0, 3)], s_back), (wm.at[pl.ds(0, 3 * share), :], s_merge),
        (up.at[pl.ds(0, half), :], s_up), (down.at[0], s_down), (lvl, s_lvl), (slo, s_slo), (bsend, s_sum),
    ):
        all_of(ref, sends.at[n])
def store_kernel(coarse_in, gcoarse_in, gup_in, gdown_in, coarse, gcoarse, gup, gdown, sem):
    pairs = ((gup_in, gup, 4), (gdown_in, gdown, 4), (coarse_in, coarse, 1), (gcoarse_in, gcoarse, 1))
    for n, (src, dst, parts) in enumerate(pairs):
        rows = src.shape[0] // parts
        for part in range(parts):
            at = pl.ds(part * rows, rows)
            pltpu.make_async_copy(src.at[at, :], dst.at[at, :], sem.at[n]).start()
    for n, (src, dst, _) in enumerate(pairs):
        pltpu.make_async_copy(src, dst, sem.at[n]).wait()


def fused(fields, logit_scale, w_qkv, w_proj, w_merge, w_up, w_down, cotangent):
    tile_rows, tile_cols, ch = fields.shape
    ni, nj = lax.axis_size("rows"), lax.axis_size("cols")
    own = cotangent.shape[0] * cotangent.shape[1]
    c4 = cotangent.shape[-1]
    half, ff = w_up.shape
    f32, bf16 = jnp.float32, jnp.bfloat16
    quad = (WIN // 2) ** 2
    hb = pl.BlockSpec(memory_space=pltpu.HBM)
    anywhere = pl.BlockSpec(memory_space=pl.ANY)
    dma = pltpu.SemaphoreType.DMA
    outs = (
        jax.ShapeDtypeStruct((own, c4), f32),
        jax.ShapeDtypeStruct((own, c4), f32),
        jax.ShapeDtypeStruct((half, ff), f32),
        jax.ShapeDtypeStruct((ff, half), f32),
    )
    gathered = pltpu.VMEM((ni, nj, ni, own, half), bf16)
    operands = [fields, logit_scale, w_qkv, w_proj, w_merge.T, w_up, w_down, cotangent.reshape(own, c4)]
    operands = [pltpu.with_memory_space_constraint(v, pltpu.HBM) for v in operands]
    values = pl.pallas_call(
        fused_kernel,
        out_shape=outs,
        in_specs=[hb] * 8,
        out_specs=(pl.BlockSpec(memory_space=pltpu.VMEM),) * 4,
        scratch_shapes=[
            pltpu.VMEM(fields.shape, f32),
            pltpu.SMEM(logit_scale.shape, f32),
            pltpu.VMEM(w_qkv.shape, bf16),
            pltpu.VMEM(w_proj.shape, bf16),
            pltpu.VMEM((own, c4), bf16),
            pltpu.VMEM((3, quad, ch), bf16),
            pltpu.VMEM((4, quad, ch), bf16),
            pltpu.VMEM((4, quad, ch), bf16),
            pltpu.VMEM((4, quad, ch), bf16),
            pltpu.VMEM((4 * quad, 4 * quad), bf16),
            pltpu.VMEM((c4, w_merge.shape[0]), bf16),
            pltpu.VMEM((2, own, c4 // 2), f32),
            pltpu.VMEM((c4, ff), bf16),
            pltpu.VMEM((ni, ff, half), bf16),
            pltpu.VMEM((ni, ff, half), bf16),
            pltpu.VMEM((c4, ff), bf16),
            gathered,
            pltpu.VMEM((ni, 2, 2 * own, ff), bf16),
            pltpu.VMEM((ni, half, nj * own), bf16),
            pltpu.VMEM((ni, ff, nj * own), bf16),
            pltpu.VMEM((ni, 2, 2 * own, ff), f32),
            pltpu.VMEM((nj, ni, own, half), bf16),
            pltpu.VMEM((4, ni, own, half), bf16),
            gathered,
            pltpu.VMEM((ni, 2, 2 * own, ff), bf16),
            pltpu.VMEM((nj, ni, own, half), bf16),
            pltpu.VMEM((4, ni, own, half), bf16),
            dma((8,)),
            dma((N_SENDS,)),
            dma((N_RECVS,)),
        ],
        compiler_params=pltpu.CompilerParams(
            collective_id=0, has_side_effects=True, vmem_limit_bytes=44 << 20
        ),
    )(*operands)
    values = pl.pallas_call(
        store_kernel,
        out_shape=outs,
        in_specs=[anywhere] * 4,
        out_specs=(hb,) * 4,
        scratch_shapes=[dma((4,))],
        compiler_params=pltpu.CompilerParams(vmem_limit_bytes=4 << 20),
    )(*values)
    shape = (tile_rows // 2, tile_cols // 2, c4)
    return values[0].reshape(shape), values[1].reshape(shape), values[2], values[3]


def device_body(*args):
    fields, _, w_qkv, _, w_merge, w_up, w_down, _ = args
    fits = (
        lax.axis_size("rows") == 2
        and lax.axis_size("cols") == 4
        and lax.axis_size("dp") % 2 == 0
        and fields.shape[:2] == (WIN, WIN)
        and w_up.shape[0] % 128 == 0
        and w_up.shape[1] % 128 == 0
        and w_merge.shape[1] % 64 == 0
        and w_merge.shape[0] % 1536 == 0
        and w_up.shape[0] % 384 == 0
        and w_up.shape[1] % 256 == 0
        and fields.shape[-1] % 128 == 0
    )
    return fused(*args) if fits else local(*args)


def solution(mesh):
    return jax.shard_map(
        device_body,
        mesh=mesh,
        in_specs=(
            P(("dp", "rows"), "cols", None),
            P(),
            P(),
            P(),
            P(None, "cols"),
            P("rows", "cols"),
            P("cols", "rows"),
            P(("dp", "rows"), "cols", None),
        ),
        out_specs=(
            P(("dp", "rows"), "cols", None),
            P(("dp", "rows"), "cols", None),
            P("rows", ("dp", "cols")),
            P("cols", ("dp", "rows")),
        ),
        check_vma=False,
    )
```

```python
import jax
import jax.numpy as jnp
import numpy as np
from jax import lax
from jax.experimental import pallas as pl
from jax.experimental.pallas import tpu as pltpu
from jax.sharding import PartitionSpec as P

WIN = 16


eps_norm = 1e-05
eps_unit = 1e-06
N_RECVS = 37


def padded_2(cells, sides, width):
    for axis, dim in sides:
        count = lax.axis_size(axis)
        head = lax.slice_in_dim(cells, 0, width, axis=dim)
        tail = lax.slice_in_dim(cells, cells.shape[dim] - width, cells.shape[dim], axis=dim)
        cells = jnp.concatenate(
            [
                lax.ppermute(tail, axis, [(i, (i + 1) % count) for i in range(count)]),
                cells,
                lax.ppermute(head, axis, [((i + 1) % count, i) for i in range(count)]),
            ],
            axis=dim,
        )
    return cells


def layer_norm(value):
    average = jnp.mean(value, axis=-1, keepdims=True)
    centred = value - average
    spread = jnp.mean(centred * centred, axis=-1, keepdims=True)
    inverse = lax.rsqrt(spread + eps_norm)
    return (centred * inverse, inverse)


def norm_slope(upstream, normed, inverse):
    first_mean = jnp.mean(upstream, axis=-1, keepdims=True)
    second_mean = jnp.mean(upstream * normed, axis=-1, keepdims=True)
    return inverse * (upstream - first_mean - normed * second_mean)


def unit_heads(value, head_count):
    shaped = value.reshape(value.shape[:-1] + (head_count, value.shape[-1] // head_count))
    squares = jnp.sum(shaped * shaped, axis=-1, keepdims=True)
    return (shaped * lax.rsqrt(squares + eps_unit)).reshape(value.shape)


def windows_of(field_grid, window):
    grid_rows, grid_cols, channels = field_grid.shape
    shaped = field_grid.reshape(grid_rows // window, window, grid_cols // window, window, channels)
    return shaped.transpose(0, 2, 1, 3, 4).reshape(-1, window * window, channels)


def grid_of(blocks, grid_rows, grid_cols, window):
    channels = blocks.shape[-1]
    shaped = blocks.reshape(grid_rows // window, grid_cols // window, window, window, channels)
    return shaped.transpose(0, 2, 1, 3, 4).reshape(grid_rows, grid_cols, channels)


def attend(queries, key_rows, value_rows, logit_scale, head_count):
    number, window_size, channels = queries.shape
    width_head = channels // head_count
    query_heads = queries.reshape(number, window_size, head_count, width_head)
    key_heads = key_rows.reshape(number, window_size, head_count, width_head)
    value_heads = value_rows.reshape(number, window_size, head_count, width_head)
    scores = jnp.einsum(
        "wqhd,wkhd->whqk", query_heads, key_heads, preferred_element_type=jnp.float32
    )
    weights = jnp.exp(scores * logit_scale[None, :, None, None])
    weights = (weights / jnp.sum(weights, axis=-1, keepdims=True)).astype(jnp.bfloat16)
    mixed_out = jnp.einsum(
        "whqk,wkhd->wqhd", weights, value_heads, preferred_element_type=jnp.float32
    )
    return mixed_out.reshape(number, window_size, channels)


def merge_patches(field_grid):
    quarters = (
        field_grid[0::2, 0::2],
        field_grid[1::2, 0::2],
        field_grid[0::2, 1::2],
        field_grid[1::2, 1::2],
    )
    return jnp.concatenate(quarters, axis=-1)


def exact_gelu(value):
    return jax.nn.gelu(value, approximate=False)


def local(fields, logit_scale, w_qkv, w_proj, w_merge, w_up, w_down, cotangent):
    tile_rows, tile_cols, channels = fields.shape
    offset = WIN // 2
    head_count = logit_scale.shape[0]
    tokens = fields.astype(jnp.bfloat16)
    token_rows = tokens.reshape(-1, channels)
    wide_rows = tile_rows + WIN
    wide_cols = tile_cols + WIN
    widened = padded_2(tokens, (("rows", 0), ("cols", 1)), offset)
    wide_proj = jnp.dot(
        widened.reshape(-1, channels), w_qkv[:, channels:], preferred_element_type=jnp.float32
    )
    key_grid = unit_heads(wide_proj[:, :channels], head_count).astype(jnp.bfloat16)
    value_grid = wide_proj[:, channels:].astype(jnp.bfloat16)
    query_raw = jnp.dot(token_rows, w_qkv[:, :channels], preferred_element_type=jnp.float32)
    queries = (
        unit_heads(query_raw, head_count)
        .astype(jnp.bfloat16)
        .reshape(tile_rows, tile_cols, channels)
    )
    padded = jnp.pad(queries, ((offset, offset), (offset, offset), (0, 0)))
    key_blocks = windows_of(key_grid.reshape(wide_rows, wide_cols, channels), WIN)
    value_blocks = windows_of(value_grid.reshape(wide_rows, wide_cols, channels), WIN)
    mixed = attend(windows_of(padded, WIN), key_blocks, value_blocks, logit_scale, head_count)
    mixed = grid_of(mixed, wide_rows, wide_cols, WIN)[
        offset : offset + tile_rows, offset : offset + tile_cols
    ]
    mixed = mixed.astype(jnp.bfloat16).reshape(-1, channels)
    normed, _ = layer_norm(jnp.dot(mixed, w_proj, preferred_element_type=jnp.float32))
    stream = fields + normed.reshape(fields.shape)
    merged = merge_patches(stream).astype(jnp.bfloat16)
    merged_rows = merged.reshape(-1, merged.shape[-1])
    own_count = merged_rows.shape[0]
    partial_band = jnp.dot(
        lax.all_gather(merged_rows, "cols", axis=0, tiled=True),
        w_merge,
        preferred_element_type=jnp.float32,
    )
    projected_band = lax.all_gather(
        partial_band.astype(jnp.bfloat16), "cols", axis=1, tiled=True
    ).astype(partial_band.dtype)
    level_band, _ = layer_norm(projected_band)
    level_b = level_band.astype(jnp.bfloat16)
    level_own = lax.dynamic_slice_in_dim(
        level_band, lax.axis_index("cols") * own_count, own_count, 0
    )
    up_full = lax.all_gather(w_up, "rows", axis=0, tiled=True)
    down_full = lax.all_gather(w_down, "rows", axis=1, tiled=True)
    hidden_pre = jnp.dot(level_b, up_full, preferred_element_type=jnp.float32)
    hidden = exact_gelu(hidden_pre).astype(jnp.bfloat16)
    rows_part = hidden
    branch_out = lax.psum_scatter(
        jnp.dot(rows_part, down_full, preferred_element_type=jnp.float32).astype(jnp.bfloat16),
        "cols",
        scatter_dimension=0,
        tiled=True,
    ).astype(jnp.float32)
    branch_norm, branch_inv = layer_norm(branch_out)
    coarse = level_own + branch_norm
    upstream = cotangent.astype(jnp.float32).reshape(own_count, -1)
    slope_own = norm_slope(upstream, branch_norm, branch_inv).astype(jnp.bfloat16)
    slope_out = lax.all_gather(slope_own, "cols", axis=0, tiled=True)
    slope_hidden = jnp.einsum("tc,fc->tf", slope_out, down_full, preferred_element_type=jnp.float32)
    _, pullback = jax.vjp(exact_gelu, hidden_pre)
    slope_pre = pullback(slope_hidden)[0].astype(jnp.bfloat16)
    rows_part = slope_pre
    slope_input = lax.psum_scatter(
        jnp.einsum("tf,cf->tc", rows_part, up_full, preferred_element_type=jnp.float32).astype(
            jnp.bfloat16
        ),
        "cols",
        scatter_dimension=0,
        tiled=True,
    ).astype(jnp.float32)
    grad_coarse = upstream + slope_input
    term_up = jnp.einsum("tc,tf->cf", level_b, slope_pre, preferred_element_type=jnp.float32)
    term_down = jnp.einsum("tf,tc->fc", hidden, slope_out, preferred_element_type=jnp.float32)
    grad_up, grad_down = (
        lax.psum_scatter(
            term_up.astype(jnp.bfloat16), "rows", scatter_dimension=0, tiled=True
        ).astype(jnp.float32),
        lax.psum_scatter(
            term_down.astype(jnp.bfloat16), "rows", scatter_dimension=1, tiled=True
        ).astype(jnp.float32),
    )
    coarse_shape = (tile_rows // 2, tile_cols // 2, coarse.shape[-1])
    return (coarse.reshape(coarse_shape), grad_coarse.reshape(coarse_shape), grad_up, grad_down)


def _ln(value):
    average = jnp.mean(value, axis=-1, keepdims=True)
    centred = value - average
    spread = jnp.mean(centred * centred, axis=-1, keepdims=True)
    inverse = lax.rsqrt(spread + eps_norm)
    return centred * inverse, inverse


def _dot(a, b, ca=1, cb=0):
    return lax.dot_general(
        a, b, (((ca,), (cb,)), ((), ())), preferred_element_type=jnp.float32
    )


def fused_kernel(
    fields_h, logit_h, w_qkv_h, w_proj_h, w_merge, w_up, w_down, cot_h,
    coarse, gcoarse, gup, gdown,
    fields, logit, w_qkv, w_proj, cot,
    sendq, winq, mixw, mixq, perm, wm, proj, up, down, up_t, down_t,
    lvl, hid, lvl_t, hid_t, dgel, dgel_p, bsend, brecv, slo, spre, spre_p, gown, gsend, grecv,
    tally, loc, sent, recvs,
):
    f32, bf16 = jnp.float32, jnp.bfloat16
    i, j = lax.axis_index("rows"), lax.axis_index("cols")
    ni, nj = lax.axis_size("rows"), lax.axis_size("cols")
    z = lax.axis_index("dp")
    beside = z + 1 - 2 * (z % 2)
    bit = z % 2
    half_side = WIN // 2
    quad = half_side * half_side
    ch = fields.shape[-1]
    c4 = cot.shape[-1]
    own = cot.shape[0]
    half = c4 // ni
    ff = w_up.shape[1]
    share = w_merge.shape[0]
    heads = logit.shape[0]
    width = ch // heads
    other = (i + 1) % ni
    prev_j, next_j = (j + nj - 1) % nj, (j + 1) % nj
    partner = j + 1 - 2 * (j % 2)
    far = (j + 2) % nj
    far_partner = (partner + 2) % nj
    peers = (partner, far, far_partner)
    numbers = iter(range(N_RECVS))

    def remote(src, dst, row, col, recv=None, part=z):
        n = next(numbers) if recv is None else recv
        return pltpu.make_async_remote_copy(
            src_ref=src, dst_ref=dst, send_sem=sent, recv_sem=recvs.at[n],
            device_id={"rows": row, "cols": col, "dp": part},
            device_id_type=pl.DeviceIdType.MESH,
        )

    def all_of(ref, sem):
        pltpu.make_async_copy(ref, ref, sem).wait()

    def elements(count):
        return tally.at[pl.ds(0, count // tally.shape[1]), :]

    first_copy = pltpu.make_async_copy(fields_h, fields, loc.at[0])
    first_copy.start()
    barrier = pltpu.get_barrier_semaphore()
    greet = [(i, p) for p in peers] + [(other, j), (other, prev_j), (other, next_j)]
    for row, col in greet:
        pl.semaphore_signal(
            barrier, inc=1, device_id={"rows": row, "cols": col},
            device_id_type=pl.DeviceIdType.MESH,
        )
    pl.semaphore_signal(
        barrier, inc=1, device_id={"dp": beside}, device_id_type=pl.DeviceIdType.MESH
    )

    def rows_at(start, size):
        return pl.ds(pl.multiple_of(start, 16), size)

    locals_ = [first_copy] + [
        pltpu.make_async_copy(src, dst, loc.at[min(n + 1, 3)])
        for n, (src, dst) in enumerate((
            (w_qkv_h, w_qkv),
            (logit_h, logit),
            (w_proj_h, w_proj),
            (cot_h, cot),
            (w_merge, wm.at[rows_at(j * share, share), :]),
            (w_up, up.at[rows_at(i * half, half), :]),
            (w_down, down.at[i]),
        ))
    ]
    lane = lax.broadcasted_iota(jnp.int32, (ch, ch), 0) // width
    lane_t = lax.broadcasted_iota(jnp.int32, (ch, ch), 1) // width
    block_ones = (lane == lane_t).astype(f32).astype(bf16)
    rows_out = lax.broadcasted_iota(jnp.int32, (4 * quad, 4 * quad), 0)
    cols_in = lax.broadcasted_iota(jnp.int32, (4 * quad, 4 * quad), 1)
    which, place = rows_out // quad, rows_out % quad
    r = 2 * (place // half_side) + which % 2
    c = 2 * (place % half_side) + which // 2
    source = ((r // half_side) * 2 + c // half_side) * quad + (r % half_side) * half_side + c % half_side
    perm[...] = (source == cols_in).astype(f32).astype(bf16)

    def quarter(a, b):
        part = fields[a * half_side:(a + 1) * half_side, b * half_side:(b + 1) * half_side, :]
        return part.reshape(quad, ch)

    locals_[0].wait()
    for k in range(3):
        sendq[k] = quarter(k // 2, k % 2).astype(bf16)
    winq[3] = quarter(1, 1).astype(bf16)
    pl.semaphore_wait(barrier, len(greet) + 1)

    targets = ((other, prev_j), (other, j), (i, prev_j))
    backs = ((other, next_j), (other, j), (i, next_j))
    r_quads = next(numbers)
    quads = [
        remote(sendq.at[k], winq.at[k], *targets[k], r_quads if k < 2 else None)
        for k in range(3)
    ]
    for c in quads:
        c.start()

    part_m = w_merge.shape[1] // 12
    pieces_m = (
        (bit * 2 * part_m, 2 * part_m), (4 * part_m, 4 * part_m), (8 * part_m, 3 * part_m),
        (11 * part_m, part_m), ((1 - bit) * 2 * part_m, 2 * part_m),
    )

    def features(start, size):
        return pl.ds(pl.multiple_of(start, 128), size)

    def merge_out(start, size):
        at = features(start, size)
        return remote(
            w_merge.at[:, at], wm.at[rows_at(j * share, share), at], i, far
        )

    r_on, r_on_last = next(numbers), next(numbers)
    far_shard = rows_at(far * share, share)

    def merge_pass(start, size, recv):
        at = features(start, size)
        return remote(wm.at[far_shard, at], wm.at[far_shard, at], i, partner, recv)

    merge_far = [merge_out(*piece) for piece in pieces_m[:4]]
    merge_on = [merge_pass(*piece, r_on_last if n == 3 else r_on) for n, piece in enumerate(pieces_m)]
    at = features(*pieces_m[0])
    merge_side = remote(wm.at[far_shard, at], wm.at[far_shard, at], i, j, part=beside)
    merge_beside = remote(w_merge, wm.at[rows_at(j * share, share), :], i, partner)

    part_u = half // 12
    r_up = next(numbers)

    def up_piece(start, size):
        here = rows_at(other * half + bit * 6 * part_u + start, size)
        return (
            remote(
                w_up.at[rows_at(bit * 6 * part_u + start, size), :],
                up.at[rows_at(i * half + bit * 6 * part_u + start, size), :], other, j,
            ),
            remote(up.at[here, :], up.at[here, :], i, j, r_up, beside),
        )

    up_out, up_on = zip(
        up_piece(0, 2 * part_u), up_piece(2 * part_u, 3 * part_u), up_piece(5 * part_u, part_u)
    )
    part_d = ff // 16
    spans = (
        rows_at(bit * 5 * part_d, 2 * part_d),
        rows_at(bit * 5 * part_d + 2 * part_d, 3 * part_d),
        pl.ds(10 * part_d, 6 * part_d),
    )
    r_down = next(numbers)
    down_out = [remote(w_down.at[at, :], down.at[i, at, :], other, j) for at in spans]
    down_on = [
        remote(down.at[other, at, :], down.at[other, at, :], i, j, r_down, beside)
        for at in spans[:2]
    ]
    for c in (merge_far[0], merge_beside, up_out[0], up_out[1]):
        c.start()
    for c in locals_[1:]:
        c.start()

    def unit(value):
        squares = value * value
        top = squares.astype(bf16)
        low = (squares - top.astype(f32)).astype(bf16)
        total = _dot(top, block_ones) + _dot(low, block_ones)
        return (value * lax.rsqrt(total + eps_unit)).astype(bf16)

    def project(first):
        tokens = winq[first:first + 2].reshape(2 * quad, ch)
        return (
            unit(_dot(tokens, w_qkv[:, :ch])),
            unit(_dot(tokens, w_qkv[:, ch:2 * ch])),
            _dot(tokens, w_qkv[:, 2 * ch:]).astype(bf16),
        )

    def turn_up(k):
        up_t[0, k] = up[rows_at(k * half, half), :].T

    def turn_down(k):
        down_t[0, rows_at(k * half, half), :] = down[k].T

    r_turn, r_own = next(numbers), next(numbers)

    def share_up(k):
        remote(up_t.at[0, k], up_t.at[1, k], i, partner, r_turn).start()

    def share_down(k):
        at = rows_at(k * half, half)
        remote(down_t.at[0, at, :], down_t.at[1, at, :], i, partner, r_turn).start()

    locals_[1].wait()
    quads[2].wait_recv()
    late = project(2)
    merge_far[1].start()
    all_of(winq.at[pl.ds(0, 2)], recvs.at[r_quads])
    early = project(0)
    qhat, khat, vals = (jnp.concatenate([a, b], axis=0) for a, b in zip(early, late))
    merge_far[0].wait_recv()
    merge_side.start()
    merge_on[0].start()
    locals_[2].wait()
    per = 128 // width
    lanes = lax.broadcasted_iota(jnp.int32, (4 * quad, 128), 1) // width
    for b in range(ch // 128):
        cut = slice(b * 128, (b + 1) * 128)
        qb, kb, vb = qhat[:, cut], khat[:, cut], vals[:, cut]
        acc = None
        for t in range(per):
            mine = lanes == t
            zero = jnp.zeros_like(qb)
            scores = _dot(jnp.where(mine, qb, zero), kb, 1, 1) * logit[b * per + t]
            weights = jnp.exp(scores)
            weights = (weights / jnp.sum(weights, axis=-1, keepdims=True)).astype(bf16)
            term = _dot(weights, jnp.where(mine, vb, zero))
            acc = term if acc is None else acc + term
        mixw[:, :, cut] = acc.astype(bf16).reshape(4, quad, 128)
    r_back = next(numbers)
    for k in range(3):
        remote(mixw.at[k], mixq.at[k], *backs[k], r_back).start()
    merge_far[2].start()
    merge_far[3].start()
    up_out[2].start()
    mixq[3] = mixw[3]
    up_out[0].wait_recv()
    up_on[0].start()
    all_of(elements(ch * ch + own * c4 + share * w_merge.shape[1] + 2 * half * ff), loc.at[3])
    turn_up(i)
    turn_down(i)
    share_up(i)
    share_down(i)
    up_out[1].wait_recv()
    up_on[1].start()
    down_out[0].start()
    down_out[1].start()
    merge_far[1].wait_recv()
    merge_on[1].start()
    merge_side.wait_recv()
    merge_on[4].start()
    all_of(mixq.at[pl.ds(0, 3)], recvs.at[r_back])
    normed, _ = _ln(_dot(mixq[...].reshape(4 * quad, ch), w_proj[...]))
    flat = jnp.concatenate([quarter(k // 2, k % 2) for k in range(4)], axis=0)
    stream = (flat + normed).astype(bf16)
    picked = _dot(perm[...], stream).astype(bf16)
    merged = jnp.concatenate([picked[k * quad:(k + 1) * quad] for k in range(4)], axis=1)
    up_out[2].wait_recv()
    up_on[2].start()

    pair = j // 2
    pairs = (pair, (pair + 1) % 2)

    def project_pair(p, start, stop):
        at = pl.ds(pl.multiple_of(p * 2 * share, 128), 2 * share)
        return _dot(merged[:, start:stop], wm[at, start:stop], 1, 1)

    features_in = w_merge.shape[1]
    merge_beside.wait_recv()
    proj[pairs[0]] = project_pair(pairs[0], 0, features_in)
    down_out[2].start()
    merge_far[2].wait_recv()
    merge_on[2].start()
    merge_far[3].wait_recv()
    merge_on[3].start()
    all_of(wm.at[rows_at(far_partner * share, share), pl.ds(0, 11 * part_m)], recvs.at[r_on])
    proj[pairs[1]] = project_pair(pairs[1], 0, features_in - part_m)
    down_out[0].wait_recv()
    down_on[0].start()
    merge_last = wm.at[rows_at(far_partner * share, share), pl.ds(11 * part_m, part_m)]
    all_of(merge_last, recvs.at[r_on_last])
    proj[pairs[1]] += project_pair(pairs[1], features_in - part_m, features_in)
    level, _ = _ln(jnp.concatenate([proj[p] for p in range(2)], axis=1))

    def put(ref, value):
        for k in range(ni):
            ref[0, j, k] = value[:, k * half:(k + 1) * half].astype(bf16)

    def take(ref, b, p):
        return jnp.concatenate(
            [ref[b, pl.ds(p * 2, 2), k].reshape(2 * own, half) for k in range(ni)], axis=1
        )

    put(lvl, level)
    r_gather = [next(numbers) for _ in range(4)]
    r_sum = [next(numbers) for _ in range(4)]

    class Gathered:
        def __init__(self, ref, parts):
            def send(b, slot, to, row, col, recv=None, rows=(0, own)):
                at = pl.ds(*rows)
                return remote(
                    ref.at[b, slot, :, at, :], ref.at[to, slot, :, at, :], row, col, recv
                )

            cuts = [(n * own // parts, own // parts) for n in range(parts)]
            self.out_partner = send(0, j, 0, i, partner, r_gather[0])
            self.out_far = [send(0, j, 0, i, far, r_gather[2 + n], c) for n, c in enumerate(cuts)]
            self.onward = send(0, far, 0, i, partner, r_gather[1])
            self.across = send(0, j, 1, other, j)
            self.r_far = next(numbers)
            self.across_far = [send(0, far, 1, other, j, self.r_far, c) for c in cuts]
            self.across_on = [send(1, s, 1, i, partner) for s in (j, far)]

    levels = Gathered(lvl, 1)
    levels.out_far[0].start()
    levels.out_partner.start()

    def forward(b, p):
        pre = _dot(take(lvl, b, p), up[...])
        cdf = 0.5 * (1.0 + lax.erf(pre * np.float32(np.sqrt(0.5))))
        hid[b, p] = (pre * cdf).astype(bf16)
        slope = cdf + pre * (jnp.exp(-0.5 * pre * pre) * np.float32(1 / np.sqrt(2 * np.pi)))
        dgel[b, pl.ds(p * 2, 2)] = slope.reshape(2, own, ff)

    def branch(p, k):
        bsend[pl.ds(p * 2, 2), k] = _dot(hid[0, p], down[k]).astype(bf16).reshape(2, own, half)

    def turn_tokens(b):
        for p in range(2):
            lvl_t[b, p] = lvl[b, 2 * p:2 * p + 2, i].reshape(2 * own, half).T
            hid_t[b, p] = hid[b, p].T

    class Reduced:
        def __init__(self, sums, got, parts):
            self.sums, self.got, self.parts = sums, got, parts

            def send(src, slot, dst, to, col, recv, part):
                return remote(
                    src.at[(slot, *part)], dst.at[(to, *part)], i, col, r_sum[recv]
                )

            self.first = [
                send(sums, far_partner, got, 1, partner, n, p) for n, p in enumerate(parts)
            ]
            self.near = [send(sums, partner, got, 0, partner, 2, p) for p in parts]
            self.last = [send(got, 3, got, 2, far, 3, p) for p in parts]

        def pass_on(self, n):
            self.first[n].wait_recv()
            part = self.parts[n]
            both = self.sums[(far, *part)].astype(f32) + self.got[(1, *part)].astype(f32)
            self.got[(3, *part)] = both.astype(bf16)
            self.last[n].start()

    def total_of(sums, got):
        all_of(got.at[0], recvs.at[r_sum[2]])
        all_of(got.at[2], recvs.at[r_sum[3]])
        total = sums[j].astype(f32) + got[0].astype(f32) + got[2].astype(f32)
        return jnp.concatenate([total[k] for k in range(ni)], axis=1)

    branches = Reduced(bsend, brecv, ((i,), (other,)))
    down_out[1].wait_recv()
    down_on[1].start()
    all_of(up.at[rows_at(other * half + (1 - bit) * 6 * part_u, 6 * part_u), :], recvs.at[r_up])
    levels.out_partner.wait_recv()
    forward(0, pairs[0])
    branch(pairs[0], i)
    levels.out_far[0].wait_recv()
    levels.onward.start()
    turn_up(other)
    levels.onward.wait_recv()
    forward(0, pairs[1])
    branch(pairs[1], i)
    branches.first[0].start()
    branches.near[0].start()
    down_out[2].wait_recv()
    levels.across.start()
    levels.across_far[0].start()
    all_of(down.at[other, rows_at((1 - bit) * 5 * part_d, 5 * part_d), :], recvs.at[r_down])
    branch(pairs[1], other)
    branches.first[1].start()
    branches.pass_on(0)
    branch(pairs[0], other)
    branches.near[1].start()
    branches.pass_on(1)
    for n, blk in enumerate((partner, far_partner)):
        remote(dgel.at[0, blk], dgel_p.at[n], i, partner, r_turn).start()
    turn_down(other)
    share_down(other)
    share_up(other)
    turn_tokens(0)
    total = total_of(bsend, brecv)
    norm, inverse = _ln(total)
    coarse[...] = level + norm
    g = cot[...].astype(f32)
    put(
        slo,
        inverse * (
            g - jnp.mean(g, axis=-1, keepdims=True)
            - norm * jnp.mean(g * norm, axis=-1, keepdims=True)
        ),
    )
    slopes = Gathered(slo, 2)
    for c in slopes.out_far:
        c.start()
    slopes.across.start()
    slopes.out_partner.start()

    def backward(b, p):
        slope = dgel[b, pl.ds(p * 2, 2)].reshape(2 * own, ff) * _dot(take(slo, b, p), down_t[0])
        spre[b, pl.ds(p * 2, 2)] = slope.astype(bf16).reshape(2, own, ff)

    def block_slopes(blk, n):
        so = jnp.concatenate([slo[0, blk, k] for k in range(ni)], axis=1)
        mine = (dgel[0, blk] * _dot(so, down_t[0])).astype(bf16)
        theirs = (dgel_p[n] * _dot(so, down_t[1])).astype(bf16)
        spre[0, blk] = mine
        spre_p[n] = theirs
        remote(spre_p.at[n], spre.at[0, blk], i, partner, r_own).start()
        return mine, theirs

    def input_slopes(slopes_of, start, stop):
        terms = [
            _dot(v, jnp.concatenate([up_t[n, k] for k in range(ni)], axis=1)[:, start:stop])
            for n, v in enumerate(slopes_of)
        ]
        return terms[0] + terms[1]

    def weight_terms(b, ps):
        def lanes_of(ref):
            return jnp.concatenate([ref[b, p] for p in ps], axis=1)

        def rows_of(ref, *at):
            parts = [ref[(b, pl.ds(p * 2, 2), *at)] for p in ps]
            return jnp.concatenate([v.reshape(2 * own, v.shape[-1]) for v in parts], axis=0)

        return _dot(lanes_of(lvl_t), rows_of(spre)), _dot(lanes_of(hid_t), rows_of(slo, i))

    all_of(elements(2 * c4 * ff + 4 * own * ff), recvs.at[r_turn])
    own_slopes = block_slopes(j, 0)
    levels.across.wait_recv()
    levels.across_on[0].start()
    levels.across_far[0].wait_recv()
    levels.across_on[1].start()
    gown[...] = input_slopes(own_slopes, 0, c4)
    levels.across_on[0].wait_recv()
    forward(1, pairs[0])
    levels.across_on[1].wait_recv()
    forward(1, pairs[1])
    turn_tokens(1)
    for n in range(2):
        slopes.out_far[n].wait_recv()
        slopes.across_far[n].start()
    slopes.onward.start()
    far_slopes = block_slopes(far, 1)
    slopes.across.wait_recv()
    slopes.across_on[0].start()
    cut = c4 * 2 // 3
    for n, (start, stop) in enumerate(((0, cut), (cut, c4))):
        gsend[:, start:stop] = input_slopes(far_slopes, start, stop).astype(bf16)
        at = pl.ds(start, stop - start)
        remote(gsend.at[:, at], grecv.at[:, at], i, far, r_sum[3]).start()
    slopes.across_on[0].wait_recv()
    backward(1, pairs[0])
    slopes.out_partner.wait_recv()
    slopes.onward.wait_recv()
    all_of(spre_p, recvs.at[r_own])
    gup[...], gdown[...] = weight_terms(0, (0, 1))
    all_of(slo.at[1, far], recvs.at[slopes.r_far])
    slopes.across_on[1].start()
    terms = weight_terms(1, pairs[:1])
    gup[...] += terms[0]
    gdown[...] += terms[1]
    slopes.across_on[1].wait_recv()
    backward(1, pairs[1])
    terms = weight_terms(1, pairs[1:])
    gup[...] += terms[0]
    gdown[...] += terms[1]
    all_of(grecv, recvs.at[r_sum[3]])
    gcoarse[...] = g + gown[...] + grecv[...].astype(f32)
    all_of(tally, sent)
def store_kernel(coarse_in, gcoarse_in, gup_in, gdown_in, coarse, gcoarse, gup, gdown, sem):
    pairs = ((gup_in, gup, 4), (gdown_in, gdown, 4), (coarse_in, coarse, 1), (gcoarse_in, gcoarse, 1))
    for n, (src, dst, parts) in enumerate(pairs):
        rows = src.shape[0] // parts
        for part in range(parts):
            at = pl.ds(part * rows, rows)
            pltpu.make_async_copy(src.at[at, :], dst.at[at, :], sem.at[n]).start()
    for n, (src, dst, _) in enumerate(pairs):
        pltpu.make_async_copy(src, dst, sem.at[n]).wait()


def fused(fields, logit_scale, w_qkv, w_proj, w_merge, w_up, w_down, cotangent):
    tile_rows, tile_cols, ch = fields.shape
    ni, nj = lax.axis_size("rows"), lax.axis_size("cols")
    own = cotangent.shape[0] * cotangent.shape[1]
    c4 = cotangent.shape[-1]
    half, ff = w_up.shape
    f32, bf16 = jnp.float32, jnp.bfloat16
    quad = (WIN // 2) ** 2
    hb = pl.BlockSpec(memory_space=pltpu.HBM)
    anywhere = pl.BlockSpec(memory_space=pl.ANY)
    dma = pltpu.SemaphoreType.DMA
    sent = (
        6 * quad * ch + 3 * w_merge.size + 2 * w_up.size + 18 * own * c4 + 2 * c4 * ff + 6 * own * ff
    )
    outs = (
        jax.ShapeDtypeStruct((own, c4), f32),
        jax.ShapeDtypeStruct((own, c4), f32),
        jax.ShapeDtypeStruct((half, ff), f32),
        jax.ShapeDtypeStruct((ff, half), f32),
    )
    gathered = pltpu.VMEM((ni, nj, ni, own, half), bf16)
    operands = [fields, logit_scale, w_qkv, w_proj, w_merge.T, w_up, w_down, cotangent.reshape(own, c4)]
    operands = [pltpu.with_memory_space_constraint(v, pltpu.HBM) for v in operands]
    values = pl.pallas_call(
        fused_kernel,
        out_shape=outs,
        in_specs=[hb] * 8,
        out_specs=(pl.BlockSpec(memory_space=pltpu.VMEM),) * 4,
        scratch_shapes=[
            pltpu.VMEM(fields.shape, f32),
            pltpu.SMEM(logit_scale.shape, f32),
            pltpu.VMEM(w_qkv.shape, bf16),
            pltpu.VMEM(w_proj.shape, bf16),
            pltpu.VMEM((own, c4), bf16),
            pltpu.VMEM((3, quad, ch), bf16),
            pltpu.VMEM((4, quad, ch), bf16),
            pltpu.VMEM((4, quad, ch), bf16),
            pltpu.VMEM((4, quad, ch), bf16),
            pltpu.VMEM((4 * quad, 4 * quad), bf16),
            pltpu.VMEM((c4, w_merge.shape[0]), bf16),
            pltpu.VMEM((2, own, c4 // 2), f32),
            pltpu.VMEM((c4, ff), bf16),
            pltpu.VMEM((ni, ff, half), bf16),
            pltpu.VMEM((2, ni, ff, half), bf16),
            pltpu.VMEM((2, c4, ff), bf16),
            gathered,
            pltpu.VMEM((ni, 2, 2 * own, ff), bf16),
            pltpu.VMEM((ni, 2, half, 2 * own), bf16),
            pltpu.VMEM((ni, 2, ff, 2 * own), bf16),
            pltpu.VMEM((ni, nj, own, ff), f32),
            pltpu.VMEM((2, own, ff), f32),
            pltpu.VMEM((nj, ni, own, half), bf16),
            pltpu.VMEM((4, ni, own, half), bf16),
            gathered,
            pltpu.VMEM((ni, nj, own, ff), bf16),
            pltpu.VMEM((2, own, ff), bf16),
            pltpu.VMEM((own, c4), f32),
            pltpu.VMEM((own, c4), bf16),
            pltpu.VMEM((own, c4), bf16),
            pltpu.VMEM((sent // 128, 128), bf16),
            dma((4,)),
            dma,
            dma((N_RECVS,)),
        ],
        compiler_params=pltpu.CompilerParams(
            collective_id=0, has_side_effects=True, vmem_limit_bytes=44 << 20
        ),
    )(*operands)
    values = pl.pallas_call(
        store_kernel,
        out_shape=outs,
        in_specs=[anywhere] * 4,
        out_specs=(hb,) * 4,
        scratch_shapes=[dma((4,))],
        compiler_params=pltpu.CompilerParams(vmem_limit_bytes=4 << 20),
    )(*values)
    shape = (tile_rows // 2, tile_cols // 2, c4)
    return values[0].reshape(shape), values[1].reshape(shape), values[2], values[3]


def device_body(*args):
    fields, _, w_qkv, _, w_merge, w_up, w_down, _ = args
    fits = (
        lax.axis_size("rows") == 2
        and lax.axis_size("cols") == 4
        and lax.axis_size("dp") % 2 == 0
        and fields.shape[:2] == (WIN, WIN)
        and w_up.shape[0] % 128 == 0
        and w_up.shape[1] % 128 == 0
        and w_merge.shape[1] % 64 == 0
        and w_merge.shape[0] % 1536 == 0
        and w_up.shape[0] % 384 == 0
        and w_up.shape[1] % 256 == 0
        and fields.shape[-1] % 128 == 0
    )
    return fused(*args) if fits else local(*args)


def solution(mesh):
    return jax.shard_map(
        device_body,
        mesh=mesh,
        in_specs=(
            P(("dp", "rows"), "cols", None),
            P(),
            P(),
            P(),
            P(None, "cols"),
            P("rows", "cols"),
            P("cols", "rows"),
            P(("dp", "rows"), "cols", None),
        ),
        out_specs=(
            P(("dp", "rows"), "cols", None),
            P(("dp", "rows"), "cols", None),
            P("rows", ("dp", "cols")),
            P("cols", ("dp", "rows")),
        ),
        check_vma=False,
    )
```

```python
import jax
import jax.numpy as jnp
import numpy as np
from jax import lax
from jax.experimental import pallas as pl
from jax.experimental.pallas import tpu as pltpu
from jax.sharding import PartitionSpec as P

WIN = 16


eps_norm = 1e-05
eps_unit = 1e-06
N_RECVS = 40


def padded_2(cells, sides, width):
    for axis, dim in sides:
        count = lax.axis_size(axis)
        head = lax.slice_in_dim(cells, 0, width, axis=dim)
        tail = lax.slice_in_dim(cells, cells.shape[dim] - width, cells.shape[dim], axis=dim)
        cells = jnp.concatenate(
            [
                lax.ppermute(tail, axis, [(i, (i + 1) % count) for i in range(count)]),
                cells,
                lax.ppermute(head, axis, [((i + 1) % count, i) for i in range(count)]),
            ],
            axis=dim,
        )
    return cells


def layer_norm(value):
    average = jnp.mean(value, axis=-1, keepdims=True)
    centred = value - average
    spread = jnp.mean(centred * centred, axis=-1, keepdims=True)
    inverse = lax.rsqrt(spread + eps_norm)
    return (centred * inverse, inverse)


def norm_slope(upstream, normed, inverse):
    first_mean = jnp.mean(upstream, axis=-1, keepdims=True)
    second_mean = jnp.mean(upstream * normed, axis=-1, keepdims=True)
    return inverse * (upstream - first_mean - normed * second_mean)


def unit_heads(value, head_count):
    shaped = value.reshape(value.shape[:-1] + (head_count, value.shape[-1] // head_count))
    squares = jnp.sum(shaped * shaped, axis=-1, keepdims=True)
    return (shaped * lax.rsqrt(squares + eps_unit)).reshape(value.shape)


def windows_of(field_grid, window):
    grid_rows, grid_cols, channels = field_grid.shape
    shaped = field_grid.reshape(grid_rows // window, window, grid_cols // window, window, channels)
    return shaped.transpose(0, 2, 1, 3, 4).reshape(-1, window * window, channels)


def grid_of(blocks, grid_rows, grid_cols, window):
    channels = blocks.shape[-1]
    shaped = blocks.reshape(grid_rows // window, grid_cols // window, window, window, channels)
    return shaped.transpose(0, 2, 1, 3, 4).reshape(grid_rows, grid_cols, channels)


def attend(queries, key_rows, value_rows, logit_scale, head_count):
    number, window_size, channels = queries.shape
    width_head = channels // head_count
    query_heads = queries.reshape(number, window_size, head_count, width_head)
    key_heads = key_rows.reshape(number, window_size, head_count, width_head)
    value_heads = value_rows.reshape(number, window_size, head_count, width_head)
    scores = jnp.einsum(
        "wqhd,wkhd->whqk", query_heads, key_heads, preferred_element_type=jnp.float32
    )
    weights = jnp.exp(scores * logit_scale[None, :, None, None])
    weights = (weights / jnp.sum(weights, axis=-1, keepdims=True)).astype(jnp.bfloat16)
    mixed_out = jnp.einsum(
        "whqk,wkhd->wqhd", weights, value_heads, preferred_element_type=jnp.float32
    )
    return mixed_out.reshape(number, window_size, channels)


def merge_patches(field_grid):
    quarters = (
        field_grid[0::2, 0::2],
        field_grid[1::2, 0::2],
        field_grid[0::2, 1::2],
        field_grid[1::2, 1::2],
    )
    return jnp.concatenate(quarters, axis=-1)


def exact_gelu(value):
    return jax.nn.gelu(value, approximate=False)


def local(fields, logit_scale, w_qkv, w_proj, w_merge, w_up, w_down, cotangent):
    tile_rows, tile_cols, channels = fields.shape
    offset = WIN // 2
    head_count = logit_scale.shape[0]
    tokens = fields.astype(jnp.bfloat16)
    token_rows = tokens.reshape(-1, channels)
    wide_rows = tile_rows + WIN
    wide_cols = tile_cols + WIN
    widened = padded_2(tokens, (("rows", 0), ("cols", 1)), offset)
    wide_proj = jnp.dot(
        widened.reshape(-1, channels), w_qkv[:, channels:], preferred_element_type=jnp.float32
    )
    key_grid = unit_heads(wide_proj[:, :channels], head_count).astype(jnp.bfloat16)
    value_grid = wide_proj[:, channels:].astype(jnp.bfloat16)
    query_raw = jnp.dot(token_rows, w_qkv[:, :channels], preferred_element_type=jnp.float32)
    queries = (
        unit_heads(query_raw, head_count)
        .astype(jnp.bfloat16)
        .reshape(tile_rows, tile_cols, channels)
    )
    padded = jnp.pad(queries, ((offset, offset), (offset, offset), (0, 0)))
    key_blocks = windows_of(key_grid.reshape(wide_rows, wide_cols, channels), WIN)
    value_blocks = windows_of(value_grid.reshape(wide_rows, wide_cols, channels), WIN)
    mixed = attend(windows_of(padded, WIN), key_blocks, value_blocks, logit_scale, head_count)
    mixed = grid_of(mixed, wide_rows, wide_cols, WIN)[
        offset : offset + tile_rows, offset : offset + tile_cols
    ]
    mixed = mixed.astype(jnp.bfloat16).reshape(-1, channels)
    normed, _ = layer_norm(jnp.dot(mixed, w_proj, preferred_element_type=jnp.float32))
    stream = fields + normed.reshape(fields.shape)
    merged = merge_patches(stream).astype(jnp.bfloat16)
    merged_rows = merged.reshape(-1, merged.shape[-1])
    own_count = merged_rows.shape[0]
    partial_band = jnp.dot(
        lax.all_gather(merged_rows, "cols", axis=0, tiled=True),
        w_merge,
        preferred_element_type=jnp.float32,
    )
    projected_band = lax.all_gather(
        partial_band.astype(jnp.bfloat16), "cols", axis=1, tiled=True
    ).astype(partial_band.dtype)
    level_band, _ = layer_norm(projected_band)
    level_b = level_band.astype(jnp.bfloat16)
    level_own = lax.dynamic_slice_in_dim(
        level_band, lax.axis_index("cols") * own_count, own_count, 0
    )
    up_full = lax.all_gather(w_up, "rows", axis=0, tiled=True)
    down_full = lax.all_gather(w_down, "rows", axis=1, tiled=True)
    hidden_pre = jnp.dot(level_b, up_full, preferred_element_type=jnp.float32)
    hidden = exact_gelu(hidden_pre).astype(jnp.bfloat16)
    rows_part = hidden
    branch_out = lax.psum_scatter(
        jnp.dot(rows_part, down_full, preferred_element_type=jnp.float32).astype(jnp.bfloat16),
        "cols",
        scatter_dimension=0,
        tiled=True,
    ).astype(jnp.float32)
    branch_norm, branch_inv = layer_norm(branch_out)
    coarse = level_own + branch_norm
    upstream = cotangent.astype(jnp.float32).reshape(own_count, -1)
    slope_own = norm_slope(upstream, branch_norm, branch_inv).astype(jnp.bfloat16)
    slope_out = lax.all_gather(slope_own, "cols", axis=0, tiled=True)
    slope_hidden = jnp.einsum("tc,fc->tf", slope_out, down_full, preferred_element_type=jnp.float32)
    _, pullback = jax.vjp(exact_gelu, hidden_pre)
    slope_pre = pullback(slope_hidden)[0].astype(jnp.bfloat16)
    rows_part = slope_pre
    slope_input = lax.psum_scatter(
        jnp.einsum("tf,cf->tc", rows_part, up_full, preferred_element_type=jnp.float32).astype(
            jnp.bfloat16
        ),
        "cols",
        scatter_dimension=0,
        tiled=True,
    ).astype(jnp.float32)
    grad_coarse = upstream + slope_input
    term_up = jnp.einsum("tc,tf->cf", level_b, slope_pre, preferred_element_type=jnp.float32)
    term_down = jnp.einsum("tf,tc->fc", hidden, slope_out, preferred_element_type=jnp.float32)
    grad_up, grad_down = (
        lax.psum_scatter(
            term_up.astype(jnp.bfloat16), "rows", scatter_dimension=0, tiled=True
        ).astype(jnp.float32),
        lax.psum_scatter(
            term_down.astype(jnp.bfloat16), "rows", scatter_dimension=1, tiled=True
        ).astype(jnp.float32),
    )
    coarse_shape = (tile_rows // 2, tile_cols // 2, coarse.shape[-1])
    return (coarse.reshape(coarse_shape), grad_coarse.reshape(coarse_shape), grad_up, grad_down)


def _ln(value):
    average = jnp.mean(value, axis=-1, keepdims=True)
    centred = value - average
    spread = jnp.mean(centred * centred, axis=-1, keepdims=True)
    inverse = lax.rsqrt(spread + eps_norm)
    return centred * inverse, inverse


def _dot(a, b, ca=1, cb=0):
    return lax.dot_general(
        a, b, (((ca,), (cb,)), ((), ())), preferred_element_type=jnp.float32
    )


def fused_kernel(
    fields_h, logit_h, w_qkv_h, w_proj_h, w_merge, w_up, w_down, cot_h,
    coarse, gcoarse, gup, gdown,
    fields, logit, w_qkv, w_proj, cot, cot_far,
    sendq, winq, mixw, mixq, perm, wm, proj, up, down, up_t, down_t,
    lvl, hid, lvl_t, hid_t, dgel, dgel_p, bsend, brecv, slo, spre, spre_p, gown, gsend, grecv,
    tally, loc, sent, recvs,
):
    f32, bf16 = jnp.float32, jnp.bfloat16
    i, j = lax.axis_index("rows"), lax.axis_index("cols")
    ni, nj = lax.axis_size("rows"), lax.axis_size("cols")
    z = lax.axis_index("dp")
    beside = z + 1 - 2 * (z % 2)
    bit = z % 2
    half_side = WIN // 2
    quad = half_side * half_side
    ch = fields.shape[-1]
    c4 = cot.shape[-1]
    own = cot.shape[0]
    half = c4 // ni
    ff = w_up.shape[1]
    share = w_merge.shape[0]
    heads = logit.shape[0]
    width = ch // heads
    other = (i + 1) % ni
    prev_j, next_j = (j + nj - 1) % nj, (j + 1) % nj
    partner = j + 1 - 2 * (j % 2)
    far = (j + 2) % nj
    far_partner = (partner + 2) % nj
    peers = (partner, far, far_partner)
    numbers = iter(range(N_RECVS))

    def remote(src, dst, row, col, recv=None, part=z):
        n = next(numbers) if recv is None else recv
        return pltpu.make_async_remote_copy(
            src_ref=src, dst_ref=dst, send_sem=sent, recv_sem=recvs.at[n],
            device_id={"rows": row, "cols": col, "dp": part},
            device_id_type=pl.DeviceIdType.MESH,
        )

    def all_of(ref, sem):
        pltpu.make_async_copy(ref, ref, sem).wait()

    def elements(count):
        return tally.at[pl.ds(0, count // tally.shape[1]), :]

    first_copy = pltpu.make_async_copy(fields_h, fields, loc.at[0])
    first_copy.start()
    barrier = pltpu.get_barrier_semaphore()
    greet = [(i, p) for p in peers] + [(other, j), (other, prev_j), (other, next_j)]
    for row, col in greet:
        pl.semaphore_signal(
            barrier, inc=1, device_id={"rows": row, "cols": col},
            device_id_type=pl.DeviceIdType.MESH,
        )
    pl.semaphore_signal(
        barrier, inc=1, device_id={"dp": beside}, device_id_type=pl.DeviceIdType.MESH
    )

    def rows_at(start, size):
        return pl.ds(pl.multiple_of(start, 16), size)

    locals_ = [first_copy] + [
        pltpu.make_async_copy(src, dst, loc.at[min(n + 1, 3)])
        for n, (src, dst) in enumerate((
            (w_qkv_h, w_qkv),
            (logit_h, logit),
            (w_proj_h, w_proj),
            (cot_h, cot),
            (w_merge, wm.at[rows_at(j * share, share), :]),
            (w_up, up.at[rows_at(i * half, half), :]),
            (w_down, down.at[i]),
        ))
    ]
    lane = lax.broadcasted_iota(jnp.int32, (ch, ch), 0) // width
    lane_t = lax.broadcasted_iota(jnp.int32, (ch, ch), 1) // width
    block_ones = (lane == lane_t).astype(f32).astype(bf16)
    rows_out = lax.broadcasted_iota(jnp.int32, (4 * quad, 4 * quad), 0)
    cols_in = lax.broadcasted_iota(jnp.int32, (4 * quad, 4 * quad), 1)
    which, place = rows_out // quad, rows_out % quad
    r = 2 * (place // half_side) + which % 2
    c = 2 * (place % half_side) + which // 2
    source = ((r // half_side) * 2 + c // half_side) * quad + (r % half_side) * half_side + c % half_side
    perm[...] = (source == cols_in).astype(f32).astype(bf16)

    def quarter(a, b):
        part = fields[a * half_side:(a + 1) * half_side, b * half_side:(b + 1) * half_side, :]
        return part.reshape(quad, ch)

    locals_[0].wait()
    for k in range(3):
        sendq[k] = quarter(k // 2, k % 2).astype(bf16)
    winq[3] = quarter(1, 1).astype(bf16)
    pl.semaphore_wait(barrier, len(greet) + 1)

    targets = ((other, prev_j), (other, j), (i, prev_j))
    backs = ((other, next_j), (other, j), (i, next_j))
    r_quads = next(numbers)
    quads = [
        remote(sendq.at[k], winq.at[k], *targets[k], r_quads if k < 2 else None)
        for k in range(3)
    ]
    for c in quads:
        c.start()

    part_m = w_merge.shape[1] // 12
    pieces_m = (
        (bit * 2 * part_m, 2 * part_m), (4 * part_m, 4 * part_m), (8 * part_m, 3 * part_m),
        (11 * part_m, part_m), ((1 - bit) * 2 * part_m, 2 * part_m),
    )

    def features(start, size):
        return pl.ds(pl.multiple_of(start, 128), size)

    def merge_out(start, size):
        at = features(start, size)
        return remote(
            w_merge.at[:, at], wm.at[rows_at(j * share, share), at], i, far
        )

    r_on, r_on_last = next(numbers), next(numbers)
    far_shard = rows_at(far * share, share)

    def merge_pass(start, size, recv):
        at = features(start, size)
        return remote(wm.at[far_shard, at], wm.at[far_shard, at], i, partner, recv)

    merge_far = [merge_out(*piece) for piece in pieces_m[:4]]
    merge_on = [merge_pass(*piece, r_on_last if n == 3 else r_on) for n, piece in enumerate(pieces_m)]
    at = features(*pieces_m[0])
    merge_side = remote(wm.at[far_shard, at], wm.at[far_shard, at], i, j, part=beside)
    merge_beside = remote(w_merge, wm.at[rows_at(j * share, share), :], i, partner)

    part_u = half // 12
    r_up = next(numbers)

    def up_piece(start, size):
        here = rows_at(other * half + bit * 6 * part_u + start, size)
        return (
            remote(
                w_up.at[rows_at(bit * 6 * part_u + start, size), :],
                up.at[rows_at(i * half + bit * 6 * part_u + start, size), :], other, j,
            ),
            remote(up.at[here, :], up.at[here, :], i, j, r_up, beside),
        )

    up_out, up_on = zip(
        up_piece(0, 2 * part_u), up_piece(2 * part_u, 3 * part_u), up_piece(5 * part_u, part_u)
    )
    part_d = ff // 16
    spans = (
        rows_at(bit * 5 * part_d, 2 * part_d),
        rows_at(bit * 5 * part_d + 2 * part_d, 3 * part_d),
        pl.ds(10 * part_d, 6 * part_d),
    )
    r_down = next(numbers)
    down_out = [remote(w_down.at[at, :], down.at[i, at, :], other, j) for at in spans]
    down_on = [
        remote(down.at[other, at, :], down.at[other, at, :], i, j, r_down, beside)
        for at in spans[:2]
    ]
    for c in (merge_far[0], merge_beside, up_out[0], up_out[1]):
        c.start()
    for c in locals_[1:]:
        c.start()

    def unit(value):
        squares = value * value
        top = squares.astype(bf16)
        low = (squares - top.astype(f32)).astype(bf16)
        total = _dot(top, block_ones) + _dot(low, block_ones)
        return (value * lax.rsqrt(total + eps_unit)).astype(bf16)

    def project(first):
        tokens = winq[first:first + 2].reshape(2 * quad, ch)
        return (
            unit(_dot(tokens, w_qkv[:, :ch])),
            unit(_dot(tokens, w_qkv[:, ch:2 * ch])),
            _dot(tokens, w_qkv[:, 2 * ch:]).astype(bf16),
        )

    def turn_up(k):
        up_t[0, k] = up[rows_at(k * half, half), :].T

    def turn_down(k):
        down_t[0, rows_at(k * half, half), :] = down[k].T

    r_turn, r_own = next(numbers), next(numbers)

    def share_up(k):
        remote(up_t.at[0, k], up_t.at[1, k], i, partner, r_turn).start()

    def share_down(k):
        at = rows_at(k * half, half)
        remote(down_t.at[0, at, :], down_t.at[1, at, :], i, partner, r_turn).start()

    locals_[1].wait()
    quads[2].wait_recv()
    late = project(2)
    merge_far[1].start()
    all_of(winq.at[pl.ds(0, 2)], recvs.at[r_quads])
    early = project(0)
    qhat, khat, vals = (jnp.concatenate([a, b], axis=0) for a, b in zip(early, late))
    merge_far[0].wait_recv()
    merge_side.start()
    merge_on[0].start()
    locals_[2].wait()
    per = 128 // width
    lanes = lax.broadcasted_iota(jnp.int32, (4 * quad, 128), 1) // width
    for b in range(ch // 128):
        cut = slice(b * 128, (b + 1) * 128)
        qb, kb, vb = qhat[:, cut], khat[:, cut], vals[:, cut]
        acc = None
        for t in range(per):
            mine = lanes == t
            zero = jnp.zeros_like(qb)
            scores = _dot(jnp.where(mine, qb, zero), kb, 1, 1) * logit[b * per + t]
            weights = jnp.exp(scores)
            weights = (weights / jnp.sum(weights, axis=-1, keepdims=True)).astype(bf16)
            term = _dot(weights, jnp.where(mine, vb, zero))
            acc = term if acc is None else acc + term
        mixw[:, :, cut] = acc.astype(bf16).reshape(4, quad, 128)
    r_back = next(numbers)
    for k in range(3):
        remote(mixw.at[k], mixq.at[k], *backs[k], r_back).start()
    merge_far[2].start()
    merge_far[3].start()
    up_out[2].start()
    mixq[3] = mixw[3]
    up_out[0].wait_recv()
    up_on[0].start()
    all_of(elements(ch * ch + own * c4 + share * w_merge.shape[1] + 2 * half * ff), loc.at[3])
    turn_up(i)
    turn_down(i)
    share_up(i)
    share_down(i)
    up_out[1].wait_recv()
    up_on[1].start()
    down_out[0].start()
    down_out[1].start()
    merge_far[1].wait_recv()
    merge_on[1].start()
    merge_side.wait_recv()
    merge_on[4].start()
    all_of(mixq.at[pl.ds(0, 3)], recvs.at[r_back])
    normed, _ = _ln(_dot(mixq[...].reshape(4 * quad, ch), w_proj[...]))
    flat = jnp.concatenate([quarter(k // 2, k % 2) for k in range(4)], axis=0)
    stream = (flat + normed).astype(bf16)
    picked = _dot(perm[...], stream).astype(bf16)
    merged = jnp.concatenate([picked[k * quad:(k + 1) * quad] for k in range(4)], axis=1)
    up_out[2].wait_recv()
    up_on[2].start()

    pair = j // 2
    pairs = (pair, (pair + 1) % 2)

    def project_pair(p, start, stop):
        at = pl.ds(pl.multiple_of(p * 2 * share, 128), 2 * share)
        return _dot(merged[:, start:stop], wm[at, start:stop], 1, 1)

    features_in = w_merge.shape[1]
    merge_beside.wait_recv()
    proj[pairs[0]] = project_pair(pairs[0], 0, features_in)
    down_out[2].start()
    merge_far[2].wait_recv()
    merge_on[2].start()
    merge_far[3].wait_recv()
    merge_on[3].start()
    down_out[0].wait_recv()
    down_on[0].start()
    all_of(wm.at[rows_at(far_partner * share, share), pl.ds(0, 11 * part_m)], recvs.at[r_on])
    proj[pairs[1]] = project_pair(pairs[1], 0, features_in - part_m)
    merge_last = wm.at[rows_at(far_partner * share, share), pl.ds(11 * part_m, part_m)]
    all_of(merge_last, recvs.at[r_on_last])
    proj[pairs[1]] += project_pair(pairs[1], features_in - part_m, features_in)
    level, _ = _ln(jnp.concatenate([proj[p] for p in range(2)], axis=1))

    def put(ref, blk, value):
        for k in range(ni):
            ref[0, blk, k] = value[:, k * half:(k + 1) * half].astype(bf16)

    def take(ref, b, p):
        return jnp.concatenate(
            [ref[b, pl.ds(p * 2, 2), k].reshape(2 * own, half) for k in range(ni)], axis=1
        )

    put(lvl, j, level)
    r_gather = [next(numbers) for _ in range(3)]
    r_far_sum, r_own_sum, r_grad = next(numbers), next(numbers), next(numbers)

    class Gathered:
        def __init__(self, ref):
            def send(b, slot, to, row, col, recv=None):
                return remote(ref.at[b, slot], ref.at[to, slot], row, col, recv)

            self.out_partner = send(0, j, 0, i, partner, r_gather[0])
            self.out_far = send(0, j, 0, i, far, r_gather[2])
            self.onward = send(0, far, 0, i, partner, r_gather[1])
            self.across = send(0, j, 1, other, j)
            self.across_far = send(0, far, 1, other, j)
            self.across_on = [send(1, s, 1, i, partner) for s in (j, far)]

    levels = Gathered(lvl)
    levels.out_far.start()
    levels.out_partner.start()
    cot_out = remote(cot, cot_far, i, far)

    def forward(b, p):
        pre = _dot(take(lvl, b, p), up[...])
        cdf = 0.5 * (1.0 + lax.erf(pre * np.float32(np.sqrt(0.5))))
        hid[b, p] = (pre * cdf).astype(bf16)
        slope = cdf + pre * (jnp.exp(-0.5 * pre * pre) * np.float32(1 / np.sqrt(2 * np.pi)))
        dgel[b, pl.ds(p * 2, 2)] = slope.reshape(2, own, ff)

    def branch(p, k):
        bsend[pl.ds(p * 2, 2), k] = _dot(hid[0, p], down[k]).astype(bf16).reshape(2, own, half)

    def turn_tokens(b):
        for p in range(2):
            lvl_t[b, p] = lvl[b, 2 * p:2 * p + 2, i].reshape(2 * own, half).T
            hid_t[b, p] = hid[b, p].T

    order = (i, other)
    near = [remote(bsend.at[partner, k], brecv.at[0, k], i, partner) for k in order]
    first = [
        remote(bsend.at[far_partner, k], brecv.at[1, k], i, partner) for k in order
    ]
    far_sum = [remote(brecv.at[3, k], brecv.at[2, k], i, far, r_far_sum) for k in order]
    own_sum = [remote(brecv.at[5, k], brecv.at[4, k], i, far, r_own_sum) for k in order]

    def pass_far(n):
        first[n].wait_recv()
        k = order[n]
        brecv[3, k] = (bsend[far, k].astype(f32) + brecv[1, k].astype(f32)).astype(bf16)
        far_sum[n].start()

    def pass_own(n):
        near[n].wait_recv()
        k = order[n]
        brecv[5, k] = (bsend[j, k].astype(f32) + brecv[0, k].astype(f32)).astype(bf16)
        own_sum[n].start()

    def total_of(blk, in_chip, from_far, sem):
        all_of(brecv.at[from_far], recvs.at[sem])
        total = bsend[blk].astype(f32) + brecv[in_chip].astype(f32) + brecv[from_far].astype(f32)
        return jnp.concatenate([total[k] for k in range(ni)], axis=1)

    def slopes_of(total, g):
        norm, inverse = _ln(total)
        return norm, inverse * (
            g - jnp.mean(g, axis=-1, keepdims=True)
            - norm * jnp.mean(g * norm, axis=-1, keepdims=True)
        )

    down_out[1].wait_recv()
    down_on[1].start()
    all_of(up.at[rows_at(other * half + (1 - bit) * 6 * part_u, 6 * part_u), :], recvs.at[r_up])
    levels.out_partner.wait_recv()
    forward(0, pairs[0])
    branch(pairs[0], i)
    near[0].start()
    pass_own(0)
    cot_out.start()
    levels.out_far.wait_recv()
    levels.onward.start()
    turn_up(other)
    levels.onward.wait_recv()
    forward(0, pairs[1])
    branch(pairs[1], i)
    first[0].start()
    down_out[2].wait_recv()
    levels.across.start()
    levels.across_far.start()
    all_of(down.at[other, rows_at((1 - bit) * 5 * part_d, 5 * part_d), :], recvs.at[r_down])
    branch(pairs[1], other)
    first[1].start()
    pass_far(0)
    branch(pairs[0], other)
    near[1].start()
    pass_far(1)
    for n, blk in enumerate((partner, far_partner)):
        remote(dgel.at[0, blk], dgel_p.at[n], i, partner, r_turn).start()
    turn_down(other)
    pass_own(1)
    share_down(other)
    share_up(other)
    turn_tokens(0)
    levels.across.wait_recv()
    levels.across_on[0].start()
    total = total_of(j, 0, 2, r_far_sum)
    g = cot[...].astype(f32)
    norm, slope = slopes_of(total, g)
    put(slo, j, slope)
    slopes = Gathered(slo)
    slopes.across.start()
    slopes.out_partner.start()
    coarse[...] = level + norm
    def backward(b, p):
        slope = dgel[b, pl.ds(p * 2, 2)].reshape(2 * own, ff) * _dot(take(slo, b, p), down_t[0])
        spre[b, pl.ds(p * 2, 2)] = slope.astype(bf16).reshape(2, own, ff)

    def block_slopes(blk, n):
        so = jnp.concatenate([slo[0, blk, k] for k in range(ni)], axis=1)
        mine = (dgel[0, blk] * _dot(so, down_t[0])).astype(bf16)
        theirs = (dgel_p[n] * _dot(so, down_t[1])).astype(bf16)
        spre[0, blk] = mine
        spre_p[n] = theirs
        remote(spre_p.at[n], spre.at[0, blk], i, partner, r_own).start()
        return mine, theirs

    def input_slopes(slopes_here):
        terms = [
            _dot(v, jnp.concatenate([up_t[n, k] for k in range(ni)], axis=1))
            for n, v in enumerate(slopes_here)
        ]
        return terms[0] + terms[1]

    def weight_terms(*band_pairs):
        def lanes_of(ref):
            return jnp.concatenate([ref[b, p] for b, p in band_pairs], axis=1)

        def rows_of(ref, *at):
            parts = [ref[(b, pl.ds(p * 2, 2), *at)] for b, p in band_pairs]
            return jnp.concatenate([v.reshape(2 * own, v.shape[-1]) for v in parts], axis=0)

        return _dot(lanes_of(lvl_t), rows_of(spre)), _dot(lanes_of(hid_t), rows_of(slo, i))

    all_of(elements(2 * c4 * ff + 4 * own * ff), recvs.at[r_turn])
    cot_out.wait_recv()
    total = total_of(far, 1, 4, r_own_sum)
    _, slope = slopes_of(total, cot_far[...].astype(f32))
    put(slo, far, slope)
    slopes.across_far.start()
    slopes.onward.start()

    levels.across_far.wait_recv()
    levels.across_on[1].start()
    far_slopes = block_slopes(far, 1)
    gsend[...] = input_slopes(far_slopes).astype(bf16)
    remote(gsend, grecv, i, far, r_grad).start()
    own_slopes = block_slopes(j, 0)
    gown[...] = input_slopes(own_slopes)
    levels.across_on[0].wait_recv()
    forward(1, pairs[0])
    levels.across_on[1].wait_recv()
    forward(1, pairs[1])
    turn_tokens(1)
    slopes.across.wait_recv()
    slopes.across_on[0].start()
    slopes.out_partner.wait_recv()
    slopes.onward.wait_recv()
    all_of(spre_p, recvs.at[r_own])
    slopes.across_on[0].wait_recv()
    backward(1, pairs[0])
    slopes.across_far.wait_recv()
    slopes.across_on[1].start()
    gup[...], gdown[...] = weight_terms((0, 0), (0, 1), (1, pairs[0]))
    slopes.across_on[1].wait_recv()
    backward(1, pairs[1])
    terms = weight_terms((1, pairs[1]))
    gup[...] += terms[0]
    gdown[...] += terms[1]
    all_of(grecv, recvs.at[r_grad])
    gcoarse[...] = g + gown[...] + grecv[...].astype(f32)
    all_of(tally, sent)
def store_kernel(coarse_in, gcoarse_in, gup_in, gdown_in, coarse, gcoarse, gup, gdown, sem):
    pairs = ((gup_in, gup, 4), (gdown_in, gdown, 4), (coarse_in, coarse, 1), (gcoarse_in, gcoarse, 1))
    for n, (src, dst, parts) in enumerate(pairs):
        rows = src.shape[0] // parts
        for part in range(parts):
            at = pl.ds(part * rows, rows)
            pltpu.make_async_copy(src.at[at, :], dst.at[at, :], sem.at[n]).start()
    for n, (src, dst, _) in enumerate(pairs):
        pltpu.make_async_copy(src, dst, sem.at[n]).wait()


def fused(fields, logit_scale, w_qkv, w_proj, w_merge, w_up, w_down, cotangent):
    tile_rows, tile_cols, ch = fields.shape
    ni, nj = lax.axis_size("rows"), lax.axis_size("cols")
    own = cotangent.shape[0] * cotangent.shape[1]
    c4 = cotangent.shape[-1]
    half, ff = w_up.shape
    f32, bf16 = jnp.float32, jnp.bfloat16
    quad = (WIN // 2) ** 2
    hb = pl.BlockSpec(memory_space=pltpu.HBM)
    anywhere = pl.BlockSpec(memory_space=pl.ANY)
    dma = pltpu.SemaphoreType.DMA
    sent = (
        6 * quad * ch + 3 * w_merge.size + 2 * w_up.size + 19 * own * c4 + 2 * c4 * ff + 6 * own * ff
    )
    outs = (
        jax.ShapeDtypeStruct((own, c4), f32),
        jax.ShapeDtypeStruct((own, c4), f32),
        jax.ShapeDtypeStruct((half, ff), f32),
        jax.ShapeDtypeStruct((ff, half), f32),
    )
    gathered = pltpu.VMEM((ni, nj, ni, own, half), bf16)
    operands = [fields, logit_scale, w_qkv, w_proj, w_merge.T, w_up, w_down, cotangent.reshape(own, c4)]
    operands = [pltpu.with_memory_space_constraint(v, pltpu.HBM) for v in operands]
    values = pl.pallas_call(
        fused_kernel,
        out_shape=outs,
        in_specs=[hb] * 8,
        out_specs=(pl.BlockSpec(memory_space=pltpu.VMEM),) * 4,
        scratch_shapes=[
            pltpu.VMEM(fields.shape, f32),
            pltpu.SMEM(logit_scale.shape, f32),
            pltpu.VMEM(w_qkv.shape, bf16),
            pltpu.VMEM(w_proj.shape, bf16),
            pltpu.VMEM((own, c4), bf16),
            pltpu.VMEM((own, c4), bf16),
            pltpu.VMEM((3, quad, ch), bf16),
            pltpu.VMEM((4, quad, ch), bf16),
            pltpu.VMEM((4, quad, ch), bf16),
            pltpu.VMEM((4, quad, ch), bf16),
            pltpu.VMEM((4 * quad, 4 * quad), bf16),
            pltpu.VMEM((c4, w_merge.shape[0]), bf16),
            pltpu.VMEM((2, own, c4 // 2), f32),
            pltpu.VMEM((c4, ff), bf16),
            pltpu.VMEM((ni, ff, half), bf16),
            pltpu.VMEM((2, ni, ff, half), bf16),
            pltpu.VMEM((2, c4, ff), bf16),
            gathered,
            pltpu.VMEM((ni, 2, 2 * own, ff), bf16),
            pltpu.VMEM((ni, 2, half, 2 * own), bf16),
            pltpu.VMEM((ni, 2, ff, 2 * own), bf16),
            pltpu.VMEM((ni, nj, own, ff), f32),
            pltpu.VMEM((2, own, ff), f32),
            pltpu.VMEM((nj, ni, own, half), bf16),
            pltpu.VMEM((6, ni, own, half), bf16),
            gathered,
            pltpu.VMEM((ni, nj, own, ff), bf16),
            pltpu.VMEM((2, own, ff), bf16),
            pltpu.VMEM((own, c4), f32),
            pltpu.VMEM((own, c4), bf16),
            pltpu.VMEM((own, c4), bf16),
            pltpu.VMEM((sent // 128, 128), bf16),
            dma((4,)),
            dma,
            dma((N_RECVS,)),
        ],
        compiler_params=pltpu.CompilerParams(
            collective_id=0, has_side_effects=True, vmem_limit_bytes=44 << 20
        ),
    )(*operands)
    values = pl.pallas_call(
        store_kernel,
        out_shape=outs,
        in_specs=[anywhere] * 4,
        out_specs=(hb,) * 4,
        scratch_shapes=[dma((4,))],
        compiler_params=pltpu.CompilerParams(vmem_limit_bytes=4 << 20),
    )(*values)
    shape = (tile_rows // 2, tile_cols // 2, c4)
    return values[0].reshape(shape), values[1].reshape(shape), values[2], values[3]


def device_body(*args):
    fields, _, w_qkv, _, w_merge, w_up, w_down, _ = args
    fits = (
        lax.axis_size("rows") == 2
        and lax.axis_size("cols") == 4
        and lax.axis_size("dp") % 2 == 0
        and fields.shape[:2] == (WIN, WIN)
        and w_up.shape[0] % 128 == 0
        and w_up.shape[1] % 128 == 0
        and w_merge.shape[1] % 64 == 0
        and w_merge.shape[0] % 1536 == 0
        and w_up.shape[0] % 384 == 0
        and w_up.shape[1] % 256 == 0
        and fields.shape[-1] % 128 == 0
    )
    return fused(*args) if fits else local(*args)


def solution(mesh):
    return jax.shard_map(
        device_body,
        mesh=mesh,
        in_specs=(
            P(("dp", "rows"), "cols", None),
            P(),
            P(),
            P(),
            P(None, "cols"),
            P("rows", "cols"),
            P("cols", "rows"),
            P(("dp", "rows"), "cols", None),
        ),
        out_specs=(
            P(("dp", "rows"), "cols", None),
            P(("dp", "rows"), "cols", None),
            P("rows", ("dp", "cols")),
            P("cols", ("dp", "rows")),
        ),
        check_vma=False,
    )
```

```python
import jax
import jax.numpy as jnp
import numpy as np
from jax import lax
from jax.experimental import pallas as pl
from jax.experimental.pallas import tpu as pltpu
from jax.sharding import PartitionSpec as P

WIN = 16


eps_norm = 1e-05
eps_unit = 1e-06
N_RECVS = 40
PARTS = 4


def padded_2(cells, sides, width):
    for axis, dim in sides:
        count = lax.axis_size(axis)
        head = lax.slice_in_dim(cells, 0, width, axis=dim)
        tail = lax.slice_in_dim(cells, cells.shape[dim] - width, cells.shape[dim], axis=dim)
        cells = jnp.concatenate(
            [
                lax.ppermute(tail, axis, [(i, (i + 1) % count) for i in range(count)]),
                cells,
                lax.ppermute(head, axis, [((i + 1) % count, i) for i in range(count)]),
            ],
            axis=dim,
        )
    return cells


def layer_norm(value):
    average = jnp.mean(value, axis=-1, keepdims=True)
    centred = value - average
    spread = jnp.mean(centred * centred, axis=-1, keepdims=True)
    inverse = lax.rsqrt(spread + eps_norm)
    return (centred * inverse, inverse)


def norm_slope(upstream, normed, inverse):
    first_mean = jnp.mean(upstream, axis=-1, keepdims=True)
    second_mean = jnp.mean(upstream * normed, axis=-1, keepdims=True)
    return inverse * (upstream - first_mean - normed * second_mean)


def unit_heads(value, head_count):
    shaped = value.reshape(value.shape[:-1] + (head_count, value.shape[-1] // head_count))
    squares = jnp.sum(shaped * shaped, axis=-1, keepdims=True)
    return (shaped * lax.rsqrt(squares + eps_unit)).reshape(value.shape)


def windows_of(field_grid, window):
    grid_rows, grid_cols, channels = field_grid.shape
    shaped = field_grid.reshape(grid_rows // window, window, grid_cols // window, window, channels)
    return shaped.transpose(0, 2, 1, 3, 4).reshape(-1, window * window, channels)


def grid_of(blocks, grid_rows, grid_cols, window):
    channels = blocks.shape[-1]
    shaped = blocks.reshape(grid_rows // window, grid_cols // window, window, window, channels)
    return shaped.transpose(0, 2, 1, 3, 4).reshape(grid_rows, grid_cols, channels)


def attend(queries, key_rows, value_rows, logit_scale, head_count):
    number, window_size, channels = queries.shape
    width_head = channels // head_count
    query_heads = queries.reshape(number, window_size, head_count, width_head)
    key_heads = key_rows.reshape(number, window_size, head_count, width_head)
    value_heads = value_rows.reshape(number, window_size, head_count, width_head)
    scores = jnp.einsum(
        "wqhd,wkhd->whqk", query_heads, key_heads, preferred_element_type=jnp.float32
    )
    weights = jnp.exp(scores * logit_scale[None, :, None, None])
    weights = (weights / jnp.sum(weights, axis=-1, keepdims=True)).astype(jnp.bfloat16)
    mixed_out = jnp.einsum(
        "whqk,wkhd->wqhd", weights, value_heads, preferred_element_type=jnp.float32
    )
    return mixed_out.reshape(number, window_size, channels)


def merge_patches(field_grid):
    quarters = (
        field_grid[0::2, 0::2],
        field_grid[1::2, 0::2],
        field_grid[0::2, 1::2],
        field_grid[1::2, 1::2],
    )
    return jnp.concatenate(quarters, axis=-1)


def exact_gelu(value):
    return jax.nn.gelu(value, approximate=False)


def local(fields, logit_scale, w_qkv, w_proj, w_merge, w_up, w_down, cotangent):
    tile_rows, tile_cols, channels = fields.shape
    offset = WIN // 2
    head_count = logit_scale.shape[0]
    tokens = fields.astype(jnp.bfloat16)
    token_rows = tokens.reshape(-1, channels)
    wide_rows = tile_rows + WIN
    wide_cols = tile_cols + WIN
    widened = padded_2(tokens, (("rows", 0), ("cols", 1)), offset)
    wide_proj = jnp.dot(
        widened.reshape(-1, channels), w_qkv[:, channels:], preferred_element_type=jnp.float32
    )
    key_grid = unit_heads(wide_proj[:, :channels], head_count).astype(jnp.bfloat16)
    value_grid = wide_proj[:, channels:].astype(jnp.bfloat16)
    query_raw = jnp.dot(token_rows, w_qkv[:, :channels], preferred_element_type=jnp.float32)
    queries = (
        unit_heads(query_raw, head_count)
        .astype(jnp.bfloat16)
        .reshape(tile_rows, tile_cols, channels)
    )
    padded = jnp.pad(queries, ((offset, offset), (offset, offset), (0, 0)))
    key_blocks = windows_of(key_grid.reshape(wide_rows, wide_cols, channels), WIN)
    value_blocks = windows_of(value_grid.reshape(wide_rows, wide_cols, channels), WIN)
    mixed = attend(windows_of(padded, WIN), key_blocks, value_blocks, logit_scale, head_count)
    mixed = grid_of(mixed, wide_rows, wide_cols, WIN)[
        offset : offset + tile_rows, offset : offset + tile_cols
    ]
    mixed = mixed.astype(jnp.bfloat16).reshape(-1, channels)
    normed, _ = layer_norm(jnp.dot(mixed, w_proj, preferred_element_type=jnp.float32))
    stream = fields + normed.reshape(fields.shape)
    merged = merge_patches(stream).astype(jnp.bfloat16)
    merged_rows = merged.reshape(-1, merged.shape[-1])
    own_count = merged_rows.shape[0]
    partial_band = jnp.dot(
        lax.all_gather(merged_rows, "cols", axis=0, tiled=True),
        w_merge,
        preferred_element_type=jnp.float32,
    )
    projected_band = lax.all_gather(
        partial_band.astype(jnp.bfloat16), "cols", axis=1, tiled=True
    ).astype(partial_band.dtype)
    level_band, _ = layer_norm(projected_band)
    level_b = level_band.astype(jnp.bfloat16)
    level_own = lax.dynamic_slice_in_dim(
        level_band, lax.axis_index("cols") * own_count, own_count, 0
    )
    up_full = lax.all_gather(w_up, "rows", axis=0, tiled=True)
    down_full = lax.all_gather(w_down, "rows", axis=1, tiled=True)
    hidden_pre = jnp.dot(level_b, up_full, preferred_element_type=jnp.float32)
    hidden = exact_gelu(hidden_pre).astype(jnp.bfloat16)
    rows_part = hidden
    branch_out = lax.psum_scatter(
        jnp.dot(rows_part, down_full, preferred_element_type=jnp.float32).astype(jnp.bfloat16),
        "cols",
        scatter_dimension=0,
        tiled=True,
    ).astype(jnp.float32)
    branch_norm, branch_inv = layer_norm(branch_out)
    coarse = level_own + branch_norm
    upstream = cotangent.astype(jnp.float32).reshape(own_count, -1)
    slope_own = norm_slope(upstream, branch_norm, branch_inv).astype(jnp.bfloat16)
    slope_out = lax.all_gather(slope_own, "cols", axis=0, tiled=True)
    slope_hidden = jnp.einsum("tc,fc->tf", slope_out, down_full, preferred_element_type=jnp.float32)
    _, pullback = jax.vjp(exact_gelu, hidden_pre)
    slope_pre = pullback(slope_hidden)[0].astype(jnp.bfloat16)
    rows_part = slope_pre
    slope_input = lax.psum_scatter(
        jnp.einsum("tf,cf->tc", rows_part, up_full, preferred_element_type=jnp.float32).astype(
            jnp.bfloat16
        ),
        "cols",
        scatter_dimension=0,
        tiled=True,
    ).astype(jnp.float32)
    grad_coarse = upstream + slope_input
    term_up = jnp.einsum("tc,tf->cf", level_b, slope_pre, preferred_element_type=jnp.float32)
    term_down = jnp.einsum("tf,tc->fc", hidden, slope_out, preferred_element_type=jnp.float32)
    grad_up, grad_down = (
        lax.psum_scatter(
            term_up.astype(jnp.bfloat16), "rows", scatter_dimension=0, tiled=True
        ).astype(jnp.float32),
        lax.psum_scatter(
            term_down.astype(jnp.bfloat16), "rows", scatter_dimension=1, tiled=True
        ).astype(jnp.float32),
    )
    coarse_shape = (tile_rows // 2, tile_cols // 2, coarse.shape[-1])
    return (coarse.reshape(coarse_shape), grad_coarse.reshape(coarse_shape), grad_up, grad_down)


def _ln(value):
    average = jnp.mean(value, axis=-1, keepdims=True)
    centred = value - average
    spread = jnp.mean(centred * centred, axis=-1, keepdims=True)
    inverse = lax.rsqrt(spread + eps_norm)
    return centred * inverse, inverse


def _dot(a, b, ca=1, cb=0):
    return lax.dot_general(
        a, b, (((ca,), (cb,)), ((), ())), preferred_element_type=jnp.float32
    )


def fused_kernel(
    fields_h, logit_h, w_qkv_h, w_proj_h, w_merge, w_up, w_down, cot_h,
    coarse, gcoarse, gup, gdown, back_lvl, back_spre, back_hid, back_slo,
    fields, logit, w_qkv, w_proj, cot, cot_far,
    sendq, winq, mixw, mixq, perm, wm, proj, up, down, up_t, down_t,
    lvl, hid, lvl_t, hid_t, dgel, dgel_p, bsend, brecv, slo, spre, spre_p, gown, gsend, grecv,
    tally, loc, sent, recvs,
):
    f32, bf16 = jnp.float32, jnp.bfloat16
    i, j = lax.axis_index("rows"), lax.axis_index("cols")
    ni, nj = lax.axis_size("rows"), lax.axis_size("cols")
    z = lax.axis_index("dp")
    beside = z + 1 - 2 * (z % 2)
    bit = z % 2
    half_side = WIN // 2
    quad = half_side * half_side
    ch = fields.shape[-1]
    c4 = cot.shape[-1]
    own = cot.shape[0]
    half = c4 // ni
    ff = w_up.shape[1]
    share = w_merge.shape[0]
    heads = logit.shape[0]
    width = ch // heads
    other = (i + 1) % ni
    prev_j, next_j = (j + nj - 1) % nj, (j + 1) % nj
    partner = j + 1 - 2 * (j % 2)
    far = (j + 2) % nj
    far_partner = (partner + 2) % nj
    peers = (partner, far, far_partner)
    numbers = iter(range(N_RECVS))

    def remote(src, dst, row, col, recv=None, part=z):
        n = next(numbers) if recv is None else recv
        return pltpu.make_async_remote_copy(
            src_ref=src, dst_ref=dst, send_sem=sent, recv_sem=recvs.at[n],
            device_id={"rows": row, "cols": col, "dp": part},
            device_id_type=pl.DeviceIdType.MESH,
        )

    def all_of(ref, sem):
        pltpu.make_async_copy(ref, ref, sem).wait()

    def elements(count):
        return tally.at[pl.ds(0, count // tally.shape[1]), :]

    first_copy = pltpu.make_async_copy(fields_h, fields, loc.at[0])
    first_copy.start()
    barrier = pltpu.get_barrier_semaphore()
    greet = [(i, p) for p in peers] + [(other, j), (other, prev_j), (other, next_j)]
    for row, col in greet:
        pl.semaphore_signal(
            barrier, inc=1, device_id={"rows": row, "cols": col},
            device_id_type=pl.DeviceIdType.MESH,
        )
    pl.semaphore_signal(
        barrier, inc=1, device_id={"dp": beside}, device_id_type=pl.DeviceIdType.MESH
    )

    def rows_at(start, size):
        return pl.ds(pl.multiple_of(start, 16), size)

    locals_ = [first_copy] + [
        pltpu.make_async_copy(src, dst, loc.at[min(n + 1, 3)])
        for n, (src, dst) in enumerate((
            (w_qkv_h, w_qkv),
            (logit_h, logit),
            (w_proj_h, w_proj),
            (cot_h, cot),
            (w_merge, wm.at[rows_at(j * share, share), :]),
            (w_up, up.at[rows_at(i * half, half), :]),
            (w_down, down.at[i]),
        ))
    ]
    lane = lax.broadcasted_iota(jnp.int32, (ch, ch), 0) // width
    lane_t = lax.broadcasted_iota(jnp.int32, (ch, ch), 1) // width
    block_ones = (lane == lane_t).astype(f32).astype(bf16)
    rows_out = lax.broadcasted_iota(jnp.int32, (4 * quad, 4 * quad), 0)
    cols_in = lax.broadcasted_iota(jnp.int32, (4 * quad, 4 * quad), 1)
    which, place = rows_out // quad, rows_out % quad
    r = 2 * (place // half_side) + which % 2
    c = 2 * (place % half_side) + which // 2
    source = ((r // half_side) * 2 + c // half_side) * quad + (r % half_side) * half_side + c % half_side
    perm[...] = (source == cols_in).astype(f32).astype(bf16)

    def quarter(a, b):
        part = fields[a * half_side:(a + 1) * half_side, b * half_side:(b + 1) * half_side, :]
        return part.reshape(quad, ch)

    locals_[0].wait()
    for k in range(3):
        sendq[k] = quarter(k // 2, k % 2).astype(bf16)
    winq[3] = quarter(1, 1).astype(bf16)
    pl.semaphore_wait(barrier, len(greet) + 1)

    targets = ((other, prev_j), (other, j), (i, prev_j))
    backs = ((other, next_j), (other, j), (i, next_j))
    r_quads = next(numbers)
    quads = [
        remote(sendq.at[k], winq.at[k], *targets[k], r_quads if k < 2 else None)
        for k in range(3)
    ]
    for c in quads:
        c.start()

    part_m = w_merge.shape[1] // 12
    pieces_m = (
        (bit * 2 * part_m, 2 * part_m), (4 * part_m, 4 * part_m), (8 * part_m, 3 * part_m),
        (11 * part_m, part_m), ((1 - bit) * 2 * part_m, 2 * part_m),
    )

    def features(start, size):
        return pl.ds(pl.multiple_of(start, 128), size)

    def merge_out(start, size):
        at = features(start, size)
        return remote(
            w_merge.at[:, at], wm.at[rows_at(j * share, share), at], i, far
        )

    r_on, r_on_last = next(numbers), next(numbers)
    far_shard = rows_at(far * share, share)

    def merge_pass(start, size, recv):
        at = features(start, size)
        return remote(wm.at[far_shard, at], wm.at[far_shard, at], i, partner, recv)

    merge_far = [merge_out(*piece) for piece in pieces_m[:4]]
    merge_on = [merge_pass(*piece, r_on_last if n == 3 else r_on) for n, piece in enumerate(pieces_m)]
    at = features(*pieces_m[0])
    merge_side = remote(wm.at[far_shard, at], wm.at[far_shard, at], i, j, part=beside)
    merge_beside = remote(w_merge, wm.at[rows_at(j * share, share), :], i, partner)

    part_u = half // 12
    r_up = next(numbers)

    def up_piece(start, size):
        here = rows_at(other * half + bit * 6 * part_u + start, size)
        return (
            remote(
                w_up.at[rows_at(bit * 6 * part_u + start, size), :],
                up.at[rows_at(i * half + bit * 6 * part_u + start, size), :], other, j,
            ),
            remote(up.at[here, :], up.at[here, :], i, j, r_up, beside),
        )

    up_out, up_on = zip(
        up_piece(0, 2 * part_u), up_piece(2 * part_u, 3 * part_u), up_piece(5 * part_u, part_u)
    )
    part_d = ff // 16
    spans = (
        rows_at(bit * 5 * part_d, 2 * part_d),
        rows_at(bit * 5 * part_d + 2 * part_d, 3 * part_d),
        pl.ds(10 * part_d, 6 * part_d),
    )
    r_down = next(numbers)
    down_out = [remote(w_down.at[at, :], down.at[i, at, :], other, j) for at in spans]
    down_on = [
        remote(down.at[other, at, :], down.at[other, at, :], i, j, r_down, beside)
        for at in spans[:2]
    ]
    for c in (merge_far[0], merge_beside, up_out[0], up_out[1]):
        c.start()
    for c in locals_[1:]:
        c.start()

    def unit(value):
        squares = value * value
        top = squares.astype(bf16)
        low = (squares - top.astype(f32)).astype(bf16)
        total = _dot(top, block_ones) + _dot(low, block_ones)
        return (value * lax.rsqrt(total + eps_unit)).astype(bf16)

    def project(first):
        tokens = winq[first:first + 2].reshape(2 * quad, ch)
        return (
            unit(_dot(tokens, w_qkv[:, :ch])),
            unit(_dot(tokens, w_qkv[:, ch:2 * ch])),
            _dot(tokens, w_qkv[:, 2 * ch:]).astype(bf16),
        )

    def turn_up(k):
        up_t[0, k] = up[rows_at(k * half, half), :].T

    def turn_down(k):
        down_t[0, rows_at(k * half, half), :] = down[k].T

    r_turn, r_own = next(numbers), next(numbers)

    def share_up(k):
        remote(up_t.at[0, k], up_t.at[1, k], i, partner, r_turn).start()

    def share_down(k):
        at = rows_at(k * half, half)
        remote(down_t.at[0, at, :], down_t.at[1, at, :], i, partner, r_turn).start()

    locals_[1].wait()
    quads[2].wait_recv()
    late = project(2)
    merge_far[1].start()
    all_of(winq.at[pl.ds(0, 2)], recvs.at[r_quads])
    early = project(0)
    qhat, khat, vals = (jnp.concatenate([a, b], axis=0) for a, b in zip(early, late))
    merge_far[0].wait_recv()
    merge_side.start()
    merge_on[0].start()
    locals_[2].wait()
    per = 128 // width
    lanes = lax.broadcasted_iota(jnp.int32, (4 * quad, 128), 1) // width
    for b in range(ch // 128):
        cut = slice(b * 128, (b + 1) * 128)
        qb, kb, vb = qhat[:, cut], khat[:, cut], vals[:, cut]
        acc = None
        for t in range(per):
            mine = lanes == t
            zero = jnp.zeros_like(qb)
            scores = _dot(jnp.where(mine, qb, zero), kb, 1, 1) * logit[b * per + t]
            weights = jnp.exp(scores)
            weights = (weights / jnp.sum(weights, axis=-1, keepdims=True)).astype(bf16)
            term = _dot(weights, jnp.where(mine, vb, zero))
            acc = term if acc is None else acc + term
        mixw[:, :, cut] = acc.astype(bf16).reshape(4, quad, 128)
    r_back = next(numbers)
    for k in range(3):
        remote(mixw.at[k], mixq.at[k], *backs[k], r_back).start()
    merge_far[2].start()
    merge_far[3].start()
    up_out[2].start()
    mixq[3] = mixw[3]
    up_out[0].wait_recv()
    up_on[0].start()
    all_of(elements(ch * ch + own * c4 + share * w_merge.shape[1] + 2 * half * ff), loc.at[3])
    turn_up(i)
    turn_down(i)
    share_up(i)
    share_down(i)
    up_out[1].wait_recv()
    up_on[1].start()
    down_out[0].start()
    down_out[1].start()
    merge_far[1].wait_recv()
    merge_on[1].start()
    merge_side.wait_recv()
    merge_on[4].start()
    all_of(mixq.at[pl.ds(0, 3)], recvs.at[r_back])
    normed, _ = _ln(_dot(mixq[...].reshape(4 * quad, ch), w_proj[...]))
    flat = jnp.concatenate([quarter(k // 2, k % 2) for k in range(4)], axis=0)
    stream = (flat + normed).astype(bf16)
    picked = _dot(perm[...], stream).astype(bf16)
    merged = jnp.concatenate([picked[k * quad:(k + 1) * quad] for k in range(4)], axis=1)
    up_out[2].wait_recv()
    up_on[2].start()

    pair = j // 2
    pairs = (pair, (pair + 1) % 2)

    def project_pair(p, start, stop):
        at = pl.ds(pl.multiple_of(p * 2 * share, 128), 2 * share)
        return _dot(merged[:, start:stop], wm[at, start:stop], 1, 1)

    features_in = w_merge.shape[1]
    merge_beside.wait_recv()
    proj[pairs[0]] = project_pair(pairs[0], 0, features_in)
    down_out[2].start()
    merge_far[2].wait_recv()
    merge_on[2].start()
    merge_far[3].wait_recv()
    merge_on[3].start()
    down_out[0].wait_recv()
    down_on[0].start()
    all_of(wm.at[rows_at(far_partner * share, share), pl.ds(0, 11 * part_m)], recvs.at[r_on])
    proj[pairs[1]] = project_pair(pairs[1], 0, features_in - part_m)
    merge_last = wm.at[rows_at(far_partner * share, share), pl.ds(11 * part_m, part_m)]
    all_of(merge_last, recvs.at[r_on_last])
    proj[pairs[1]] += project_pair(pairs[1], features_in - part_m, features_in)
    level, _ = _ln(jnp.concatenate([proj[p] for p in range(2)], axis=1))

    def put(ref, blk, value):
        for k in range(ni):
            ref[0, blk, k] = value[:, k * half:(k + 1) * half].astype(bf16)

    def take(ref, b, p):
        return jnp.concatenate(
            [ref[b, pl.ds(p * 2, 2), k].reshape(2 * own, half) for k in range(ni)], axis=1
        )

    put(lvl, j, level)
    r_gather = [next(numbers) for _ in range(3)]
    r_far_sum, r_own_sum, r_grad = next(numbers), next(numbers), next(numbers)

    class Gathered:
        def __init__(self, ref):
            def send(b, slot, to, row, col, recv=None):
                return remote(ref.at[b, slot], ref.at[to, slot], row, col, recv)

            self.out_partner = send(0, j, 0, i, partner, r_gather[0])
            self.out_far = send(0, j, 0, i, far, r_gather[2])
            self.onward = send(0, far, 0, i, partner, r_gather[1])
            self.across = send(0, j, 1, other, j)
            self.across_far = send(0, far, 1, other, j)
            self.across_on = [send(1, s, 1, i, partner) for s in (j, far)]

    levels = Gathered(lvl)
    levels.out_far.start()
    levels.out_partner.start()
    cot_out = remote(cot, cot_far, i, far)

    def forward(b, p):
        pre = _dot(take(lvl, b, p), up[...])
        cdf = 0.5 * (1.0 + lax.erf(pre * np.float32(np.sqrt(0.5))))
        hid[b, p] = (pre * cdf).astype(bf16)
        slope = cdf + pre * (jnp.exp(-0.5 * pre * pre) * np.float32(1 / np.sqrt(2 * np.pi)))
        dgel[b, pl.ds(p * 2, 2)] = slope.reshape(2, own, ff)

    def branch(p, k):
        bsend[pl.ds(p * 2, 2), k] = _dot(hid[0, p], down[k]).astype(bf16).reshape(2, own, half)

    def turn_tokens(b, lvl_out, hid_out):
        for p in range(2):
            at = slice(p * 2 * own, (p + 1) * 2 * own)
            lvl_out[:, at] = lvl[b, 2 * p:2 * p + 2, i].reshape(2 * own, half).T
            hid_out[:, at] = hid[b, p].T

    order = (i, other)
    near = [remote(bsend.at[partner, k], brecv.at[0, k], i, partner) for k in order]
    first = [
        remote(bsend.at[far_partner, k], brecv.at[1, k], i, partner) for k in order
    ]
    far_sum = [remote(brecv.at[3, k], brecv.at[2, k], i, far, r_far_sum) for k in order]
    own_sum = [remote(brecv.at[5, k], brecv.at[4, k], i, far, r_own_sum) for k in order]

    def pass_far(n):
        first[n].wait_recv()
        k = order[n]
        brecv[3, k] = (bsend[far, k].astype(f32) + brecv[1, k].astype(f32)).astype(bf16)
        far_sum[n].start()

    def pass_own(n):
        near[n].wait_recv()
        k = order[n]
        brecv[5, k] = (bsend[j, k].astype(f32) + brecv[0, k].astype(f32)).astype(bf16)
        own_sum[n].start()

    def total_of(blk, in_chip, from_far, sem):
        all_of(brecv.at[from_far], recvs.at[sem])
        total = bsend[blk].astype(f32) + brecv[in_chip].astype(f32) + brecv[from_far].astype(f32)
        return jnp.concatenate([total[k] for k in range(ni)], axis=1)

    def slopes_of(total, g):
        norm, inverse = _ln(total)
        return norm, inverse * (
            g - jnp.mean(g, axis=-1, keepdims=True)
            - norm * jnp.mean(g * norm, axis=-1, keepdims=True)
        )

    down_out[1].wait_recv()
    down_on[1].start()
    all_of(up.at[rows_at(other * half + (1 - bit) * 6 * part_u, 6 * part_u), :], recvs.at[r_up])
    levels.out_partner.wait_recv()
    forward(0, pairs[0])
    branch(pairs[0], i)
    near[0].start()
    pass_own(0)
    cot_out.start()
    levels.out_far.wait_recv()
    levels.onward.start()
    turn_up(other)
    levels.onward.wait_recv()
    forward(0, pairs[1])
    branch(pairs[1], i)
    first[0].start()
    down_out[2].wait_recv()
    levels.across.start()
    levels.across_far.start()
    all_of(down.at[other, rows_at((1 - bit) * 5 * part_d, 5 * part_d), :], recvs.at[r_down])
    branch(pairs[1], other)
    first[1].start()
    branch(pairs[0], other)
    near[1].start()
    pass_far(0)
    pass_far(1)
    for n, blk in enumerate((partner, far_partner)):
        remote(dgel.at[0, blk], dgel_p.at[n], i, partner, r_turn).start()
    turn_down(other)
    pass_own(1)
    share_down(other)
    share_up(other)
    turn_tokens(0, lvl_t, hid_t)
    levels.across.wait_recv()
    levels.across_on[0].start()
    total = total_of(j, 0, 2, r_far_sum)
    g = cot[...].astype(f32)
    norm, slope = slopes_of(total, g)
    put(slo, j, slope)
    slopes = Gathered(slo)
    slopes.across.start()
    slopes.out_partner.start()
    coarse[...] = level + norm
    def backward(p):
        blocks = pl.ds(p * 2, 2)
        slope = dgel[1, blocks].reshape(2 * own, ff) * _dot(take(slo, 1, p), down_t[0])
        rows = pl.ds(pl.multiple_of(p * 2 * own, 128), 2 * own)
        back_spre[rows, :] = slope.astype(bf16)
        back_slo[rows, :] = slo[1, blocks, i].reshape(2 * own, half)

    def block_slopes(blk, n):
        so = jnp.concatenate([slo[0, blk, k] for k in range(ni)], axis=1)
        mine = (dgel[0, blk] * _dot(so, down_t[0])).astype(bf16)
        theirs = (dgel_p[n] * _dot(so, down_t[1])).astype(bf16)
        spre[blk] = mine
        spre_p[n] = theirs
        remote(spre_p.at[n], spre.at[blk], i, partner, r_own).start()
        return mine, theirs

    def input_slopes(slopes_here):
        terms = [
            _dot(v, jnp.concatenate([up_t[n, k] for k in range(ni)], axis=1))
            for n, v in enumerate(slopes_here)
        ]
        return terms[0] + terms[1]

    all_of(elements(2 * c4 * ff + 4 * own * ff), recvs.at[r_turn])
    cot_out.wait_recv()
    total = total_of(far, 1, 4, r_own_sum)
    _, slope = slopes_of(total, cot_far[...].astype(f32))
    put(slo, far, slope)
    slopes.across_far.start()
    slopes.onward.start()

    levels.across_far.wait_recv()
    levels.across_on[1].start()
    far_slopes = block_slopes(far, 1)
    gsend[...] = input_slopes(far_slopes).astype(bf16)
    remote(gsend, grecv, i, far, r_grad).start()
    own_slopes = block_slopes(j, 0)
    gown[...] = input_slopes(own_slopes)
    levels.across_on[0].wait_recv()
    forward(1, pairs[0])
    levels.across_on[1].wait_recv()
    forward(1, pairs[1])
    turn_tokens(1, back_lvl, back_hid)
    slopes.across.wait_recv()
    slopes.across_on[0].start()
    slopes.out_partner.wait_recv()
    slopes.onward.wait_recv()
    all_of(spre_p, recvs.at[r_own])
    gup[...] = _dot(lvl_t[...], spre[...].reshape(nj * own, ff))
    gdown[...] = _dot(hid_t[...], slo[0, :, i].reshape(nj * own, half))
    slopes.across_far.wait_recv()
    slopes.across_on[1].start()
    slopes.across_on[0].wait_recv()
    backward(pairs[0])
    slopes.across_on[1].wait_recv()
    backward(pairs[1])
    all_of(grecv, recvs.at[r_grad])
    gcoarse[...] = g + gown[...] + grecv[...].astype(f32)
    all_of(tally, sent)
def store_kernel(
    coarse_in, gcoarse_in, gup_in, gdown_in, lvl_t, spre, hid_t, slo,
    coarse, gcoarse, gup, gdown, up_sum, down_sum, sem,
):
    for n, (src, dst) in enumerate(((coarse_in, coarse), (gcoarse_in, gcoarse))):
        pltpu.make_async_copy(src, dst, sem.at[n]).start()
    pieces = ((gup_in, lvl_t, spre, up_sum, gup), (gdown_in, hid_t, slo, down_sum, gdown))
    for part in range(PARTS):
        for n, (before, left, right, total, out) in enumerate(pieces):
            rows = total.shape[0] // PARTS
            at = pl.ds(part * rows, rows)
            total[at, :] = before[at, :] + _dot(left[at, :], right[...])
            pltpu.make_async_copy(total.at[at, :], out.at[at, :], sem.at[2 + n]).start()
    pltpu.make_async_copy(coarse_in, coarse, sem.at[0]).wait()
    pltpu.make_async_copy(gcoarse_in, gcoarse, sem.at[1]).wait()
    pltpu.make_async_copy(up_sum, gup, sem.at[2]).wait()
    pltpu.make_async_copy(down_sum, gdown, sem.at[3]).wait()


def fused(fields, logit_scale, w_qkv, w_proj, w_merge, w_up, w_down, cotangent):
    tile_rows, tile_cols, ch = fields.shape
    ni, nj = lax.axis_size("rows"), lax.axis_size("cols")
    own = cotangent.shape[0] * cotangent.shape[1]
    c4 = cotangent.shape[-1]
    half, ff = w_up.shape
    f32, bf16 = jnp.float32, jnp.bfloat16
    quad = (WIN // 2) ** 2
    hb = pl.BlockSpec(memory_space=pltpu.HBM)
    vm = pl.BlockSpec(memory_space=pltpu.VMEM)
    dma = pltpu.SemaphoreType.DMA
    sent = (
        6 * quad * ch + 3 * w_merge.size + 2 * w_up.size + 19 * own * c4 + 2 * c4 * ff + 6 * own * ff
    )
    outs = (
        jax.ShapeDtypeStruct((own, c4), f32),
        jax.ShapeDtypeStruct((own, c4), f32),
        jax.ShapeDtypeStruct((half, ff), f32),
        jax.ShapeDtypeStruct((ff, half), f32),
    )
    gathered = pltpu.VMEM((ni, nj, ni, own, half), bf16)
    operands = [fields, logit_scale, w_qkv, w_proj, w_merge.T, w_up, w_down, cotangent.reshape(own, c4)]
    operands = [pltpu.with_memory_space_constraint(v, pltpu.HBM) for v in operands]
    values = pl.pallas_call(
        fused_kernel,
        out_shape=outs + (
            jax.ShapeDtypeStruct((half, nj * own), bf16),
            jax.ShapeDtypeStruct((nj * own, ff), bf16),
            jax.ShapeDtypeStruct((ff, nj * own), bf16),
            jax.ShapeDtypeStruct((nj * own, half), bf16),
        ),
        in_specs=[hb] * 8,
        out_specs=(vm,) * 8,
        scratch_shapes=[
            pltpu.VMEM(fields.shape, f32),
            pltpu.SMEM(logit_scale.shape, f32),
            pltpu.VMEM(w_qkv.shape, bf16),
            pltpu.VMEM(w_proj.shape, bf16),
            pltpu.VMEM((own, c4), bf16),
            pltpu.VMEM((own, c4), bf16),
            pltpu.VMEM((3, quad, ch), bf16),
            pltpu.VMEM((4, quad, ch), bf16),
            pltpu.VMEM((4, quad, ch), bf16),
            pltpu.VMEM((4, quad, ch), bf16),
            pltpu.VMEM((4 * quad, 4 * quad), bf16),
            pltpu.VMEM((c4, w_merge.shape[0]), bf16),
            pltpu.VMEM((2, own, c4 // 2), f32),
            pltpu.VMEM((c4, ff), bf16),
            pltpu.VMEM((ni, ff, half), bf16),
            pltpu.VMEM((2, ni, ff, half), bf16),
            pltpu.VMEM((2, c4, ff), bf16),
            gathered,
            pltpu.VMEM((ni, 2, 2 * own, ff), bf16),
            pltpu.VMEM((half, nj * own), bf16),
            pltpu.VMEM((ff, nj * own), bf16),
            pltpu.VMEM((ni, nj, own, ff), f32),
            pltpu.VMEM((2, own, ff), f32),
            pltpu.VMEM((nj, ni, own, half), bf16),
            pltpu.VMEM((6, ni, own, half), bf16),
            gathered,
            pltpu.VMEM((nj, own, ff), bf16),
            pltpu.VMEM((2, own, ff), bf16),
            pltpu.VMEM((own, c4), f32),
            pltpu.VMEM((own, c4), bf16),
            pltpu.VMEM((own, c4), bf16),
            pltpu.VMEM((sent // 128, 128), bf16),
            dma((4,)),
            dma,
            dma((N_RECVS,)),
        ],
        compiler_params=pltpu.CompilerParams(
            collective_id=0, has_side_effects=True, vmem_limit_bytes=44 << 20
        ),
    )(*operands)
    values = pl.pallas_call(
        store_kernel,
        out_shape=outs,
        in_specs=[vm] * 8,
        out_specs=(hb,) * 4,
        scratch_shapes=[pltpu.VMEM((half, ff), f32), pltpu.VMEM((ff, half), f32), dma((4,))],
        compiler_params=pltpu.CompilerParams(vmem_limit_bytes=12 << 20),
    )(*values)
    shape = (tile_rows // 2, tile_cols // 2, c4)
    return values[0].reshape(shape), values[1].reshape(shape), values[2], values[3]


def device_body(*args):
    fields, _, w_qkv, _, w_merge, w_up, w_down, _ = args
    fits = (
        lax.axis_size("rows") == 2
        and lax.axis_size("cols") == 4
        and lax.axis_size("dp") % 2 == 0
        and fields.shape[:2] == (WIN, WIN)
        and w_up.shape[0] % 128 == 0
        and w_up.shape[1] % 128 == 0
        and w_merge.shape[1] % 64 == 0
        and w_merge.shape[0] % 1536 == 0
        and w_up.shape[0] % 384 == 0
        and w_up.shape[1] % 256 == 0
        and fields.shape[-1] % 128 == 0
    )
    return fused(*args) if fits else local(*args)


def solution(mesh):
    return jax.shard_map(
        device_body,
        mesh=mesh,
        in_specs=(
            P(("dp", "rows"), "cols", None),
            P(),
            P(),
            P(),
            P(None, "cols"),
            P("rows", "cols"),
            P("cols", "rows"),
            P(("dp", "rows"), "cols", None),
        ),
        out_specs=(
            P(("dp", "rows"), "cols", None),
            P(("dp", "rows"), "cols", None),
            P("rows", ("dp", "cols")),
            P("cols", ("dp", "rows")),
        ),
        check_vma=False,
    )
```

```python
import jax
import jax.numpy as jnp
import numpy as np
from jax import lax
from jax.experimental import pallas as pl
from jax.experimental.pallas import tpu as pltpu
from jax.sharding import PartitionSpec as P

WIN = 16


eps_norm = 1e-05
eps_unit = 1e-06
N_RECVS = 43
PARTS = 4


def padded_2(cells, sides, width):
    for axis, dim in sides:
        count = lax.axis_size(axis)
        head = lax.slice_in_dim(cells, 0, width, axis=dim)
        tail = lax.slice_in_dim(cells, cells.shape[dim] - width, cells.shape[dim], axis=dim)
        cells = jnp.concatenate(
            [
                lax.ppermute(tail, axis, [(i, (i + 1) % count) for i in range(count)]),
                cells,
                lax.ppermute(head, axis, [((i + 1) % count, i) for i in range(count)]),
            ],
            axis=dim,
        )
    return cells


def layer_norm(value):
    average = jnp.mean(value, axis=-1, keepdims=True)
    centred = value - average
    spread = jnp.mean(centred * centred, axis=-1, keepdims=True)
    inverse = lax.rsqrt(spread + eps_norm)
    return (centred * inverse, inverse)


def norm_slope(upstream, normed, inverse):
    first_mean = jnp.mean(upstream, axis=-1, keepdims=True)
    second_mean = jnp.mean(upstream * normed, axis=-1, keepdims=True)
    return inverse * (upstream - first_mean - normed * second_mean)


def unit_heads(value, head_count):
    shaped = value.reshape(value.shape[:-1] + (head_count, value.shape[-1] // head_count))
    squares = jnp.sum(shaped * shaped, axis=-1, keepdims=True)
    return (shaped * lax.rsqrt(squares + eps_unit)).reshape(value.shape)


def windows_of(field_grid, window):
    grid_rows, grid_cols, channels = field_grid.shape
    shaped = field_grid.reshape(grid_rows // window, window, grid_cols // window, window, channels)
    return shaped.transpose(0, 2, 1, 3, 4).reshape(-1, window * window, channels)


def grid_of(blocks, grid_rows, grid_cols, window):
    channels = blocks.shape[-1]
    shaped = blocks.reshape(grid_rows // window, grid_cols // window, window, window, channels)
    return shaped.transpose(0, 2, 1, 3, 4).reshape(grid_rows, grid_cols, channels)


def attend(queries, key_rows, value_rows, logit_scale, head_count):
    number, window_size, channels = queries.shape
    width_head = channels // head_count
    query_heads = queries.reshape(number, window_size, head_count, width_head)
    key_heads = key_rows.reshape(number, window_size, head_count, width_head)
    value_heads = value_rows.reshape(number, window_size, head_count, width_head)
    scores = jnp.einsum(
        "wqhd,wkhd->whqk", query_heads, key_heads, preferred_element_type=jnp.float32
    )
    weights = jnp.exp(scores * logit_scale[None, :, None, None])
    weights = (weights / jnp.sum(weights, axis=-1, keepdims=True)).astype(jnp.bfloat16)
    mixed_out = jnp.einsum(
        "whqk,wkhd->wqhd", weights, value_heads, preferred_element_type=jnp.float32
    )
    return mixed_out.reshape(number, window_size, channels)


def merge_patches(field_grid):
    quarters = (
        field_grid[0::2, 0::2],
        field_grid[1::2, 0::2],
        field_grid[0::2, 1::2],
        field_grid[1::2, 1::2],
    )
    return jnp.concatenate(quarters, axis=-1)


def exact_gelu(value):
    return jax.nn.gelu(value, approximate=False)


def local(fields, logit_scale, w_qkv, w_proj, w_merge, w_up, w_down, cotangent):
    tile_rows, tile_cols, channels = fields.shape
    offset = WIN // 2
    head_count = logit_scale.shape[0]
    tokens = fields.astype(jnp.bfloat16)
    token_rows = tokens.reshape(-1, channels)
    wide_rows = tile_rows + WIN
    wide_cols = tile_cols + WIN
    widened = padded_2(tokens, (("rows", 0), ("cols", 1)), offset)
    wide_proj = jnp.dot(
        widened.reshape(-1, channels), w_qkv[:, channels:], preferred_element_type=jnp.float32
    )
    key_grid = unit_heads(wide_proj[:, :channels], head_count).astype(jnp.bfloat16)
    value_grid = wide_proj[:, channels:].astype(jnp.bfloat16)
    query_raw = jnp.dot(token_rows, w_qkv[:, :channels], preferred_element_type=jnp.float32)
    queries = (
        unit_heads(query_raw, head_count)
        .astype(jnp.bfloat16)
        .reshape(tile_rows, tile_cols, channels)
    )
    padded = jnp.pad(queries, ((offset, offset), (offset, offset), (0, 0)))
    key_blocks = windows_of(key_grid.reshape(wide_rows, wide_cols, channels), WIN)
    value_blocks = windows_of(value_grid.reshape(wide_rows, wide_cols, channels), WIN)
    mixed = attend(windows_of(padded, WIN), key_blocks, value_blocks, logit_scale, head_count)
    mixed = grid_of(mixed, wide_rows, wide_cols, WIN)[
        offset : offset + tile_rows, offset : offset + tile_cols
    ]
    mixed = mixed.astype(jnp.bfloat16).reshape(-1, channels)
    normed, _ = layer_norm(jnp.dot(mixed, w_proj, preferred_element_type=jnp.float32))
    stream = fields + normed.reshape(fields.shape)
    merged = merge_patches(stream).astype(jnp.bfloat16)
    merged_rows = merged.reshape(-1, merged.shape[-1])
    own_count = merged_rows.shape[0]
    partial_band = jnp.dot(
        lax.all_gather(merged_rows, "cols", axis=0, tiled=True),
        w_merge,
        preferred_element_type=jnp.float32,
    )
    projected_band = lax.all_gather(
        partial_band.astype(jnp.bfloat16), "cols", axis=1, tiled=True
    ).astype(partial_band.dtype)
    level_band, _ = layer_norm(projected_band)
    level_b = level_band.astype(jnp.bfloat16)
    level_own = lax.dynamic_slice_in_dim(
        level_band, lax.axis_index("cols") * own_count, own_count, 0
    )
    up_full = lax.all_gather(w_up, "rows", axis=0, tiled=True)
    down_full = lax.all_gather(w_down, "rows", axis=1, tiled=True)
    hidden_pre = jnp.dot(level_b, up_full, preferred_element_type=jnp.float32)
    hidden = exact_gelu(hidden_pre).astype(jnp.bfloat16)
    rows_part = hidden
    branch_out = lax.psum_scatter(
        jnp.dot(rows_part, down_full, preferred_element_type=jnp.float32).astype(jnp.bfloat16),
        "cols",
        scatter_dimension=0,
        tiled=True,
    ).astype(jnp.float32)
    branch_norm, branch_inv = layer_norm(branch_out)
    coarse = level_own + branch_norm
    upstream = cotangent.astype(jnp.float32).reshape(own_count, -1)
    slope_own = norm_slope(upstream, branch_norm, branch_inv).astype(jnp.bfloat16)
    slope_out = lax.all_gather(slope_own, "cols", axis=0, tiled=True)
    slope_hidden = jnp.einsum("tc,fc->tf", slope_out, down_full, preferred_element_type=jnp.float32)
    _, pullback = jax.vjp(exact_gelu, hidden_pre)
    slope_pre = pullback(slope_hidden)[0].astype(jnp.bfloat16)
    rows_part = slope_pre
    slope_input = lax.psum_scatter(
        jnp.einsum("tf,cf->tc", rows_part, up_full, preferred_element_type=jnp.float32).astype(
            jnp.bfloat16
        ),
        "cols",
        scatter_dimension=0,
        tiled=True,
    ).astype(jnp.float32)
    grad_coarse = upstream + slope_input
    term_up = jnp.einsum("tc,tf->cf", level_b, slope_pre, preferred_element_type=jnp.float32)
    term_down = jnp.einsum("tf,tc->fc", hidden, slope_out, preferred_element_type=jnp.float32)
    grad_up, grad_down = (
        lax.psum_scatter(
            term_up.astype(jnp.bfloat16), "rows", scatter_dimension=0, tiled=True
        ).astype(jnp.float32),
        lax.psum_scatter(
            term_down.astype(jnp.bfloat16), "rows", scatter_dimension=1, tiled=True
        ).astype(jnp.float32),
    )
    coarse_shape = (tile_rows // 2, tile_cols // 2, coarse.shape[-1])
    return (coarse.reshape(coarse_shape), grad_coarse.reshape(coarse_shape), grad_up, grad_down)


def _ln(value):
    average = jnp.mean(value, axis=-1, keepdims=True)
    centred = value - average
    spread = jnp.mean(centred * centred, axis=-1, keepdims=True)
    inverse = lax.rsqrt(spread + eps_norm)
    return centred * inverse, inverse


def _dot(a, b, ca=1, cb=0):
    return lax.dot_general(
        a, b, (((ca,), (cb,)), ((), ())), preferred_element_type=jnp.float32
    )


def fused_kernel(
    fields_h, logit_h, w_qkv_h, w_proj_h, w_merge, w_up, w_down, cot_h,
    coarse, gcoarse, gup, gdown, back_lvl, back_spre, back_hid, back_slo,
    fields, logit, w_qkv, w_proj, cot, cot_far,
    sendq, winq, mixw, mixq, perm, wm, proj, up, down, up_t, down_t,
    lvl, hid, lvl_t, hid_t, dgel, dgel_p, bsend, brecv, slo, spre, spre_p, gown, gsend, grecv,
    tally, loc, sent, recvs,
):
    f32, bf16 = jnp.float32, jnp.bfloat16
    i, j = lax.axis_index("rows"), lax.axis_index("cols")
    ni, nj = lax.axis_size("rows"), lax.axis_size("cols")
    z = lax.axis_index("dp")
    beside = z + 1 - 2 * (z % 2)
    bit = z % 2
    half_side = WIN // 2
    quad = half_side * half_side
    ch = fields.shape[-1]
    c4 = cot.shape[-1]
    own = cot.shape[0]
    half = c4 // ni
    ff = w_up.shape[1]
    share = w_merge.shape[0]
    heads = logit.shape[0]
    width = ch // heads
    other = (i + 1) % ni
    prev_j, next_j = (j + nj - 1) % nj, (j + 1) % nj
    partner = j + 1 - 2 * (j % 2)
    far = (j + 2) % nj
    far_partner = (partner + 2) % nj
    peers = (partner, far, far_partner)
    numbers = iter(range(N_RECVS))

    def remote(src, dst, row, col, recv=None, part=z):
        n = next(numbers) if recv is None else recv
        return pltpu.make_async_remote_copy(
            src_ref=src, dst_ref=dst, send_sem=sent, recv_sem=recvs.at[n],
            device_id={"rows": row, "cols": col, "dp": part},
            device_id_type=pl.DeviceIdType.MESH,
        )

    def all_of(ref, sem):
        pltpu.make_async_copy(ref, ref, sem).wait()

    def elements(count):
        return tally.at[pl.ds(0, count // tally.shape[1]), :]

    first_copy = pltpu.make_async_copy(fields_h, fields, loc.at[0])
    first_copy.start()
    barrier = pltpu.get_barrier_semaphore()
    greet = [(i, p) for p in peers] + [(other, j), (other, prev_j), (other, next_j)]
    for row, col in greet:
        pl.semaphore_signal(
            barrier, inc=1, device_id={"rows": row, "cols": col},
            device_id_type=pl.DeviceIdType.MESH,
        )
    pl.semaphore_signal(
        barrier, inc=1, device_id={"dp": beside}, device_id_type=pl.DeviceIdType.MESH
    )

    def rows_at(start, size):
        return pl.ds(pl.multiple_of(start, 16), size)

    locals_ = [first_copy] + [
        pltpu.make_async_copy(src, dst, loc.at[min(n + 1, 3)])
        for n, (src, dst) in enumerate((
            (w_qkv_h, w_qkv),
            (logit_h, logit),
            (w_proj_h, w_proj),
            (cot_h, cot),
            (w_merge, wm.at[rows_at(j * share, share), :]),
            (w_up, up.at[rows_at(i * half, half), :]),
            (w_down, down.at[i]),
        ))
    ]
    lane = lax.broadcasted_iota(jnp.int32, (ch, ch), 0) // width
    lane_t = lax.broadcasted_iota(jnp.int32, (ch, ch), 1) // width
    block_ones = (lane == lane_t).astype(f32).astype(bf16)
    rows_out = lax.broadcasted_iota(jnp.int32, (4 * quad, 4 * quad), 0)
    cols_in = lax.broadcasted_iota(jnp.int32, (4 * quad, 4 * quad), 1)
    which, place = rows_out // quad, rows_out % quad
    r = 2 * (place // half_side) + which % 2
    c = 2 * (place % half_side) + which // 2
    source = ((r // half_side) * 2 + c // half_side) * quad + (r % half_side) * half_side + c % half_side
    perm[...] = (source == cols_in).astype(f32).astype(bf16)

    def quarter(a, b):
        part = fields[a * half_side:(a + 1) * half_side, b * half_side:(b + 1) * half_side, :]
        return part.reshape(quad, ch)

    locals_[0].wait()
    for k in range(3):
        sendq[k] = quarter(k // 2, k % 2).astype(bf16)
    winq[3] = quarter(1, 1).astype(bf16)
    pl.semaphore_wait(barrier, len(greet) + 1)

    targets = ((other, prev_j), (other, j), (i, prev_j))
    backs = ((other, next_j), (other, j), (i, next_j))
    r_quads = next(numbers)
    quads = [
        remote(sendq.at[k], winq.at[k], *targets[k], r_quads if k < 2 else None)
        for k in range(3)
    ]
    for c in quads:
        c.start()

    part_m = w_merge.shape[1] // 12
    pieces_m = (
        (bit * 2 * part_m, 2 * part_m), (4 * part_m, 4 * part_m), (8 * part_m, 3 * part_m),
        (11 * part_m, part_m), ((1 - bit) * 2 * part_m, 2 * part_m),
    )

    def features(start, size):
        return pl.ds(pl.multiple_of(start, 128), size)

    def merge_out(start, size):
        at = features(start, size)
        return remote(
            w_merge.at[:, at], wm.at[rows_at(j * share, share), at], i, far
        )

    r_on, r_on_last = next(numbers), next(numbers)
    far_shard = rows_at(far * share, share)

    def merge_pass(start, size, recv):
        at = features(start, size)
        return remote(wm.at[far_shard, at], wm.at[far_shard, at], i, partner, recv)

    merge_far = [merge_out(*piece) for piece in pieces_m[:4]]
    merge_on = [merge_pass(*piece, r_on_last if n == 3 else r_on) for n, piece in enumerate(pieces_m)]
    at = features(*pieces_m[0])
    merge_side = remote(wm.at[far_shard, at], wm.at[far_shard, at], i, j, part=beside)
    merge_beside = remote(w_merge, wm.at[rows_at(j * share, share), :], i, partner)

    part_u = half // 12
    r_up = next(numbers)

    def up_piece(start, size):
        here = rows_at(other * half + bit * 6 * part_u + start, size)
        return (
            remote(
                w_up.at[rows_at(bit * 6 * part_u + start, size), :],
                up.at[rows_at(i * half + bit * 6 * part_u + start, size), :], other, j,
            ),
            remote(up.at[here, :], up.at[here, :], i, j, r_up, beside),
        )

    up_out, up_on = zip(
        up_piece(0, 2 * part_u), up_piece(2 * part_u, 3 * part_u), up_piece(5 * part_u, part_u)
    )
    part_d = ff // 16
    spans = (
        rows_at(bit * 5 * part_d, 2 * part_d),
        rows_at(bit * 5 * part_d + 2 * part_d, 3 * part_d),
        pl.ds(10 * part_d, 6 * part_d),
    )
    r_down = next(numbers)
    down_out = [remote(w_down.at[at, :], down.at[i, at, :], other, j) for at in spans]
    down_on = [
        remote(down.at[other, at, :], down.at[other, at, :], i, j, r_down, beside)
        for at in spans[:2]
    ]
    for c in (merge_far[0], merge_beside, up_out[0], up_out[1]):
        c.start()
    for c in locals_[1:]:
        c.start()

    def unit(value):
        squares = value * value
        top = squares.astype(bf16)
        low = (squares - top.astype(f32)).astype(bf16)
        total = _dot(top, block_ones) + _dot(low, block_ones)
        return (value * lax.rsqrt(total + eps_unit)).astype(bf16)

    def project(first):
        tokens = winq[first:first + 2].reshape(2 * quad, ch)
        return (
            unit(_dot(tokens, w_qkv[:, :ch])),
            unit(_dot(tokens, w_qkv[:, ch:2 * ch])),
            _dot(tokens, w_qkv[:, 2 * ch:]).astype(bf16),
        )

    def turn_up(k):
        up_t[0, k] = up[rows_at(k * half, half), :].T

    def turn_down(k):
        down_t[0, rows_at(k * half, half), :] = down[k].T

    r_turn, r_own = next(numbers), next(numbers)

    def share_up(k):
        remote(up_t.at[0, k], up_t.at[1, k], i, partner, r_turn).start()

    def share_down(k):
        at = rows_at(k * half, half)
        remote(down_t.at[0, at, :], down_t.at[1, at, :], i, partner, r_turn).start()

    locals_[1].wait()
    quads[2].wait_recv()
    late = project(2)
    merge_far[1].start()
    all_of(winq.at[pl.ds(0, 2)], recvs.at[r_quads])
    early = project(0)
    qhat, khat, vals = (jnp.concatenate([a, b], axis=0) for a, b in zip(early, late))
    merge_far[0].wait_recv()
    merge_side.start()
    merge_on[0].start()
    locals_[2].wait()
    per = 128 // width
    lanes = lax.broadcasted_iota(jnp.int32, (4 * quad, 128), 1) // width
    for b in range(ch // 128):
        cut = slice(b * 128, (b + 1) * 128)
        qb, kb, vb = qhat[:, cut], khat[:, cut], vals[:, cut]
        acc = None
        for t in range(per):
            mine = lanes == t
            zero = jnp.zeros_like(qb)
            scores = _dot(jnp.where(mine, qb, zero), kb, 1, 1) * logit[b * per + t]
            weights = jnp.exp(scores)
            weights = (weights / jnp.sum(weights, axis=-1, keepdims=True)).astype(bf16)
            term = _dot(weights, jnp.where(mine, vb, zero))
            acc = term if acc is None else acc + term
        mixw[:, :, cut] = acc.astype(bf16).reshape(4, quad, 128)
    r_back = next(numbers)
    for k in range(3):
        remote(mixw.at[k], mixq.at[k], *backs[k], r_back).start()
    merge_far[2].start()
    merge_far[3].start()
    up_out[2].start()
    mixq[3] = mixw[3]
    up_out[0].wait_recv()
    up_on[0].start()
    all_of(elements(ch * ch + own * c4 + share * w_merge.shape[1] + 2 * half * ff), loc.at[3])
    turn_up(i)
    turn_down(i)
    share_up(i)
    share_down(i)
    up_out[1].wait_recv()
    up_on[1].start()
    down_out[0].start()
    down_out[1].start()
    merge_far[1].wait_recv()
    merge_on[1].start()
    merge_side.wait_recv()
    merge_on[4].start()
    all_of(mixq.at[pl.ds(0, 3)], recvs.at[r_back])
    normed, _ = _ln(_dot(mixq[...].reshape(4 * quad, ch), w_proj[...]))
    flat = jnp.concatenate([quarter(k // 2, k % 2) for k in range(4)], axis=0)
    stream = (flat + normed).astype(bf16)
    picked = _dot(perm[...], stream).astype(bf16)
    merged = jnp.concatenate([picked[k * quad:(k + 1) * quad] for k in range(4)], axis=1)
    up_out[2].wait_recv()
    up_on[2].start()

    pair = j // 2
    pairs = (pair, (pair + 1) % 2)

    def project_pair(p, start, stop):
        at = pl.ds(pl.multiple_of(p * 2 * share, 128), 2 * share)
        return _dot(merged[:, start:stop], wm[at, start:stop], 1, 1)

    features_in = w_merge.shape[1]
    merge_beside.wait_recv()
    proj[pairs[0]] = project_pair(pairs[0], 0, features_in)
    down_out[2].start()
    merge_far[2].wait_recv()
    merge_on[2].start()
    merge_far[3].wait_recv()
    merge_on[3].start()
    down_out[0].wait_recv()
    down_on[0].start()
    all_of(wm.at[rows_at(far_partner * share, share), pl.ds(0, 11 * part_m)], recvs.at[r_on])
    proj[pairs[1]] = project_pair(pairs[1], 0, features_in - part_m)
    merge_last = wm.at[rows_at(far_partner * share, share), pl.ds(11 * part_m, part_m)]
    all_of(merge_last, recvs.at[r_on_last])
    proj[pairs[1]] += project_pair(pairs[1], features_in - part_m, features_in)
    level, _ = _ln(jnp.concatenate([proj[p] for p in range(2)], axis=1))

    def put(ref, blk, value):
        for k in range(ni):
            ref[0, blk, k] = value[:, k * half:(k + 1) * half].astype(bf16)

    def take(ref, b, p):
        return jnp.concatenate(
            [ref[b, pl.ds(p * 2, 2), k].reshape(2 * own, half) for k in range(ni)], axis=1
        )

    put(lvl, j, level)
    r_gather = [next(numbers) for _ in range(4)]
    r_far_sum, r_own_sum, r_grad = next(numbers), next(numbers), next(numbers)

    class Gathered:
        def __init__(self, ref):
            self.ref = ref
            halves = [pl.ds(n * (own // 2), own // 2) for n in range(2)]

            def send(b, slot, to, row, col, recv=None, at=pl.ds(0, own)):
                return remote(
                    ref.at[b, slot, :, at, :], ref.at[to, slot, :, at, :], row, col, recv
                )

            self.out_partner = send(0, j, 0, i, partner, r_gather[0])
            self.out_far = [send(0, j, 0, i, far, r_gather[2 + n], at) for n, at in enumerate(halves)]
            self.onward = [send(0, far, 0, i, partner, r_gather[1], at) for at in halves]
            self.across = send(0, j, 1, other, j)
            self.across_on = send(1, j, 1, i, partner)
            self.across_far = [send(0, far, 1, other, j, None, at) for at in halves]
            self.r_on = next(numbers)
            self.across_far_on = [send(1, far, 1, i, partner, self.r_on, at) for at in halves]

        def relay(self, arriving, leaving):
            for come, go in zip(arriving, leaving):
                come.wait_recv()
                go.start()

        def wait_onward(self):
            all_of(self.ref.at[0, far_partner], recvs.at[r_gather[1]])

        def wait_across_far_on(self):
            all_of(self.ref.at[1, far_partner], recvs.at[self.r_on])

    levels = Gathered(lvl)
    for c in levels.out_far:
        c.start()
    levels.out_partner.start()
    cot_out = remote(cot, cot_far, i, far)

    def forward(b, p):
        pre = _dot(take(lvl, b, p), up[...])
        cdf = 0.5 * (1.0 + lax.erf(pre * np.float32(np.sqrt(0.5))))
        hid[b, p] = (pre * cdf).astype(bf16)
        slope = cdf + pre * (jnp.exp(-0.5 * pre * pre) * np.float32(1 / np.sqrt(2 * np.pi)))
        dgel[b, pl.ds(p * 2, 2)] = slope.reshape(2, own, ff)

    def branch(p, k):
        bsend[pl.ds(p * 2, 2), k] = _dot(hid[0, p], down[k]).astype(bf16).reshape(2, own, half)

    def turn_tokens(b, lvl_out, hid_out):
        for p in range(2):
            at = slice(p * 2 * own, (p + 1) * 2 * own)
            lvl_out[:, at] = lvl[b, 2 * p:2 * p + 2, i].reshape(2 * own, half).T
            hid_out[:, at] = hid[b, p].T

    order = (i, other)
    near = [remote(bsend.at[partner, k], brecv.at[0, k], i, partner) for k in order]
    first = [
        remote(bsend.at[far_partner, k], brecv.at[1, k], i, partner) for k in order
    ]
    far_sum = [remote(brecv.at[3, k], brecv.at[2, k], i, far, r_far_sum) for k in order]
    own_sum = [remote(brecv.at[5, k], brecv.at[4, k], i, far, r_own_sum) for k in order]

    def pass_far(n):
        first[n].wait_recv()
        k = order[n]
        brecv[3, k] = (bsend[far, k].astype(f32) + brecv[1, k].astype(f32)).astype(bf16)
        far_sum[n].start()

    def pass_own(n):
        near[n].wait_recv()
        k = order[n]
        brecv[5, k] = (bsend[j, k].astype(f32) + brecv[0, k].astype(f32)).astype(bf16)
        own_sum[n].start()

    def total_of(blk, in_chip, from_far, sem):
        all_of(brecv.at[from_far], recvs.at[sem])
        total = bsend[blk].astype(f32) + brecv[in_chip].astype(f32) + brecv[from_far].astype(f32)
        return jnp.concatenate([total[k] for k in range(ni)], axis=1)

    def slopes_of(total, g):
        norm, inverse = _ln(total)
        return norm, inverse * (
            g - jnp.mean(g, axis=-1, keepdims=True)
            - norm * jnp.mean(g * norm, axis=-1, keepdims=True)
        )

    down_out[1].wait_recv()
    down_on[1].start()
    all_of(up.at[rows_at(other * half + (1 - bit) * 6 * part_u, 6 * part_u), :], recvs.at[r_up])
    levels.out_partner.wait_recv()
    forward(0, pairs[0])
    branch(pairs[0], i)
    near[0].start()
    pass_own(0)
    cot_out.start()
    levels.relay(levels.out_far, levels.onward)
    turn_up(other)
    levels.wait_onward()
    forward(0, pairs[1])
    branch(pairs[1], i)
    first[0].start()
    down_out[2].wait_recv()
    levels.across.start()
    for c in levels.across_far:
        c.start()
    all_of(down.at[other, rows_at((1 - bit) * 5 * part_d, 5 * part_d), :], recvs.at[r_down])
    branch(pairs[1], other)
    first[1].start()
    branch(pairs[0], other)
    near[1].start()
    pass_far(0)
    pass_far(1)
    for n, blk in enumerate((partner, far_partner)):
        remote(dgel.at[0, blk], dgel_p.at[n], i, partner, r_turn).start()
    turn_down(other)
    pass_own(1)
    share_down(other)
    share_up(other)
    turn_tokens(0, lvl_t, hid_t)
    levels.across.wait_recv()
    levels.across_on.start()
    total = total_of(j, 0, 2, r_far_sum)
    g = cot[...].astype(f32)
    norm, slope = slopes_of(total, g)
    put(slo, j, slope)
    slopes = Gathered(slo)
    slopes.across.start()
    slopes.out_partner.start()
    coarse[...] = level + norm
    def backward(p):
        blocks = pl.ds(p * 2, 2)
        slope = dgel[1, blocks].reshape(2 * own, ff) * _dot(take(slo, 1, p), down_t[0])
        rows = pl.ds(pl.multiple_of(p * 2 * own, 128), 2 * own)
        back_spre[rows, :] = slope.astype(bf16)
        back_slo[rows, :] = slo[1, blocks, i].reshape(2 * own, half)

    def block_slopes(blk, n):
        so = jnp.concatenate([slo[0, blk, k] for k in range(ni)], axis=1)
        mine = (dgel[0, blk] * _dot(so, down_t[0])).astype(bf16)
        theirs = (dgel_p[n] * _dot(so, down_t[1])).astype(bf16)
        spre[blk] = mine
        spre_p[n] = theirs
        remote(spre_p.at[n], spre.at[blk], i, partner, r_own).start()
        return mine, theirs

    def input_slopes(slopes_here):
        terms = [
            _dot(v, jnp.concatenate([up_t[n, k] for k in range(ni)], axis=1))
            for n, v in enumerate(slopes_here)
        ]
        return terms[0] + terms[1]

    all_of(elements(2 * c4 * ff + 4 * own * ff), recvs.at[r_turn])
    cot_out.wait_recv()
    total = total_of(far, 1, 4, r_own_sum)
    _, slope = slopes_of(total, cot_far[...].astype(f32))
    put(slo, far, slope)
    for c in slopes.across_far + slopes.onward:
        c.start()

    levels.relay(levels.across_far, levels.across_far_on)
    far_slopes = block_slopes(far, 1)
    gsend[...] = input_slopes(far_slopes).astype(bf16)
    remote(gsend, grecv, i, far, r_grad).start()
    own_slopes = block_slopes(j, 0)
    gown[...] = input_slopes(own_slopes)
    levels.across_on.wait_recv()
    forward(1, pairs[0])
    levels.wait_across_far_on()
    forward(1, pairs[1])
    turn_tokens(1, back_lvl, back_hid)
    slopes.across.wait_recv()
    slopes.across_on.start()
    slopes.out_partner.wait_recv()
    slopes.wait_onward()
    all_of(spre_p, recvs.at[r_own])
    gup[...] = _dot(lvl_t[...], spre[...].reshape(nj * own, ff))
    gdown[...] = _dot(hid_t[...], slo[0, :, i].reshape(nj * own, half))
    slopes.relay(slopes.across_far, slopes.across_far_on)
    slopes.across_on.wait_recv()
    backward(pairs[0])
    slopes.wait_across_far_on()
    backward(pairs[1])
    all_of(grecv, recvs.at[r_grad])
    gcoarse[...] = g + gown[...] + grecv[...].astype(f32)
    all_of(tally, sent)
def store_kernel(
    coarse_in, gcoarse_in, gup_in, gdown_in, lvl_t, spre, hid_t, slo,
    coarse, gcoarse, gup, gdown, up_sum, down_sum, sem,
):
    for n, (src, dst) in enumerate(((coarse_in, coarse), (gcoarse_in, gcoarse))):
        pltpu.make_async_copy(src, dst, sem.at[n]).start()
    pieces = ((gup_in, lvl_t, spre, up_sum, gup), (gdown_in, hid_t, slo, down_sum, gdown))
    for part in range(PARTS):
        for n, (before, left, right, total, out) in enumerate(pieces):
            rows = total.shape[0] // PARTS
            at = pl.ds(part * rows, rows)
            total[at, :] = before[at, :] + _dot(left[at, :], right[...])
            pltpu.make_async_copy(total.at[at, :], out.at[at, :], sem.at[2 + n]).start()
    pltpu.make_async_copy(coarse_in, coarse, sem.at[0]).wait()
    pltpu.make_async_copy(gcoarse_in, gcoarse, sem.at[1]).wait()
    pltpu.make_async_copy(up_sum, gup, sem.at[2]).wait()
    pltpu.make_async_copy(down_sum, gdown, sem.at[3]).wait()


def fused(fields, logit_scale, w_qkv, w_proj, w_merge, w_up, w_down, cotangent):
    tile_rows, tile_cols, ch = fields.shape
    ni, nj = lax.axis_size("rows"), lax.axis_size("cols")
    own = cotangent.shape[0] * cotangent.shape[1]
    c4 = cotangent.shape[-1]
    half, ff = w_up.shape
    f32, bf16 = jnp.float32, jnp.bfloat16
    quad = (WIN // 2) ** 2
    hb = pl.BlockSpec(memory_space=pltpu.HBM)
    vm = pl.BlockSpec(memory_space=pltpu.VMEM)
    dma = pltpu.SemaphoreType.DMA
    sent = (
        6 * quad * ch + 3 * w_merge.size + 2 * w_up.size + 19 * own * c4 + 2 * c4 * ff + 6 * own * ff
    )
    outs = (
        jax.ShapeDtypeStruct((own, c4), f32),
        jax.ShapeDtypeStruct((own, c4), f32),
        jax.ShapeDtypeStruct((half, ff), f32),
        jax.ShapeDtypeStruct((ff, half), f32),
    )
    gathered = pltpu.VMEM((ni, nj, ni, own, half), bf16)
    operands = [fields, logit_scale, w_qkv, w_proj, w_merge.T, w_up, w_down, cotangent.reshape(own, c4)]
    operands = [pltpu.with_memory_space_constraint(v, pltpu.HBM) for v in operands]
    values = pl.pallas_call(
        fused_kernel,
        out_shape=outs + (
            jax.ShapeDtypeStruct((half, nj * own), bf16),
            jax.ShapeDtypeStruct((nj * own, ff), bf16),
            jax.ShapeDtypeStruct((ff, nj * own), bf16),
            jax.ShapeDtypeStruct((nj * own, half), bf16),
        ),
        in_specs=[hb] * 8,
        out_specs=(vm,) * 8,
        scratch_shapes=[
            pltpu.VMEM(fields.shape, f32),
            pltpu.SMEM(logit_scale.shape, f32),
            pltpu.VMEM(w_qkv.shape, bf16),
            pltpu.VMEM(w_proj.shape, bf16),
            pltpu.VMEM((own, c4), bf16),
            pltpu.VMEM((own, c4), bf16),
            pltpu.VMEM((3, quad, ch), bf16),
            pltpu.VMEM((4, quad, ch), bf16),
            pltpu.VMEM((4, quad, ch), bf16),
            pltpu.VMEM((4, quad, ch), bf16),
            pltpu.VMEM((4 * quad, 4 * quad), bf16),
            pltpu.VMEM((c4, w_merge.shape[0]), bf16),
            pltpu.VMEM((2, own, c4 // 2), f32),
            pltpu.VMEM((c4, ff), bf16),
            pltpu.VMEM((ni, ff, half), bf16),
            pltpu.VMEM((2, ni, ff, half), bf16),
            pltpu.VMEM((2, c4, ff), bf16),
            gathered,
            pltpu.VMEM((ni, 2, 2 * own, ff), bf16),
            pltpu.VMEM((half, nj * own), bf16),
            pltpu.VMEM((ff, nj * own), bf16),
            pltpu.VMEM((ni, nj, own, ff), f32),
            pltpu.VMEM((2, own, ff), f32),
            pltpu.VMEM((nj, ni, own, half), bf16),
            pltpu.VMEM((6, ni, own, half), bf16),
            gathered,
            pltpu.VMEM((nj, own, ff), bf16),
            pltpu.VMEM((2, own, ff), bf16),
            pltpu.VMEM((own, c4), f32),
            pltpu.VMEM((own, c4), bf16),
            pltpu.VMEM((own, c4), bf16),
            pltpu.VMEM((sent // 128, 128), bf16),
            dma((4,)),
            dma,
            dma((N_RECVS,)),
        ],
        compiler_params=pltpu.CompilerParams(
            collective_id=0, has_side_effects=True, vmem_limit_bytes=44 << 20
        ),
    )(*operands)
    values = pl.pallas_call(
        store_kernel,
        out_shape=outs,
        in_specs=[vm] * 8,
        out_specs=(hb,) * 4,
        scratch_shapes=[pltpu.VMEM((half, ff), f32), pltpu.VMEM((ff, half), f32), dma((4,))],
        compiler_params=pltpu.CompilerParams(vmem_limit_bytes=12 << 20),
    )(*values)
    shape = (tile_rows // 2, tile_cols // 2, c4)
    return values[0].reshape(shape), values[1].reshape(shape), values[2], values[3]


def device_body(*args):
    fields, _, w_qkv, _, w_merge, w_up, w_down, _ = args
    fits = (
        lax.axis_size("rows") == 2
        and lax.axis_size("cols") == 4
        and lax.axis_size("dp") % 2 == 0
        and fields.shape[:2] == (WIN, WIN)
        and w_up.shape[0] % 128 == 0
        and w_up.shape[1] % 128 == 0
        and w_merge.shape[1] % 64 == 0
        and w_merge.shape[0] % 1536 == 0
        and w_up.shape[0] % 384 == 0
        and w_up.shape[1] % 256 == 0
        and fields.shape[-1] % 128 == 0
    )
    return fused(*args) if fits else local(*args)


def solution(mesh):
    return jax.shard_map(
        device_body,
        mesh=mesh,
        in_specs=(
            P(("dp", "rows"), "cols", None),
            P(),
            P(),
            P(),
            P(None, "cols"),
            P("rows", "cols"),
            P("cols", "rows"),
            P(("dp", "rows"), "cols", None),
        ),
        out_specs=(
            P(("dp", "rows"), "cols", None),
            P(("dp", "rows"), "cols", None),
            P("rows", ("dp", "cols")),
            P("cols", ("dp", "rows")),
        ),
        check_vma=False,
    )
```
